32 devices in a mesh: rep: 2 (over core), dp: 4 (over y, x), seq: 4 (over z).
Axes of the slice: x: 2, y: 2, z: 4, core: 2. Of those that a mesh axis runs over, the one named last changes fastest.
Arguments:
- tokens: bfloat16 [2, 4, 2048, 2048], P(None, 'dp', ('rep', 'seq')), may hold values from -6 to 6
- lengths: int32 [2, 4], P(None, 'dp'), may hold values from 512 to 2048, as said below
- memory: float32 [2, 4, 16, 128, 128], P(None, 'dp'), may hold values from -48 to 48
- normalizer: float32 [2, 4, 16, 128], P(None, 'dp'), may hold values from 0.5 to 4
- qkv_weight: bfloat16 [6144, 2048], P(('dp', 'seq')), may hold values from -0.1875 to 0.1875
- out_weight: bfloat16 [2048, 2048], P(('dp', 'seq')), may hold values from -0.375 to 0.375
- norm_gains: bfloat16 [2, 2048], P(None, ('dp', 'seq')), may hold values from 0.5 to 1.5
- gate_logit: float32 [16], replicated, may hold values from -2 to 2
- inner_weight: bfloat16 [8192, 4096], P(('dp', 'seq')), may hold values from -0.125 to 0.125
- down_weight: bfloat16 [8192, 2048], P(('dp', 'seq')), may hold values from -0.125 to 0.125
- cotangent: bfloat16 [2, 4, 2048, 2048], P(None, 'dp', ('rep', 'seq')), may hold values from -6 to 6
Outputs:
- output: bfloat16 [2, 4, 2048, 2048], P(None, 'dp', ('rep', 'seq'))
- new_memory: float32 [2, 4, 16, 128, 128], P(None, 'dp', ('rep', 'seq'))
- new_normalizer: float32 [2, 4, 16, 128], P(None, 'dp', ('rep', 'seq'))
- grad_tokens: bfloat16 [2, 4, 2048, 2048], P(None, 'dp', ('rep', 'seq'))
- grad_qkv: float32 [6144, 2048], P(('dp', 'seq'))
- grad_out: float32 [2048, 2048], P(('dp', 'seq'))
- grad_gains: float32 [2, 2048], P(None, ('dp', 'seq'))
- grad_gate: float32 [16], replicated
- grad_inner: float32 [8192, 4096], P(('dp', 'seq'))
- grad_down: float32 [8192, 2048], P(('dp', 'seq'))
The draws below stay inside these ranges and needn't reach their ends.
Inputs may be any that keep to these rules, and one draw needn't show every extreme that they name: `lengths`: in every draw some sequence has length 2048 and some has 512.
All inputs are finite; a program needn't handle non-finite values.
Results may differ from the reference program's by a relative error of at most 0.018.
The reference program's roundings to bfloat16 on the way count: a program that leaves them out, or rounds other values in their place, can miss the bound.
Values may be sent and summed in bfloat16 or wider, within the bound.
A program may use at most 640 MiB of HBM per device.

```python
import math
import jax
import jax.numpy as jnp
from jax import lax

D = 2048
H = 16
DK = 128
FF = 8192
LEN = 2048
MB = 2
BATCH = 4


def draw_lengths(key, part):
    seq_count = MB * BATCH
    first_key, second_key, third_key = jax.random.split(jax.random.fold_in(key, 17), 3)
    picked = jax.random.randint(first_key, (seq_count,), LEN // 4, LEN + 1)
    longest_at = jax.random.randint(second_key, (), 0, seq_count)
    shortest_at = (longest_at + 1 + jax.random.randint(third_key, (), 0, seq_count - 1)) % seq_count
    picked = picked.at[longest_at].set(LEN)
    picked = picked.at[shortest_at].set(LEN // 4)
    return picked.reshape(MB, BATCH).astype(jnp.int32)


def shard_levels(stream_key, extent, pieces, low, largest):
    gain = 1.0
    for axis_at, parts in pieces:
        steps = jax.random.uniform(jax.random.fold_in(jax.random.fold_in(stream_key, 6), axis_at), (parts,), jnp.float32, low / len(pieces), largest / len(pieces))
        gain = gain * jnp.repeat(jnp.exp(steps), extent[axis_at] // parts).reshape((-1,) + (1,) * (len(extent) - 1 - axis_at))
    return gain


def noise(own_key, extent, scale, reach, cuts=(), kind=jnp.bfloat16):
    entries = scale * jax.random.normal(own_key, extent, jnp.float32)
    if cuts:
        entries = entries * shard_levels(own_key, extent, cuts, -0.22, 0.18)
    return jnp.clip(entries, -reach, reach).astype(kind)


def setup_inputs(seed: int = 0) -> dict:
    arg_keys = jax.random.split(jax.random.key(seed), 12)
    tokens = noise(arg_keys[0], (MB, BATCH, LEN, D), 1.0, 6.0, ((1, 4), (2, 8)))
    lengths = draw_lengths(jax.random.fold_in(arg_keys[11], 71), 0)
    memory = noise(arg_keys[2], (MB, BATCH, H, DK, DK), 8.0, 48.0, ((1, 4),), jnp.float32)
    normalizer = jnp.clip(jnp.exp(math.log(4.0) - 2.0794415 * jax.random.uniform(arg_keys[3], (MB, BATCH, H, DK), jnp.float32) ** shard_levels(arg_keys[3], (MB, BATCH, H, DK), ((1, 4),), -0.2, 0.2)), 0.5, 4.0)
    qkv_weight = noise(arg_keys[4], (3 * D, D), (D // 2) ** -0.5, 0.1875, ((0, 16),))
    out_weight = noise(arg_keys[5], (D, D), (D // 8) ** -0.5, 0.375, ((0, 16),))
    norm_gains = jnp.clip(1.0 + 0.1 * jax.random.normal(arg_keys[6], (2, D), jnp.float32), 0.5, 1.5).astype(jnp.bfloat16)
    gate_logit = jnp.clip(jax.random.uniform(arg_keys[7], (H,), jnp.float32, -2.0, 2.0), -2.0, 2.0)
    inner_weight = noise(arg_keys[8], (FF, 2 * D), D ** -0.5, 0.125, ((0, 16),))
    down_weight = noise(arg_keys[9], (FF, D), (FF // 4) ** -0.5, 0.125, ((0, 16),))
    cotangent = noise(arg_keys[10], (MB, BATCH, LEN, D), 1.0, 6.0, ((1, 4), (2, 8)))
    return {"tokens": tokens, "lengths": lengths, "memory": memory, "normalizer": normalizer, "qkv_weight": qkv_weight, "out_weight": out_weight, "norm_gains": norm_gains, "gate_logit": gate_logit, "inner_weight": inner_weight, "down_weight": down_weight, "cotangent": cotangent}


@jax.custom_vjp
def low(v):
    return lax.optimization_barrier(v.astype(jnp.bfloat16)).astype(jnp.float32)

@jax.custom_vjp
def low_back(v):
    return v

def low_keep(v):
    return (low(v), None)

def low_pass(kept, grad):
    return (grad,)

def back_keep(v):
    return (v, None)

def back_low(kept, grad):
    return (low(grad),)
low.defvjp(low_keep, low_pass)
low_back.defvjp(back_keep, back_low)
EPSILON = 1e-05
HIGHEST = lax.Precision.HIGHEST

def rounded_both(value):
    return low(low_back(value))

def normalize(value):
    return value * lax.rsqrt(lax.optimization_barrier(jnp.mean(value * value, axis=-1, keepdims=True)) + EPSILON)

def attend(queries, key_rows, value_rows, live_mask):
    block_rows = min(512, LEN)
    key_positions = jnp.arange(LEN)
    blocks = queries.reshape(LEN // block_rows, block_rows, H, DK)
    starts = jnp.arange(LEN // block_rows) * block_rows

    def one_block(block_args):
        query_block, first_row = block_args
        raw_scores = low_back(jnp.einsum('qhd,khd->hqk', query_block, key_rows, precision=HIGHEST))
        scores = raw_scores * DK ** (-0.5)
        positions = first_row + jnp.arange(block_rows)
        allowed = (key_positions[None, :] <= positions[:, None]) & (live_mask[None, :] > 0.0)
        scores = jnp.where(allowed[None], scores, -1e+30)
        row_max = lax.optimization_barrier(jnp.max(scores, axis=-1, keepdims=True))
        shifted = jnp.exp(scores - row_max)
        probabilities = shifted / lax.optimization_barrier(jnp.sum(shifted, axis=-1, keepdims=True))
        return low_back(jnp.einsum('hqk,khd->qhd', low(probabilities), value_rows, precision=HIGHEST))
    return lax.map(jax.checkpoint(one_block), (blocks, starts)).reshape(LEN, H, DK)

def block_forward(tokens_row, qkv_weight, out_weight, norm_gains, gate_logit, inner_weight, down_weight, memory, normalizer, live_mask):
    normed_one = normalize(tokens_row)
    hidden_one = low(normed_one * norm_gains[0])
    projected = rounded_both(jnp.dot(hidden_one, qkv_weight.T, precision=HIGHEST))
    queries = projected[:, :D].reshape(LEN, H, DK)
    key_rows = projected[:, D:2 * D].reshape(LEN, H, DK)
    value_rows = projected[:, 2 * D:].reshape(LEN, H, DK)
    query_sig = jax.nn.elu(queries) + 1.0
    numerator = jnp.einsum('thd,hde->the', query_sig, memory, precision=HIGHEST)
    denominator = jnp.einsum('thd,hd->th', query_sig, normalizer, precision=HIGHEST)
    mem_read = numerator / denominator[..., None]
    dot_read = attend(queries, key_rows, value_rows, live_mask)
    mixing = jax.nn.sigmoid(gate_logit)[None, :, None]
    mixed = rounded_both((mixing * mem_read + (1.0 - mixing) * dot_read).reshape(LEN, D))
    branch = low_back(jnp.dot(mixed, out_weight.T, precision=HIGHEST))
    after_attn = tokens_row + branch
    hidden_two = low(normalize(after_attn) * norm_gains[1])
    gates = low_back(jnp.dot(hidden_two, inner_weight[:, :D].T, precision=HIGHEST))
    up_values = low_back(jnp.dot(hidden_two, inner_weight[:, D:].T, precision=HIGHEST))
    hidden = low(jax.nn.silu(gates) * up_values)
    mlp_out = low_back(jnp.dot(hidden, down_weight, precision=HIGHEST))
    key_sig = jax.nn.elu(key_rows) + 1.0
    recalled = jnp.einsum('thd,hde->the', key_sig, memory, precision=HIGHEST) / jnp.einsum('thd,hd->th', key_sig, normalizer, precision=HIGHEST)[..., None]
    kept_sig = key_sig * live_mask[:, None, None]
    new_memory = memory + jnp.einsum('thd,the->hde', kept_sig, value_rows - recalled, precision=HIGHEST)
    new_normalizer = normalizer + lax.optimization_barrier(jnp.sum(kept_sig, axis=0))
    return (after_attn + mlp_out, (new_memory, new_normalizer))

def reference(tokens, lengths, memory, normalizer, qkv_weight, out_weight, norm_gains, gate_logit, inner_weight, down_weight, cotangent):
    weights = (qkv_weight.astype(jnp.float32), out_weight.astype(jnp.float32), norm_gains.astype(jnp.float32), gate_logit.astype(jnp.float32), inner_weight.astype(jnp.float32), down_weight.astype(jnp.float32))
    seq_count = MB * BATCH
    per_row = (tokens.reshape(seq_count, LEN, D), cotangent.reshape(seq_count, LEN, D), lengths.reshape(seq_count), memory.reshape(seq_count, H, DK, DK), normalizer.reshape(seq_count, H, DK))

    def one_sequence(totals, row_items):
        row_tokens, row_cot, row_length, row_memory, row_norm = row_items
        live_mask = (jnp.arange(LEN) < row_length).astype(jnp.float32)

        def forward(inputs, *params):
            return block_forward(inputs, *params, row_memory, row_norm, live_mask)
        result, pullback, aux_state = jax.vjp(forward, row_tokens.astype(jnp.float32), *weights, has_aux=True)
        gradients = pullback(row_cot.astype(jnp.float32) * live_mask[:, None])
        totals = tuple((total_grad + new_grad for total_grad, new_grad in zip(totals, gradients[1:])))
        return (totals, (result.astype(jnp.bfloat16), gradients[0].astype(jnp.bfloat16), aux_state[0], aux_state[1]))
    zero_grads = tuple((jnp.zeros_like(weight) for weight in weights))
    totals, (outputs, grad_rows, memories, norm_states) = lax.scan(one_sequence, zero_grads, per_row)
    return (outputs.reshape(MB, BATCH, LEN, D), memories.reshape(MB, BATCH, H, DK, DK), norm_states.reshape(MB, BATCH, H, DK), grad_rows.reshape(MB, BATCH, LEN, D), totals[0], totals[1], totals[2], totals[3], totals[4], totals[5])
```

```python
import functools
import math

import jax
import jax.numpy as jnp
from jax import lax
from jax.experimental import pallas as pl
from jax.experimental.pallas import tpu as pltpu
from jax.sharding import PartitionSpec as P

EPSILON = 1e-05
LOG2E = 1.4426950408889634
NEG = -1e30
F32 = jnp.float32
BF16 = jnp.bfloat16
ALL = ("rep", "dp", "seq")


def nt(left_side, right_side):
    return lax.dot_general(
        left_side, right_side, (((1,), (1,)), ((), ())), preferred_element_type=F32
    )


def nn(left_side, right_side):
    return lax.dot_general(
        left_side, right_side, (((1,), (0,)), ((), ())), preferred_element_type=F32
    )


def tn(left_side, right_side):
    return lax.dot_general(
        left_side, right_side, (((0,), (0,)), ((), ())), preferred_element_type=F32
    )


def elu_one(values):
    return jnp.where(values > 0.0, values + 1.0, jnp.exp(jnp.minimum(values, 0.0)))


def project_kernel(rows_ref, gain_ref, weight_ref, hidden_ref, projected_ref):
    rows = rows_ref[...].astype(F32)
    scale = lax.rsqrt(jnp.mean(rows * rows, axis=-1, keepdims=True) + EPSILON)
    hidden = (rows * scale * gain_ref[...]).astype(BF16)
    hidden_ref[...] = hidden
    projected_ref[...] = nt(hidden, weight_ref[...]).astype(BF16)


def project(rows, gain, weight):
    count, width = rows.shape
    outs = weight.shape[0]
    block = min(256, count)
    return pl.pallas_call(
        project_kernel,
        grid=(count // block,),
        in_specs=[
            pl.BlockSpec((block, width), lambda i: (i, 0)),
            pl.BlockSpec((1, width), lambda i: (0, 0)),
            pl.BlockSpec((outs, width), lambda i: (0, 0)),
        ],
        out_specs=[
            pl.BlockSpec((block, width), lambda i: (i, 0)),
            pl.BlockSpec((block, outs), lambda i: (i, 0)),
        ],
        out_shape=[
            jax.ShapeDtypeStruct((count, width), BF16),
            jax.ShapeDtypeStruct((count, outs), BF16),
        ],
        compiler_params=pltpu.CompilerParams(vmem_limit_bytes=32 << 20),
        cost_estimate=pl.CostEstimate(
            flops=2 * count * width * outs,
            bytes_accessed=4 * count * width + 2 * outs * (width + count),
            transcendentals=count,
        ),
        name="project",
    )(rows, gain, weight)


def attend_kernel(
    block,
    length_ref,
    gate_ref,
    q_ref,
    k_ref,
    v_ref,
    mem_ref,
    norm_ref,
    mixed_ref,
    dot_ref,
    lse_ref,
    new_mem_ref,
    new_norm_ref,
    v_turned,
):
    head, step = pl.program_id(0), pl.program_id(1)
    length = length_ref[0]
    total, width = k_ref.shape
    memory = mem_ref[0]
    norm_row = norm_ref[0]
    memory_low = memory.astype(BF16)

    @pl.when(step == 0)
    def _():
        v_turned[...] = v_ref[...].T
        key_sig = elu_one(k_ref[...].astype(F32))
        below = jnp.sum(key_sig * norm_row, axis=-1, keepdims=True)
        recalled = nn(key_sig.astype(BF16), memory_low) / below
        change = v_ref[...].astype(F32) - recalled
        live = lax.broadcasted_iota(jnp.int32, (total, width), 0) < length
        kept = jnp.where(live, key_sig, 0.0)
        new_mem_ref[0] = memory + tn(kept.astype(BF16), change.astype(BF16))
        new_norm_ref[0] = norm_row + jnp.sum(kept, axis=0, keepdims=True)

    queries = q_ref[...]
    factor = LOG2E * width ** (-0.5)

    def visit(at, carry, masked):
        high, mass, acc = carry
        start = pl.multiple_of(at * block, block)
        scores = nt(k_ref[pl.ds(start, block), :], queries) * factor
        if masked:
            key_at = start + lax.broadcasted_iota(jnp.int32, (block, block), 0)
            query_at = step * block + lax.broadcasted_iota(jnp.int32, (block, block), 1)
            scores = jnp.where((key_at <= query_at) & (key_at < length), scores, NEG)
        higher = jnp.maximum(high, jnp.max(scores, axis=0, keepdims=True))
        weights = jnp.exp2(scores - higher)
        shrink = jnp.exp2(high - higher)
        mass = mass * shrink + jnp.sum(weights, axis=0, keepdims=True)
        acc = acc * shrink + nn(v_turned[:, pl.ds(start, block)], weights.astype(BF16))
        return higher, mass, acc

    full = jnp.minimum(step, length // block)
    end = jnp.minimum(step + 1, (length + block - 1) // block)
    carry = (
        jnp.full((1, block), NEG, F32),
        jnp.zeros((1, block), F32),
        jnp.zeros((width, block), F32),
    )
    carry = lax.fori_loop(0, full, functools.partial(visit, masked=False), carry)
    high, mass, acc = lax.fori_loop(full, end, functools.partial(visit, masked=True), carry)
    dot_read = (acc / mass).T
    query_sig = elu_one(queries.astype(F32))
    below = jnp.sum(query_sig * norm_row, axis=-1, keepdims=True)
    mem_read = nn(query_sig.astype(BF16), memory_low) / below
    gate = gate_ref[head]
    mixed_ref[...] = (gate * mem_read + (1.0 - gate) * dot_read).astype(BF16)
    dot_ref[...] = dot_read
    lse_ref[0] = high + jnp.log2(mass)


def attend(length, gate, projected, memory, normalizer):
    total = projected.shape[0]
    heads, width = normalizer.shape[0], normalizer.shape[2]
    block = min(512, total)
    smem = pl.BlockSpec(memory_space=pltpu.SMEM)
    return pl.pallas_call(
        functools.partial(attend_kernel, block),
        grid=(heads, total // block),
        in_specs=[
            smem,
            smem,
            pl.BlockSpec((block, width), lambda h, i: (i, h)),
            pl.BlockSpec((total, width), lambda h, i: (0, heads + h)),
            pl.BlockSpec((total, width), lambda h, i: (0, 2 * heads + h)),
            pl.BlockSpec((1, width, width), lambda h, i: (h, 0, 0)),
            pl.BlockSpec((1, 1, width), lambda h, i: (h, 0, 0)),
        ],
        out_specs=[
            pl.BlockSpec((block, width), lambda h, i: (i, h)),
            pl.BlockSpec((block, width), lambda h, i: (i, h)),
            pl.BlockSpec((1, 1, block), lambda h, i: (h, 0, i)),
            pl.BlockSpec((1, width, width), lambda h, i: (h, 0, 0)),
            pl.BlockSpec((1, 1, width), lambda h, i: (h, 0, 0)),
        ],
        out_shape=[
            jax.ShapeDtypeStruct((total, heads * width), BF16),
            jax.ShapeDtypeStruct((total, heads * width), F32),
            jax.ShapeDtypeStruct((heads, 1, total), F32),
            jax.ShapeDtypeStruct((heads, width, width), F32),
            jax.ShapeDtypeStruct((heads, 1, width), F32),
        ],
        scratch_shapes=[pltpu.VMEM((width, total), BF16)],
        compiler_params=pltpu.CompilerParams(vmem_limit_bytes=40 << 20),
        cost_estimate=pl.CostEstimate(
            flops=4 * heads * total * total * width,
            bytes_accessed=heads * total * width * 12,
            transcendentals=heads * total * total,
        ),
        name="attend",
    )(length, gate, projected, projected, projected, memory, normalizer)


def attend_back_kernel(
    block,
    length_ref,
    gate_ref,
    q_ref,
    k_ref,
    v_ref,
    mem_ref,
    norm_ref,
    dot_ref,
    lse_ref,
    grad_ref,
    out_ref,
    gate_sum_ref,
    k_turned,
    k_sum,
    v_sum,
):
    head, step = pl.program_id(0), pl.program_id(1)
    heads, steps = pl.num_programs(0), pl.num_programs(1)
    length = length_ref[0]
    total, width = k_ref.shape
    gate = gate_ref[head]

    @pl.when(step == 0)
    def _():
        k_turned[...] = k_ref[...].T
        k_sum[...] = jnp.zeros_like(k_sum)
        v_sum[...] = jnp.zeros_like(v_sum)
        gate_sum_ref[...] = jnp.zeros_like(gate_sum_ref)

    queries = q_ref[...]
    query_float = queries.astype(F32)
    grad_mixed = grad_ref[...].astype(F32)
    grad_dot = ((1.0 - gate) * grad_mixed).astype(BF16)
    dot_read = dot_ref[...]
    offset = jnp.sum((grad_dot.astype(F32) * dot_read).T, axis=0, keepdims=True)
    lse = lse_ref[0]
    scale = width ** (-0.5)
    factor = LOG2E * scale

    def visit(at, acc, masked):
        start = pl.multiple_of(at * block, block)
        here = pl.ds(start, block)
        scores = nt(k_ref[here, :], queries) * factor
        weights = jnp.exp2(scores - lse)
        if masked:
            key_at = start + lax.broadcasted_iota(jnp.int32, (block, block), 0)
            query_at = step * block + lax.broadcasted_iota(jnp.int32, (block, block), 1)
            weights = jnp.where((key_at <= query_at) & (key_at < length), weights, 0.0)
        grad_probs = nt(v_ref[here, :], grad_dot)
        grad_scores = (weights * (grad_probs - offset) * scale).astype(BF16)
        v_sum[here, :] += nn(weights.astype(BF16), grad_dot)
        k_sum[here, :] += nn(grad_scores, queries)
        return acc + nn(k_turned[:, here], grad_scores)

    full = jnp.minimum(step, length // block)
    end = jnp.minimum(step + 1, (length + block - 1) // block)
    acc = jnp.zeros((width, block), F32)
    acc = lax.fori_loop(0, full, functools.partial(visit, masked=False), acc)
    acc = lax.fori_loop(full, end, functools.partial(visit, masked=True), acc)

    memory_low = mem_ref[0].astype(BF16)
    norm_row = norm_ref[0]
    query_sig = elu_one(query_float)
    below = jnp.sum(query_sig * norm_row, axis=-1, keepdims=True)
    numerator = nn(query_sig.astype(BF16), memory_low)
    inverse = 1.0 / below
    grad_read = gate * grad_mixed
    grad_below = -jnp.sum(grad_read * numerator, axis=-1, keepdims=True) * inverse * inverse
    grad_sig = nt((grad_read * inverse).astype(BF16), memory_low) + grad_below * norm_row
    slope = jnp.where(query_float > 0.0, 1.0, jnp.exp(jnp.minimum(query_float, 0.0)))
    rows = pl.ds(pl.multiple_of(step * block, block), block)
    out_ref[rows, pl.ds(pl.multiple_of(head * width, width), width)] = (
        acc.T + grad_sig * slope
    ).astype(BF16)
    gate_sum_ref[0] += jnp.sum(
        grad_mixed * (numerator * inverse - dot_read), axis=0, keepdims=True
    )

    @pl.when(step == steps - 1)
    def _():
        k_at = pl.multiple_of((heads + head) * width, width)
        v_at = pl.multiple_of((2 * heads + head) * width, width)
        out_ref[:, pl.ds(k_at, width)] = k_sum[...].astype(BF16)
        out_ref[:, pl.ds(v_at, width)] = v_sum[...].astype(BF16)


def attend_back(length, gate, projected, memory, normalizer, dot_read, lse, grad_mixed):
    total = projected.shape[0]
    heads, width = normalizer.shape[0], normalizer.shape[2]
    block = min(512, total)
    smem = pl.BlockSpec(memory_space=pltpu.SMEM)
    return pl.pallas_call(
        functools.partial(attend_back_kernel, block),
        grid=(heads, total // block),
        in_specs=[
            smem,
            smem,
            pl.BlockSpec((block, width), lambda h, i: (i, h)),
            pl.BlockSpec((total, width), lambda h, i: (0, heads + h)),
            pl.BlockSpec((total, width), lambda h, i: (0, 2 * heads + h)),
            pl.BlockSpec((1, width, width), lambda h, i: (h, 0, 0)),
            pl.BlockSpec((1, 1, width), lambda h, i: (h, 0, 0)),
            pl.BlockSpec((block, width), lambda h, i: (i, h)),
            pl.BlockSpec((1, 1, block), lambda h, i: (h, 0, i)),
            pl.BlockSpec((block, width), lambda h, i: (i, h)),
        ],
        out_specs=[
            pl.BlockSpec((total, 3 * heads * width), lambda h, i: (0, 0)),
            pl.BlockSpec((1, 1, width), lambda h, i: (h, 0, 0)),
        ],
        out_shape=[
            jax.ShapeDtypeStruct((total, 3 * heads * width), BF16),
            jax.ShapeDtypeStruct((heads, 1, width), F32),
        ],
        scratch_shapes=[
            pltpu.VMEM((width, total), BF16),
            pltpu.VMEM((total, width), F32),
            pltpu.VMEM((total, width), F32),
        ],
        compiler_params=pltpu.CompilerParams(vmem_limit_bytes=40 << 20),
        cost_estimate=pl.CostEstimate(
            flops=10 * heads * total * total * width,
            bytes_accessed=heads * total * width * 20,
            transcendentals=heads * total * total,
        ),
        name="attend_back",
    )(length, gate, projected, projected, projected, memory, normalizer, dot_read, lse, grad_mixed)


def mlp_kernel(
    tiles,
    rows_ref,
    grad_ref,
    inner_a,
    inner_b,
    down_a,
    down_b,
    out_ref,
    grad_two_ref,
    hidden_ref,
    grad_gate_ref,
    grad_up_ref,
    out_acc,
    grad_acc,
):
    step = pl.program_id(0)
    width = rows_ref.shape[1]

    @pl.when(step == 0)
    def _():
        out_acc[...] = jnp.zeros_like(out_acc)
        grad_acc[...] = jnp.zeros_like(grad_acc)

    def visit(inner_ref, down_ref):
        gate_weight = inner_ref[:, :width]
        up_weight = inner_ref[:, width:]
        down = down_ref[...]
        rows = rows_ref[...]
        gates = nt(rows, gate_weight)
        ups = nt(rows, up_weight)
        sigmoid = 1.0 / (1.0 + jnp.exp(-gates))
        silu = gates * sigmoid
        hidden = (silu * ups).astype(BF16)
        hidden_ref[...] = hidden
        out_acc[...] += nn(hidden, down)
        grad_hidden = nt(grad_ref[...], down)
        grad_gates = (grad_hidden * ups * (sigmoid * (1.0 + gates * (1.0 - sigmoid)))).astype(BF16)
        grad_ups = (grad_hidden * silu).astype(BF16)
        grad_gate_ref[...] = grad_gates
        grad_up_ref[...] = grad_ups
        grad_acc[...] += nn(grad_gates, gate_weight) + nn(grad_ups, up_weight)

    @pl.when(step < tiles)
    def _():
        visit(inner_a, down_a)

    @pl.when(step >= tiles)
    def _():
        visit(inner_b, down_b)

    @pl.when(step == 2 * tiles - 1)
    def _():
        out_ref[...] = out_acc[...].astype(BF16)
        grad_two_ref[...] = grad_acc[...].astype(BF16)


def mlp(rows, grads, inner_a, inner_b, down_a, down_b):
    count, width = rows.shape
    units = inner_a.shape[0]
    tile = min(256, units)
    tiles = units // tile
    first = lambda t: (jnp.minimum(t, tiles - 1), 0)
    second = lambda t: (jnp.maximum(t - tiles, 0), 0)
    whole = lambda t: (0, 0)
    once = pl.Buffered(1)
    column = pl.BlockSpec((count, tile), lambda t: (0, t))
    unit_shape = jax.ShapeDtypeStruct((count, 2 * units), BF16)
    row_shape = jax.ShapeDtypeStruct((count, width), BF16)
    return pl.pallas_call(
        functools.partial(mlp_kernel, tiles),
        grid=(2 * tiles,),
        in_specs=[
            pl.BlockSpec((count, width), whole, pipeline_mode=once),
            pl.BlockSpec((count, width), whole, pipeline_mode=once),
            pl.BlockSpec((tile, 2 * width), first),
            pl.BlockSpec((tile, 2 * width), second),
            pl.BlockSpec((tile, width), first),
            pl.BlockSpec((tile, width), second),
        ],
        out_specs=[
            pl.BlockSpec((count, width), whole, pipeline_mode=once),
            pl.BlockSpec((count, width), whole, pipeline_mode=once),
            column,
            column,
            column,
        ],
        out_shape=[row_shape, row_shape, unit_shape, unit_shape, unit_shape],
        scratch_shapes=[pltpu.VMEM((count, width), F32), pltpu.VMEM((count, width), F32)],
        compiler_params=pltpu.CompilerParams(vmem_limit_bytes=60 << 20),
        cost_estimate=pl.CostEstimate(
            flops=2 * 6 * count * width * 2 * units,
            bytes_accessed=2 * units * (6 * width + 6 * count) + 8 * count * width,
            transcendentals=count * 2 * units,
        ),
        name="feed_forward",
    )(rows, grads, inner_a, inner_b, down_a, down_b)


def swap(values):
    return lax.ppermute(values, "rep", [(0, 1), (1, 0)])


def add_low(left_side, right_side):
    return (left_side.astype(F32) + right_side.astype(F32)).astype(BF16)


def line_gather(values, axis):
    count = lax.axis_size(axis)
    here = lax.axis_index(axis)
    rows = values.shape[0]
    table = jnp.zeros(((3 * count - 2) * rows,) + values.shape[1:], values.dtype)

    def put(table, piece, origin):
        return lax.dynamic_update_slice_in_dim(table, piece, (origin + count - 1) * rows, 0)

    table = put(table, values, here)
    rising = falling = values
    for hop in range(1, count):
        rising = lax.ppermute(
            rising, axis, [(a, a + 1) for a in range(count - 1) if a >= hop - 1]
        )
        falling = lax.ppermute(
            falling, axis, [(a, a - 1) for a in range(1, count) if a + hop - 1 < count]
        )
        table = put(table, rising, here - hop)
        table = put(table, falling, here + hop)
    return table[(count - 1) * rows : (2 * count - 1) * rows]


def line_scatter(values, axis):
    count = lax.axis_size(axis)
    here = lax.axis_index(axis)
    rows = values.shape[0] // count

    def block(owner):
        start = jnp.clip(owner, 0, count - 1) * rows
        return lax.dynamic_slice_in_dim(values, start, rows, 0).astype(F32)

    rising = falling = None
    for hop in range(1, count):
        reach = count - hop
        up, down = block(here + reach), block(here - reach)
        if rising is not None:
            up, down = up + rising.astype(F32), down + falling.astype(F32)
        rising = lax.ppermute(
            up.astype(BF16), axis, [(a, a + 1) for a in range(count) if a + reach < count]
        )
        falling = lax.ppermute(
            down.astype(BF16), axis, [(a, a - 1) for a in range(count) if a - reach >= 0]
        )
    return block(here) + rising.astype(F32) + falling.astype(F32)


def cube_bits(count):
    bits = [1 << b for b in range(count.bit_length() - 1)]
    return bits, bits[::-1]


def cube_order(bits):
    order = [0]
    for bit in reversed(bits):
        order = order + [k | bit for k in order]
    return order


def cube_gather(values, axis):
    count = lax.axis_size(axis)
    half = values.shape[0] // 2
    parts = []
    for bits, start in zip(cube_bits(count), (0, half)):
        held = {0: values[start : start + half]}
        for bit in bits:
            pairs = [(a, a ^ bit) for a in range(count)]
            held.update({k ^ bit: lax.ppermute(v, axis, pairs) for k, v in list(held.items())})
        parts += [held[k] for k in cube_order(bits)]
    return jnp.concatenate(parts, axis=0)


def cube_scatter(values, axis):
    count = lax.axis_size(axis)
    half = values.shape[0] // 2
    parts = []
    for bits, start in zip(cube_bits(count), (0, half)):
        held = values[start : start + half]
        for bit in bits:
            pairs = [(a, a ^ bit) for a in range(count)]
            keep = held.shape[0] // 2
            got = lax.ppermute(held[keep:].astype(BF16), axis, pairs)
            held = held[:keep].astype(F32) + got.astype(F32)
        parts.append(held)
    return jnp.concatenate(parts, axis=0)


def heads_plan(shard_rows, block_rows, dp_count, seq_count, span_count):
    unit = math.gcd(shard_rows, block_rows)
    per_shard, per_block = shard_rows // unit, block_rows // unit
    per_column = 3 * span_count // dp_count
    edges = []
    for u in range(dp_count * seq_count * per_shard):
        shard, block = u // per_shard, u // per_block
        column, source = divmod(shard, seq_count)
        core, target = divmod(block % span_count, seq_count)
        edges.append((core, column, source, target, u % per_shard, u % per_block))
    rounds = []
    for edge in edges:
        core, column, source, target = edge[:4]
        for group in rounds:
            if all(
                (core, column) != e[:2] or (source != e[2] and target != e[3]) for e in group
            ):
                group.append(edge)
                break
        else:
            rounds.append([edge])
    return unit, per_shard, per_block, per_column, rounds


def device_number(core, column, place, dp_count, seq_count):
    return (core * dp_count + column) * seq_count + place


def pick(table, number):
    return jnp.asarray(table, jnp.int32)[number]


def shards(
    tokens,
    lengths,
    memory,
    normalizer,
    qkv_weight,
    out_weight,
    norm_gains,
    gate_logit,
    inner_weight,
    down_weight,
    cotangent,
):
    micros, _, span_rows, width = tokens.shape
    head_count = gate_logit.shape[0]
    head_dim = width // head_count
    dp_count, seq_count = lax.axis_size("dp"), lax.axis_size("seq")
    span_count = 2 * seq_count
    total = span_rows * span_count
    half_total = total // 2
    heads_here = head_count // span_count
    block_rows = heads_here * head_dim
    core, column, place = lax.axis_index("rep"), lax.axis_index("dp"), lax.axis_index("seq")
    span = core * seq_count + place
    number = device_number(core, column, place, dp_count, seq_count)
    inner_half = inner_weight.shape[0] // 2

    own_rows = [tokens[m, 0] for m in range(micros)]
    near = [line_gather(rows, "seq") for rows in own_rows]
    far = [swap(rows) for rows in near]

    unit, per_shard, per_block, per_column, rounds = heads_plan(
        qkv_weight.shape[0], block_rows, dp_count, seq_count, span_count
    )
    landed = jnp.zeros(((per_block + 1) * unit, width), BF16)
    devices = 2 * dp_count * seq_count
    for group in rounds:
        send, slot, pairs = [0] * devices, [per_block] * devices, []
        for c, col, source, target, from_unit, to_unit in group:
            a = device_number(c, col, source, dp_count, seq_count)
            b = device_number(c, col, target, dp_count, seq_count)
            send[a], slot[b] = from_unit, to_unit
            pairs.append((a, b))
        piece = lax.dynamic_slice_in_dim(qkv_weight, pick(send, number) * unit, unit, 0)
        piece = lax.ppermute(piece, ALL, pairs)
        landed = lax.dynamic_update_slice_in_dim(landed, piece, pick(slot, number) * unit, 0)
    forward_bits = cube_bits(dp_count)
    blocks = cube_gather(landed[:block_rows], "dp")
    half_block = block_rows // 2
    orders = [cube_order(bits) for bits in forward_bits]
    spots = [[order.index(k) for k in range(dp_count)] for order in orders]
    head_weights = []
    for part in range(3):
        distance = ((part * span_count + span) // per_column) ^ column
        for side in range(2):
            spot = pick(spots[side], distance) + side * dp_count
            head_weights.append(
                lax.dynamic_slice_in_dim(blocks, spot * half_block, half_block, 0)
            )
    head_weight = jnp.concatenate(head_weights, axis=0)

    gains_all = lax.all_gather(norm_gains, ("dp", "seq"), axis=1, tiled=True).astype(F32)
    gain_one, gain_two = gains_all[0:1], gains_all[1:2]
    half_width = width // 2
    out_near = lax.all_gather(
        lax.dynamic_slice_in_dim(out_weight, core * half_width, half_width, 1),
        ("dp", "seq"),
        axis=0,
        tiled=True,
    )
    inner_near = lax.all_gather(
        lax.dynamic_slice_in_dim(inner_weight, core * inner_half, inner_half, 0),
        "seq",
        axis=0,
        tiled=True,
    )
    down_near = lax.all_gather(
        lax.dynamic_slice_in_dim(down_weight, core * inner_half, inner_half, 0),
        "seq",
        axis=0,
        tiled=True,
    )
    out_far, inner_far, down_far = swap(out_near), swap(inner_near), swap(down_near)

    positions = span * span_rows + jnp.arange(span_rows)
    gate_share = jax.nn.sigmoid(gate_logit)
    gate_here = lax.dynamic_slice_in_dim(gate_share, span * heads_here, heads_here, 0)
    near_at, far_at = core * half_width, (1 - core) * half_width

    live_cots, grad_lows, grad_rows = [], [], []
    for m in range(micros):
        live_rows = (positions < lengths[m, 0]).astype(F32)
        live = cotangent[m, 0].astype(F32) * live_rows[:, None]
        live_cots.append(live)
        grad_lows.append(live.astype(BF16))
        grad_rows.append(cube_gather(grad_lows[m], "dp"))

    saved = []
    outputs, new_memories, new_norms = [], [], []
    for m in range(micros):
        hidden_near, projected_near = project(near[m], gain_one, head_weight)
        hidden_far, projected_far = project(far[m], gain_one, head_weight)
        low_first = core == 0
        projected = jnp.concatenate(
            [
                jnp.where(low_first, projected_near, projected_far),
                jnp.where(low_first, projected_far, projected_near),
            ],
            axis=0,
        )
        memory_here = lax.dynamic_slice_in_dim(memory[m, 0], span * heads_here, heads_here, 0)
        norm_here = lax.dynamic_slice_in_dim(
            normalizer[m, 0], span * heads_here, heads_here, 0
        ).reshape(heads_here, 1, head_dim)
        length = lengths[m]
        mixed_heads, dot_read, lse, new_memory, new_norm = attend(
            length, gate_here, projected, memory_here, norm_here
        )
        new_memories.append(new_memory)
        new_norms.append(new_norm.reshape(heads_here, head_dim))
        mixed = lax.all_to_all(
            mixed_heads.reshape(span_count, span_rows, block_rows),
            ("rep", "seq"),
            0,
            0,
            tiled=True,
        )
        mixed = jnp.swapaxes(mixed, 0, 1).reshape(span_rows, width)
        mixed_near = lax.dynamic_slice_in_dim(mixed, near_at, half_width, 1)
        mixed_far = lax.dynamic_slice_in_dim(mixed, far_at, half_width, 1)
        after_attn = (
            own_rows[m].astype(F32) + nt(mixed_near, out_near) + nt(mixed_far, out_far)
        )
        scale_two = lax.rsqrt(jnp.mean(after_attn * after_attn, axis=-1, keepdims=True) + EPSILON)
        normed_two = after_attn * scale_two
        hidden_two = (normed_two * gain_two).astype(BF16)
        rows_all = cube_gather(hidden_two, "dp")
        mlp_part, grad_two_part, hidden, grad_gates, grad_ups = mlp(
            rows_all, grad_rows[m], inner_near, inner_far, down_near, down_far
        )
        grad_two = cube_scatter(grad_two_part, "dp")
        mlp_out = cube_scatter(mlp_part, "dp")
        outputs.append((after_attn + mlp_out).astype(BF16))
        grad_scaled = grad_two * gain_two
        grad_after = live_cots[m] + scale_two * (
            grad_scaled
            - normed_two * jnp.mean(grad_scaled * normed_two, axis=-1, keepdims=True)
        )
        grad_branch = grad_after.astype(BF16)
        grad_mixed_near = nn(grad_branch, out_near).astype(BF16)
        grad_mixed_far = nn(grad_branch, out_far).astype(BF16)
        grad_mixed = jnp.concatenate(
            [
                jnp.where(low_first, grad_mixed_near, grad_mixed_far),
                jnp.where(low_first, grad_mixed_far, grad_mixed_near),
            ],
            axis=1,
        )
        grad_heads = lax.all_to_all(
            jnp.swapaxes(grad_mixed.reshape(span_rows, span_count, block_rows), 0, 1),
            ("rep", "seq"),
            0,
            0,
            tiled=True,
        ).reshape(total, block_rows)
        grad_projected, gate_sums = attend_back(
            length, gate_here, projected, memory_here, norm_here, dot_read, lse, grad_heads
        )
        grad_near = lax.dynamic_slice_in_dim(grad_projected, core * half_total, half_total, 0)
        grad_far = lax.dynamic_slice_in_dim(
            grad_projected, (1 - core) * half_total, half_total, 0
        )
        grad_one_far = swap(nn(grad_far, head_weight).astype(BF16))
        grad_one_near = (nn(grad_near, head_weight) + grad_one_far.astype(F32)).astype(BF16)
        grad_one = line_scatter(grad_one_near, "seq")
        rows_float = own_rows[m].astype(F32)
        scale_one = lax.rsqrt(jnp.mean(rows_float * rows_float, axis=-1, keepdims=True) + EPSILON)
        normed_one = rows_float * scale_one
        grad_scaled_one = grad_one * gain_one
        grad_tokens = (
            grad_after
            + scale_one
            * (
                grad_scaled_one
                - normed_one * jnp.mean(grad_scaled_one * normed_one, axis=-1, keepdims=True)
            )
        ).astype(BF16)
        saved.append(
            dict(
                grad_tokens=grad_tokens,
                gains_one=jnp.sum(grad_one * normed_one, axis=0),
                gains_two=jnp.sum(grad_two * normed_two, axis=0),
                gate=jnp.sum(gate_sums, axis=(1, 2)),
                qkv=tn(grad_near, hidden_near) + tn(grad_far, hidden_far),
                out_near=tn(grad_branch, mixed_near),
                out_far=tn(grad_branch, mixed_far),
                rows=rows_all,
                grads=grad_rows[m],
                hidden=hidden,
                grad_gates=grad_gates,
                grad_ups=grad_ups,
            )
        )

    def joined(name):
        return functools.reduce(jnp.add, [s[name] for s in saved])

    units = inner_near.shape[0]

    def unit_grads(left, right):
        def part(start):
            return functools.reduce(
                jnp.add, [tn(s[left][:, start : start + units], s[right]) for s in saved]
            )

        far_part = swap(part(units).astype(BF16))
        near_part = (part(0) + far_part.astype(F32)).astype(BF16)
        mine = line_scatter(near_part, "seq").astype(BF16)
        other = swap(mine)
        return jnp.concatenate(
            [jnp.where(core == 0, mine, other), jnp.where(core == 0, other, mine)], axis=0
        ).astype(F32)

    grad_down = unit_grads("hidden", "grads")
    grad_inner = jnp.concatenate(
        [unit_grads("grad_gates", "rows"), unit_grads("grad_ups", "rows")], axis=1
    )

    out_other = swap(joined("out_far").astype(BF16))
    out_mine = (joined("out_near") + out_other.astype(F32)).astype(BF16)
    shard_out = out_weight.shape[0]
    out_mine = out_mine.reshape(dp_count, seq_count * shard_out, half_width)
    pieces = []
    side_rows = seq_count * shard_out // 2
    for side in range(2):
        for k in orders[side]:
            owned = lax.dynamic_index_in_dim(out_mine, column ^ k, 0, keepdims=False)
            pieces.append(owned[side * side_rows : (side + 1) * side_rows])
    out_column = cube_scatter(jnp.concatenate(pieces, axis=0), "dp").astype(BF16)
    out_mine = line_scatter(out_column, "seq").astype(BF16)
    out_other = swap(out_mine)
    grad_out = jnp.concatenate(
        [jnp.where(core == 0, out_mine, out_other), jnp.where(core == 0, out_other, out_mine)],
        axis=1,
    ).astype(F32)

    qkv_low = joined("qkv").astype(BF16).reshape(3, block_rows, width)
    qkv_low = jnp.concatenate([qkv_low, jnp.zeros((1, block_rows, width), BF16)], axis=0)
    which = [
        [3] * (span_count * dp_count) for _ in range(1)
    ][0]
    for part in range(3):
        for owner in range(span_count):
            col = (part * span_count + owner) // per_column
            which[owner * dp_count + col] = part
    pieces = []
    for side in range(2):
        for k in orders[side]:
            part = pick(which, span * dp_count + (column ^ k))
            block = lax.dynamic_index_in_dim(qkv_low, part, 0, keepdims=False)
            pieces.append(block[side * half_block : (side + 1) * half_block])
    qkv_block = cube_scatter(jnp.concatenate(pieces, axis=0), "dp").astype(BF16)
    returned = jnp.zeros(((per_shard + 1) * unit, width), BF16)
    for group in rounds:
        send, slot, pairs = [0] * devices, [per_shard] * devices, []
        for c, col, source, target, from_unit, to_unit in group:
            a = device_number(c, col, target, dp_count, seq_count)
            b = device_number(c, col, source, dp_count, seq_count)
            send[a], slot[b] = to_unit, from_unit
            pairs.append((a, b))
        piece = lax.dynamic_slice_in_dim(qkv_block, pick(send, number) * unit, unit, 0)
        piece = lax.ppermute(piece, ALL, pairs)
        returned = lax.dynamic_update_slice_in_dim(returned, piece, pick(slot, number) * unit, 0)
    returned = returned[: per_shard * unit]
    grad_qkv = returned.astype(F32) + swap(returned).astype(F32)

    gate_terms = joined("gate") * gate_here * (1.0 - gate_here)
    gate_row = lax.dynamic_update_slice_in_dim(
        jnp.zeros((head_count,), F32), gate_terms, span * heads_here, 0
    )
    small = jnp.concatenate([joined("gains_one"), joined("gains_two"), gate_row])
    small = jnp.sum(lax.all_gather(small, ALL, axis=0), axis=0)
    shard_gain = norm_gains.shape[1]
    gain_at = (column * seq_count + place) * shard_gain
    grad_gains = lax.dynamic_slice_in_dim(
        small[: 2 * width].reshape(2, width), gain_at, shard_gain, 1
    )
    grad_gate = small[2 * width :]
    return (
        jnp.stack(outputs)[:, None],
        jnp.stack(new_memories)[:, None],
        jnp.stack(new_norms)[:, None],
        jnp.stack([s["grad_tokens"] for s in saved])[:, None],
        grad_qkv,
        grad_out,
        grad_gains,
        grad_gate,
        grad_inner,
        grad_down,
    )


def solution(mesh):
    placed = (
        P(None, "dp", ("rep", "seq"), None),
        P(None, "dp"),
        P(None, "dp", None, None, None),
        P(None, "dp", None, None),
        P(("dp", "seq"), None),
        P(("dp", "seq"), None),
        P(None, ("dp", "seq")),
        P(),
        P(("dp", "seq"), None),
        P(("dp", "seq"), None),
        P(None, "dp", ("rep", "seq"), None),
    )
    return jax.shard_map(
        shards,
        mesh=mesh,
        in_specs=placed,
        out_specs=(
            P(None, "dp", ("rep", "seq"), None),
            P(None, "dp", ("rep", "seq"), None, None),
            P(None, "dp", ("rep", "seq"), None),
            P(None, "dp", ("rep", "seq"), None),
            P(("dp", "seq"), None),
            P(("dp", "seq"), None),
            P(None, ("dp", "seq")),
            P(),
            P(("dp", "seq"), None),
            P(("dp", "seq"), None),
        ),
        check_vma=False,
    )
```

```python
import functools
import math

import jax
import jax.numpy as jnp
from jax import lax
from jax.experimental import pallas as pl
from jax.experimental.pallas import tpu as pltpu
from jax.sharding import PartitionSpec as P

EPSILON = 1e-05
LOG2E = 1.4426950408889634
NEG = -1e30
F32 = jnp.float32
BF16 = jnp.bfloat16
ALL = ("rep", "dp", "seq")


def nt(left_side, right_side):
    return lax.dot_general(
        left_side, right_side, (((1,), (1,)), ((), ())), preferred_element_type=F32
    )


def nn(left_side, right_side):
    return lax.dot_general(
        left_side, right_side, (((1,), (0,)), ((), ())), preferred_element_type=F32
    )


def tn(left_side, right_side):
    return lax.dot_general(
        left_side, right_side, (((0,), (0,)), ((), ())), preferred_element_type=F32
    )


def elu_one(values):
    return jnp.where(values > 0.0, values + 1.0, jnp.exp(jnp.minimum(values, 0.0)))


def project_kernel(rows_ref, gain_ref, weight_ref, hidden_ref, projected_ref):
    rows = rows_ref[...].astype(F32)
    scale = lax.rsqrt(jnp.mean(rows * rows, axis=-1, keepdims=True) + EPSILON)
    hidden = (rows * scale * gain_ref[...]).astype(BF16)
    hidden_ref[...] = hidden
    projected_ref[...] = nt(hidden, weight_ref[...]).astype(BF16)


def project(rows, gain, weight):
    count, width = rows.shape
    outs = weight.shape[0]
    block = min(256, count)
    return pl.pallas_call(
        project_kernel,
        grid=(count // block,),
        in_specs=[
            pl.BlockSpec((block, width), lambda i: (i, 0)),
            pl.BlockSpec((1, width), lambda i: (0, 0)),
            pl.BlockSpec((outs, width), lambda i: (0, 0)),
        ],
        out_specs=[
            pl.BlockSpec((block, width), lambda i: (i, 0)),
            pl.BlockSpec((block, outs), lambda i: (i, 0)),
        ],
        out_shape=[
            jax.ShapeDtypeStruct((count, width), BF16),
            jax.ShapeDtypeStruct((count, outs), BF16),
        ],
        compiler_params=pltpu.CompilerParams(vmem_limit_bytes=32 << 20),
        cost_estimate=pl.CostEstimate(
            flops=2 * count * width * outs,
            bytes_accessed=4 * count * width + 2 * outs * (width + count),
            transcendentals=count,
        ),
        name="project",
    )(rows, gain, weight)


def attend_kernel(
    block,
    length_ref,
    gate_ref,
    q_ref,
    k_ref,
    v_ref,
    mem_ref,
    norm_ref,
    mixed_ref,
    dot_ref,
    lse_ref,
    new_mem_ref,
    new_norm_ref,
    v_turned,
):
    head, step = pl.program_id(0), pl.program_id(1)
    length = length_ref[0]
    total, width = k_ref.shape
    memory = mem_ref[0]
    norm_row = norm_ref[0]
    memory_low = memory.astype(BF16)

    @pl.when(step == 0)
    def _():
        v_turned[...] = v_ref[...].T
        key_sig = elu_one(k_ref[...].astype(F32))
        below = jnp.sum(key_sig * norm_row, axis=-1, keepdims=True)
        recalled = nn(key_sig.astype(BF16), memory_low) / below
        change = v_ref[...].astype(F32) - recalled
        live = lax.broadcasted_iota(jnp.int32, (total, width), 0) < length
        kept = jnp.where(live, key_sig, 0.0)
        new_mem_ref[0] = memory + tn(kept.astype(BF16), change.astype(BF16))
        new_norm_ref[0] = norm_row + jnp.sum(kept, axis=0, keepdims=True)

    queries = q_ref[...]
    factor = LOG2E * width ** (-0.5)

    def visit(at, carry, masked):
        high, mass, acc = carry
        start = pl.multiple_of(at * block, block)
        scores = nt(k_ref[pl.ds(start, block), :], queries) * factor
        if masked:
            key_at = start + lax.broadcasted_iota(jnp.int32, (block, block), 0)
            query_at = step * block + lax.broadcasted_iota(jnp.int32, (block, block), 1)
            scores = jnp.where((key_at <= query_at) & (key_at < length), scores, NEG)
        higher = jnp.maximum(high, jnp.max(scores, axis=0, keepdims=True))
        weights = jnp.exp2(scores - higher)
        shrink = jnp.exp2(high - higher)
        mass = mass * shrink + jnp.sum(weights, axis=0, keepdims=True)
        acc = acc * shrink + nn(v_turned[:, pl.ds(start, block)], weights.astype(BF16))
        return higher, mass, acc

    full = jnp.minimum(step, length // block)
    end = jnp.minimum(step + 1, (length + block - 1) // block)
    carry = (
        jnp.full((1, block), NEG, F32),
        jnp.zeros((1, block), F32),
        jnp.zeros((width, block), F32),
    )
    carry = lax.fori_loop(0, full, functools.partial(visit, masked=False), carry)
    high, mass, acc = lax.fori_loop(full, end, functools.partial(visit, masked=True), carry)
    dot_read = (acc / mass).T
    query_sig = elu_one(queries.astype(F32))
    below = jnp.sum(query_sig * norm_row, axis=-1, keepdims=True)
    mem_read = nn(query_sig.astype(BF16), memory_low) / below
    gate = gate_ref[head]
    mixed_ref[...] = (gate * mem_read + (1.0 - gate) * dot_read).astype(BF16)
    dot_ref[...] = dot_read
    lse_ref[0] = high + jnp.log2(mass)


def attend(length, gate, projected, memory, normalizer):
    total = projected.shape[0]
    heads, width = normalizer.shape[0], normalizer.shape[2]
    block = min(512, total)
    smem = pl.BlockSpec(memory_space=pltpu.SMEM)
    return pl.pallas_call(
        functools.partial(attend_kernel, block),
        grid=(heads, total // block),
        in_specs=[
            smem,
            smem,
            pl.BlockSpec((block, width), lambda h, i: (i, h)),
            pl.BlockSpec((total, width), lambda h, i: (0, heads + h)),
            pl.BlockSpec((total, width), lambda h, i: (0, 2 * heads + h)),
            pl.BlockSpec((1, width, width), lambda h, i: (h, 0, 0)),
            pl.BlockSpec((1, 1, width), lambda h, i: (h, 0, 0)),
        ],
        out_specs=[
            pl.BlockSpec((block, width), lambda h, i: (i, h)),
            pl.BlockSpec((block, width), lambda h, i: (i, h)),
            pl.BlockSpec((1, 1, block), lambda h, i: (h, 0, i)),
            pl.BlockSpec((1, width, width), lambda h, i: (h, 0, 0)),
            pl.BlockSpec((1, 1, width), lambda h, i: (h, 0, 0)),
        ],
        out_shape=[
            jax.ShapeDtypeStruct((total, heads * width), BF16),
            jax.ShapeDtypeStruct((total, heads * width), F32),
            jax.ShapeDtypeStruct((heads, 1, total), F32),
            jax.ShapeDtypeStruct((heads, width, width), F32),
            jax.ShapeDtypeStruct((heads, 1, width), F32),
        ],
        scratch_shapes=[pltpu.VMEM((width, total), BF16)],
        compiler_params=pltpu.CompilerParams(vmem_limit_bytes=40 << 20),
        cost_estimate=pl.CostEstimate(
            flops=4 * heads * total * total * width,
            bytes_accessed=heads * total * width * 12,
            transcendentals=heads * total * total,
        ),
        name="attend",
    )(length, gate, projected, projected, projected, memory, normalizer)


def attend_back_kernel(
    block,
    length_ref,
    gate_ref,
    q_ref,
    k_ref,
    v_ref,
    mem_ref,
    norm_ref,
    dot_ref,
    lse_ref,
    grad_ref,
    out_ref,
    gate_sum_ref,
    k_turned,
    k_sum,
    v_sum,
):
    head, step = pl.program_id(0), pl.program_id(1)
    heads, steps = pl.num_programs(0), pl.num_programs(1)
    length = length_ref[0]
    total, width = k_ref.shape
    gate = gate_ref[head]

    @pl.when(step == 0)
    def _():
        k_turned[...] = k_ref[...].T
        k_sum[...] = jnp.zeros_like(k_sum)
        v_sum[...] = jnp.zeros_like(v_sum)
        gate_sum_ref[...] = jnp.zeros_like(gate_sum_ref)

    queries = q_ref[...]
    query_float = queries.astype(F32)
    grad_mixed = grad_ref[...].astype(F32)
    grad_dot = ((1.0 - gate) * grad_mixed).astype(BF16)
    dot_read = dot_ref[...]
    offset = jnp.sum((grad_dot.astype(F32) * dot_read).T, axis=0, keepdims=True)
    lse = lse_ref[0]
    scale = width ** (-0.5)
    factor = LOG2E * scale

    def visit(at, acc, masked):
        start = pl.multiple_of(at * block, block)
        here = pl.ds(start, block)
        scores = nt(k_ref[here, :], queries) * factor
        weights = jnp.exp2(scores - lse)
        if masked:
            key_at = start + lax.broadcasted_iota(jnp.int32, (block, block), 0)
            query_at = step * block + lax.broadcasted_iota(jnp.int32, (block, block), 1)
            weights = jnp.where((key_at <= query_at) & (key_at < length), weights, 0.0)
        grad_probs = nt(v_ref[here, :], grad_dot)
        grad_scores = (weights * (grad_probs - offset) * scale).astype(BF16)
        v_sum[here, :] += nn(weights.astype(BF16), grad_dot)
        k_sum[here, :] += nn(grad_scores, queries)
        return acc + nn(k_turned[:, here], grad_scores)

    full = jnp.minimum(step, length // block)
    end = jnp.minimum(step + 1, (length + block - 1) // block)
    acc = jnp.zeros((width, block), F32)
    acc = lax.fori_loop(0, full, functools.partial(visit, masked=False), acc)
    acc = lax.fori_loop(full, end, functools.partial(visit, masked=True), acc)

    memory_low = mem_ref[0].astype(BF16)
    norm_row = norm_ref[0]
    query_sig = elu_one(query_float)
    below = jnp.sum(query_sig * norm_row, axis=-1, keepdims=True)
    numerator = nn(query_sig.astype(BF16), memory_low)
    inverse = 1.0 / below
    grad_read = gate * grad_mixed
    grad_below = -jnp.sum(grad_read * numerator, axis=-1, keepdims=True) * inverse * inverse
    grad_sig = nt((grad_read * inverse).astype(BF16), memory_low) + grad_below * norm_row
    slope = jnp.where(query_float > 0.0, 1.0, jnp.exp(jnp.minimum(query_float, 0.0)))
    rows = pl.ds(pl.multiple_of(step * block, block), block)
    out_ref[rows, pl.ds(pl.multiple_of(head * width, width), width)] = (
        acc.T + grad_sig * slope
    ).astype(BF16)
    gate_sum_ref[0] += jnp.sum(
        grad_mixed * (numerator * inverse - dot_read), axis=0, keepdims=True
    )

    @pl.when(step == steps - 1)
    def _():
        k_at = pl.multiple_of((heads + head) * width, width)
        v_at = pl.multiple_of((2 * heads + head) * width, width)
        out_ref[:, pl.ds(k_at, width)] = k_sum[...].astype(BF16)
        out_ref[:, pl.ds(v_at, width)] = v_sum[...].astype(BF16)


def attend_back(length, gate, projected, memory, normalizer, dot_read, lse, grad_mixed):
    total = projected.shape[0]
    heads, width = normalizer.shape[0], normalizer.shape[2]
    block = min(512, total)
    smem = pl.BlockSpec(memory_space=pltpu.SMEM)
    return pl.pallas_call(
        functools.partial(attend_back_kernel, block),
        grid=(heads, total // block),
        in_specs=[
            smem,
            smem,
            pl.BlockSpec((block, width), lambda h, i: (i, h)),
            pl.BlockSpec((total, width), lambda h, i: (0, heads + h)),
            pl.BlockSpec((total, width), lambda h, i: (0, 2 * heads + h)),
            pl.BlockSpec((1, width, width), lambda h, i: (h, 0, 0)),
            pl.BlockSpec((1, 1, width), lambda h, i: (h, 0, 0)),
            pl.BlockSpec((block, width), lambda h, i: (i, h)),
            pl.BlockSpec((1, 1, block), lambda h, i: (h, 0, i)),
            pl.BlockSpec((block, width), lambda h, i: (i, h)),
        ],
        out_specs=[
            pl.BlockSpec((total, 3 * heads * width), lambda h, i: (0, 0)),
            pl.BlockSpec((1, 1, width), lambda h, i: (h, 0, 0)),
        ],
        out_shape=[
            jax.ShapeDtypeStruct((total, 3 * heads * width), BF16),
            jax.ShapeDtypeStruct((heads, 1, width), F32),
        ],
        scratch_shapes=[
            pltpu.VMEM((width, total), BF16),
            pltpu.VMEM((total, width), F32),
            pltpu.VMEM((total, width), F32),
        ],
        compiler_params=pltpu.CompilerParams(vmem_limit_bytes=40 << 20),
        cost_estimate=pl.CostEstimate(
            flops=10 * heads * total * total * width,
            bytes_accessed=heads * total * width * 20,
            transcendentals=heads * total * total,
        ),
        name="attend_back",
    )(length, gate, projected, projected, projected, memory, normalizer, dot_read, lse, grad_mixed)


def unit_kernel(
    rows_ref, grad_ref, inner_ref, down_ref, hidden_ref, grad_gate_ref, grad_up_ref
):
    width = rows_ref.shape[1]
    rows = rows_ref[...]
    gates = nt(rows, inner_ref[:, :width])
    ups = nt(rows, inner_ref[:, width:])
    grad_hidden = nt(grad_ref[...], down_ref[...])
    sigmoid = 1.0 / (1.0 + jnp.exp(-gates))
    silu = gates * sigmoid
    hidden_ref[...] = (silu * ups).astype(BF16)
    grad_gate_ref[...] = (
        grad_hidden * ups * (sigmoid * (1.0 + gates * (1.0 - sigmoid)))
    ).astype(BF16)
    grad_up_ref[...] = (grad_hidden * silu).astype(BF16)


def unit_pass(rows, grads, inner, down):
    count, width = rows.shape
    units = inner.shape[0]
    tile = min(256, units)
    resident = pl.BlockSpec((count, width), lambda t: (0, 0), pipeline_mode=pl.Buffered(1))
    column = pl.BlockSpec((count, tile), lambda t: (0, t))
    unit_shape = jax.ShapeDtypeStruct((count, units), BF16)
    return pl.pallas_call(
        unit_kernel,
        grid=(units // tile,),
        in_specs=[
            resident,
            resident,
            pl.BlockSpec((tile, 2 * width), lambda t: (t, 0)),
            pl.BlockSpec((tile, width), lambda t: (t, 0)),
        ],
        out_specs=[column] * 3,
        out_shape=[unit_shape] * 3,
        compiler_params=pltpu.CompilerParams(vmem_limit_bytes=56 << 20),
        cost_estimate=pl.CostEstimate(
            flops=2 * 3 * count * width * units,
            bytes_accessed=units * (6 * width + 6 * count) + 4 * count * width,
            transcendentals=count * units,
        ),
        name="unit_pass",
    )(rows, grads, inner, down)


def row_kernel(*refs):
    hidden, gates, ups, gate_w, up_w, down_w = (refs[2 * i : 2 * i + 2] for i in range(6))
    out_ref, grad_two_ref = refs[12:]
    grad_two_ref[...] = (
        nn(gates[0][...], gate_w[0][...])
        + nn(gates[1][...], gate_w[1][...])
        + nn(ups[0][...], up_w[0][...])
        + nn(ups[1][...], up_w[1][...])
    ).astype(BF16)
    out_ref[...] = (
        nn(hidden[0][...], down_w[0][...]) + nn(hidden[1][...], down_w[1][...])
    ).astype(BF16)


def row_pass(hidden, grad_gates, grad_ups, inner, down):
    count, units = hidden[0].shape
    width = down[0].shape[1]
    tile = min(256, width)
    tiles = width // tile
    resident = pl.BlockSpec((count, units), lambda t: (0, 0), pipeline_mode=pl.Buffered(1))
    low = pl.BlockSpec((units, tile), lambda t: (0, t))
    high = pl.BlockSpec((units, tile), lambda t: (0, tiles + t))
    column = pl.BlockSpec((count, tile), lambda t: (0, t))
    row_shape = jax.ShapeDtypeStruct((count, width), BF16)
    return pl.pallas_call(
        row_kernel,
        grid=(tiles,),
        in_specs=[resident] * 6 + [low, low, high, high, low, low],
        out_specs=[column] * 2,
        out_shape=[row_shape] * 2,
        compiler_params=pltpu.CompilerParams(vmem_limit_bytes=56 << 20),
        cost_estimate=pl.CostEstimate(
            flops=2 * 3 * count * width * 2 * units,
            bytes_accessed=12 * units * (width + count) + 4 * count * width,
            transcendentals=0,
        ),
        name="row_pass",
    )(*hidden, *grad_gates, *grad_ups, *inner, *inner, *down)


def weight_kernel(pairs, *refs):
    out_ref = refs[-1]
    total = tn(refs[0][...], refs[1][...])
    for at in range(1, pairs):
        total += tn(refs[2 * at][...], refs[2 * at + 1][...])
    if len(refs) > 2 * pairs + 1:
        total += refs[2 * pairs][...].astype(F32)
    out_ref[...] = total.astype(BF16)


def weight_pass(pairs, extra=None):
    size, width = pairs[0][0].shape[1], pairs[0][1].shape[1]
    tile = min(256, size)
    in_specs, operands, flops, moved = [], [], 0, 2 * size * width
    for left, right in pairs:
        count = left.shape[0]
        in_specs.append(pl.BlockSpec((count, tile), lambda t: (0, t)))
        in_specs.append(
            pl.BlockSpec((count, width), lambda t: (0, 0), pipeline_mode=pl.Buffered(1))
        )
        operands += [left, right]
        flops += 2 * count * size * width
        moved += 2 * count * (size + width)
    if extra is not None:
        in_specs.append(pl.BlockSpec((tile, width), lambda t: (t, 0)))
        operands.append(extra)
        moved += 2 * size * width
    return pl.pallas_call(
        functools.partial(weight_kernel, len(pairs)),
        grid=(size // tile,),
        in_specs=in_specs,
        out_specs=pl.BlockSpec((tile, width), lambda t: (t, 0)),
        out_shape=jax.ShapeDtypeStruct((size, width), BF16),
        compiler_params=pltpu.CompilerParams(vmem_limit_bytes=56 << 20),
        cost_estimate=pl.CostEstimate(flops=flops, bytes_accessed=moved, transcendentals=0),
        name="weight_pass",
    )(*operands)


def back_kernel(half_ref, grad_ref, weight_ref, rows_ref, out_ref, gain_ref):
    @pl.when(pl.program_id(0) == 0)
    def _():
        gain_ref[...] = jnp.zeros_like(gain_ref)

    part = nn(grad_ref[...], weight_ref[...])
    out_ref[...] = part.astype(BF16)
    rows = rows_ref[...].astype(F32)
    scale = lax.rsqrt(jnp.mean(rows * rows, axis=-1, keepdims=True) + EPSILON)
    gain_ref[...] += jnp.sum(part * (rows * scale), axis=0, keepdims=True)


def project_back(half, grads, weight, rows):
    count, outs = grads.shape[0] // 2, grads.shape[1]
    width = weight.shape[1]
    block = min(256, count)
    steps = count // block
    return pl.pallas_call(
        back_kernel,
        grid_spec=pltpu.PrefetchScalarGridSpec(
            num_scalar_prefetch=1,
            grid=(steps,),
            in_specs=[
                pl.BlockSpec((block, outs), lambda i, at: (at[0] * steps + i, 0)),
                pl.BlockSpec((outs, width), lambda i, at: (0, 0)),
                pl.BlockSpec((block, width), lambda i, at: (at[0] * steps + i, 0)),
            ],
            out_specs=[
                pl.BlockSpec((block, width), lambda i, at: (i, 0)),
                pl.BlockSpec((1, width), lambda i, at: (0, 0)),
            ],
        ),
        out_shape=[
            jax.ShapeDtypeStruct((count, width), BF16),
            jax.ShapeDtypeStruct((1, width), F32),
        ],
        compiler_params=pltpu.CompilerParams(vmem_limit_bytes=40 << 20),
        cost_estimate=pl.CostEstimate(
            flops=2 * count * width * outs,
            bytes_accessed=4 * count * width + 2 * outs * (width + count),
            transcendentals=count,
        ),
        name="project_back",
    )(jnp.reshape(half, (1,)).astype(jnp.int32), grads, weight, rows)


def swap(values):
    return lax.ppermute(values, "rep", [(0, 1), (1, 0)])


def after(values, *earlier):
    earlier = [e for e in earlier if e is not None]
    return lax.optimization_barrier((values, *earlier))[0] if earlier else values


def add_low(left_side, right_side):
    return (left_side.astype(F32) + right_side.astype(F32)).astype(BF16)


def line_gather(values, axis):
    count = lax.axis_size(axis)
    here = lax.axis_index(axis)
    rows = values.shape[0]
    table = jnp.zeros(((3 * count - 2) * rows,) + values.shape[1:], values.dtype)

    def put(table, piece, origin):
        return lax.dynamic_update_slice_in_dim(table, piece, (origin + count - 1) * rows, 0)

    table = put(table, values, here)
    rising = falling = values
    for hop in range(1, count):
        rising = lax.ppermute(
            rising, axis, [(a, a + 1) for a in range(count - 1) if a >= hop - 1]
        )
        falling = lax.ppermute(
            falling, axis, [(a, a - 1) for a in range(1, count) if a + hop - 1 < count]
        )
        table = put(table, rising, here - hop)
        table = put(table, falling, here + hop)
    return table[(count - 1) * rows : (2 * count - 1) * rows]


def line_scatter(values, axis, pins=()):
    count = lax.axis_size(axis)
    here = lax.axis_index(axis)
    rows = values.shape[0] // count

    def block(owner):
        start = jnp.clip(owner, 0, count - 1) * rows
        return lax.dynamic_slice_in_dim(values, start, rows, 0).astype(F32)

    rising = falling = None
    for hop in range(1, count):
        reach = count - hop
        up, down = block(here + reach), block(here - reach)
        if rising is not None:
            up, down = up + rising.astype(F32), down + falling.astype(F32)
        rising = lax.ppermute(
            up.astype(BF16), axis, [(a, a + 1) for a in range(count) if a + reach < count]
        )
        falling = lax.ppermute(
            down.astype(BF16), axis, [(a, a - 1) for a in range(count) if a - reach >= 0]
        )
        if hop <= len(pins):
            rising, falling = after(rising, pins[hop - 1]), after(falling, pins[hop - 1])
    return block(here) + rising.astype(F32) + falling.astype(F32)


def cube_bits(count):
    bits = [1 << b for b in range(count.bit_length() - 1)]
    return bits, bits[::-1]


def cube_order(bits):
    order = [0]
    for bit in reversed(bits):
        order = order + [k | bit for k in order]
    return order


def cube_gather(values, axis):
    count = lax.axis_size(axis)
    half = values.shape[0] // 2
    parts = []
    for bits, start in zip(cube_bits(count), (0, half)):
        held = {0: values[start : start + half]}
        for bit in bits:
            pairs = [(a, a ^ bit) for a in range(count)]
            held.update({k ^ bit: lax.ppermute(v, axis, pairs) for k, v in list(held.items())})
        parts += [held[k] for k in cube_order(bits)]
    return jnp.concatenate(parts, axis=0)


def cube_scatter(values, axis, pins=()):
    count = lax.axis_size(axis)
    half = values.shape[0] // 2
    parts = []
    for bits, start in zip(cube_bits(count), (0, half)):
        held = values[start : start + half]
        for at, bit in enumerate(bits):
            pairs = [(a, a ^ bit) for a in range(count)]
            keep = held.shape[0] // 2
            got = lax.ppermute(held[keep:].astype(BF16), axis, pairs)
            if at < len(pins):
                got = after(got, pins[at])
            held = held[:keep].astype(F32) + got.astype(F32)
        parts.append(held)
    return jnp.concatenate(parts, axis=0)


def remote(source, target, sent, landed, device):
    return pltpu.make_async_remote_copy(
        src_ref=source,
        dst_ref=target,
        send_sem=sent,
        recv_sem=landed,
        device_id=device,
        device_id_type=pl.DeviceIdType.MESH,
    )


def greet(devices):
    barrier = pltpu.get_barrier_semaphore()
    for device in devices:
        pl.semaphore_signal(barrier, inc=1, device_id=device, device_id_type=pl.DeviceIdType.MESH)
    pl.semaphore_wait(barrier, len(devices))


def heads_kernel(
    sizes,
    qkv_ref,
    gain_ref,
    head_ref,
    gains_ref,
    landed,
    unit_sent,
    unit_here,
    block_sent,
    block_here,
    line_sent,
    line_here,
    cube_sent,
    cube_here,
    local,
):
    dp_count, seq_count, unit, per_shard, per_block, per_column = sizes
    span_count = 2 * seq_count
    block_rows = unit * per_block
    core, column, place = lax.axis_index("rep"), lax.axis_index("dp"), lax.axis_index("seq")
    span, shard = core * seq_count + place, column * seq_count + place
    line = [(core, column, (place + k) % seq_count) for k in range(1, seq_count)]
    cube = [(core, (column + k) % dp_count, place) for k in range(1, dp_count)]
    greet(line + cube)

    gains = []
    for k, device in enumerate(line):
        gains.append(
            remote(gain_ref, gains_ref.at[shard], line_sent.at[k], line_here.at[k], device)
        )
    for copy in gains:
        copy.start()
    own_gain = pltpu.make_async_copy(gain_ref, gains_ref.at[shard], local.at[0])
    own_gain.start()

    def rows(ref, at, size):
        return ref.at[pl.ds(pl.multiple_of(at * size, size), size)]

    def unit_copy(i):
        number = shard * per_shard + i
        owner = (number // per_block) % span_count
        source, target = rows(qkv_ref, i, unit), rows(landed, number % per_block, unit)
        far = remote(
            source,
            target,
            unit_sent.at[i],
            unit_here.at[number % per_block],
            (core, column, owner % seq_count),
        )
        near = pltpu.make_async_copy(source, target, local.at[1 + i])
        mine = owner // seq_count == core
        stays = owner % seq_count == place
        return far, near, mine & jnp.logical_not(stays), mine & stays

    for i in range(per_shard):
        far, near, leaves, stays = unit_copy(i)
        pl.when(leaves)(far.start)
        pl.when(stays)(near.start)
    for i in range(per_shard):
        _, near, _, stays = unit_copy(i)
        pl.when(stays)(near.wait)

    def block_copies(part):
        target = rows(head_ref, part, block_rows)
        far = [
            remote(landed, target, block_sent.at[k], block_here.at[part], device)
            for k, device in enumerate(cube)
        ]
        return far, pltpu.make_async_copy(landed, target, local.at[0])

    own_gain.wait()
    for part in range(3):
        number = part * span_count + span

        @pl.when(number // per_column == column)
        def _():
            for j in range(per_block):
                source = ((number * per_block + j) // per_shard) % seq_count

                @pl.when(source != place)
                def _():
                    here = rows(landed, j, unit)
                    remote(here, here, unit_sent.at[0], unit_here.at[j], line[0]).wait_recv()

            far, near = block_copies(part)
            for copy in far:
                copy.start()
            near.start()

    for copy in gains:
        copy.wait()
    mine = gains_ref.at[pl.ds(column * seq_count, seq_count)]
    gains = [
        remote(mine, mine, cube_sent.at[k], cube_here.at[k], device)
        for k, device in enumerate(cube)
    ]
    for copy in gains:
        copy.start()
    for part in range(3):
        number = part * span_count + span
        far, near = block_copies(part)

        @pl.when(number // per_column == column)
        def _():
            near.wait()
            for copy in far:
                copy.wait_send()

        @pl.when(number // per_column != column)
        def _():
            far[0].wait_recv()

    for k, copy in enumerate(gains):
        copy.wait_send()
        origin = (column + dp_count - k - 1) % dp_count
        theirs = gains_ref.at[pl.ds(origin * seq_count, seq_count)]
        remote(theirs, theirs, cube_sent.at[k], cube_here.at[k], cube[k]).wait_recv()
    for i in range(per_shard):
        far, _, leaves, _ = unit_copy(i)
        pl.when(leaves)(far.wait_send)


def gather_heads(qkv_weight, gains, sizes):
    dp_count, seq_count, unit, per_shard, per_block, _ = sizes
    width = qkv_weight.shape[1]
    block_rows = unit * per_block
    anywhere = pl.BlockSpec(memory_space=pl.ANY)
    dma = pltpu.SemaphoreType.DMA
    return pl.pallas_call(
        functools.partial(heads_kernel, sizes),
        in_specs=[anywhere, anywhere],
        out_specs=[anywhere, anywhere],
        out_shape=[
            jax.ShapeDtypeStruct((3 * block_rows, width), BF16),
            jax.ShapeDtypeStruct((dp_count * seq_count, *gains.shape), F32),
        ],
        scratch_shapes=[
            pltpu.VMEM((block_rows, width), BF16),
            dma((per_shard,)),
            dma((per_block,)),
            dma((dp_count - 1,)),
            dma((3,)),
            dma((seq_count - 1,)),
            dma((seq_count - 1,)),
            dma((dp_count - 1,)),
            dma((dp_count - 1,)),
            dma((1 + per_shard,)),
        ],
        compiler_params=pltpu.CompilerParams(
            collective_id=0, has_side_effects=True, vmem_limit_bytes=16 << 20
        ),
        cost_estimate=pl.CostEstimate(
            flops=0, bytes_accessed=64 * block_rows * width, transcendentals=0
        ),
        name="gather_heads",
    )(qkv_weight, gains)


def heads_plan(shard_rows, block_rows, dp_count, seq_count, span_count):
    unit = math.gcd(shard_rows, block_rows)
    per_shard, per_block = shard_rows // unit, block_rows // unit
    per_column = 3 * span_count // dp_count
    edges = []
    for u in range(dp_count * seq_count * per_shard):
        shard, block = u // per_shard, u // per_block
        column, source = divmod(shard, seq_count)
        core, target = divmod(block % span_count, seq_count)
        edges.append((core, column, source, target, u % per_shard, u % per_block))
    rounds = []
    for edge in edges:
        core, column, source, target = edge[:4]
        for group in rounds:
            if all(
                (core, column) != e[:2] or (source != e[2] and target != e[3]) for e in group
            ):
                group.append(edge)
                break
        else:
            rounds.append([edge])
    return unit, per_shard, per_block, per_column, rounds


def device_number(core, column, place, dp_count, seq_count):
    return (core * dp_count + column) * seq_count + place


def pick(table, number):
    return jnp.asarray(table, jnp.int32)[number]


def shards(
    tokens,
    lengths,
    memory,
    normalizer,
    qkv_weight,
    out_weight,
    norm_gains,
    gate_logit,
    inner_weight,
    down_weight,
    cotangent,
):
    micros, _, span_rows, width = tokens.shape
    head_count = gate_logit.shape[0]
    head_dim = width // head_count
    dp_count, seq_count = lax.axis_size("dp"), lax.axis_size("seq")
    span_count = 2 * seq_count
    total = span_rows * span_count
    heads_here = head_count // span_count
    block_rows = heads_here * head_dim
    core, column, place = lax.axis_index("rep"), lax.axis_index("dp"), lax.axis_index("seq")
    span = core * seq_count + place
    number = device_number(core, column, place, dp_count, seq_count)
    inner_half = inner_weight.shape[0] // 2

    own_rows = [tokens[m, 0] for m in range(micros)]

    def gather_rows(rows):
        return lax.all_gather(rows, ("rep", "seq"), axis=0, tiled=True)

    all_rows = [gather_rows(own_rows[0])]

    unit, per_shard, per_block, per_column, rounds = heads_plan(
        qkv_weight.shape[0], block_rows, dp_count, seq_count, span_count
    )
    devices = 2 * dp_count * seq_count
    shard_out, shard_gain = out_weight.shape[0], norm_gains.shape[1]
    lanes = -(-shard_gain // 128) * 128
    gain_tile = jnp.zeros((8, lanes), F32)
    gain_tile = lax.dynamic_update_slice(gain_tile, norm_gains.astype(F32), (0, 0))
    head_weight, gains_all = gather_heads(
        qkv_weight, gain_tile, (dp_count, seq_count, unit, per_shard, per_block, per_column)
    )
    gains_all = jnp.swapaxes(gains_all[:, :2, :shard_gain], 0, 1).reshape(2, width)
    gain_one, gain_two = gains_all[0:1], gains_all[1:2]
    orders = [cube_order(bits) for bits in cube_bits(dp_count)]
    spots = [[order.index(k) for k in range(dp_count)] for order in orders]

    def column_block(gathered, half, owner):
        sides = []
        for side in range(2):
            spot = pick(spots[side], owner ^ column) + side * dp_count
            sides.append(lax.dynamic_slice_in_dim(gathered, spot * half, half, 0))
        return sides

    half_block = block_rows // 2
    half_width = width // 2
    out_line = line_gather(
        lax.dynamic_slice_in_dim(out_weight, core * half_width, half_width, 1), "seq"
    )
    for rows in own_rows[1:]:
        all_rows.append(gather_rows(after(rows, all_rows[-1], head_weight)))
    column_out = seq_count * shard_out
    out_blocks = cube_gather(out_line, "dp")
    out_near = []
    for owner in range(dp_count):
        out_near += column_block(out_blocks, column_out // 2, owner)
    out_near = jnp.concatenate(out_near, axis=0)
    out_far = swap(out_near)

    positions = span * span_rows + jnp.arange(span_rows)
    gate_share = jax.nn.sigmoid(gate_logit)
    gate_here = lax.dynamic_slice_in_dim(gate_share, span * heads_here, heads_here, 0)
    near_at, far_at = core * half_width, (1 - core) * half_width
    low_first = core == 0

    saved = []
    outputs, new_memories, new_norms = [], [], []
    for m in range(micros):
        hidden_one, projected = project(all_rows[m], gain_one, head_weight)
        live_rows = (positions < lengths[m, 0]).astype(F32)
        live = cotangent[m, 0].astype(F32) * live_rows[:, None]
        grad_rows = cube_gather(after(live.astype(BF16), projected), "dp")
        if m == 0:
            near_units, near_downs = (
                lax.dynamic_slice_in_dim(w, core * inner_half, inner_half, 0)
                for w in (inner_weight, down_weight)
            )
        memory_here = lax.dynamic_slice_in_dim(memory[m, 0], span * heads_here, heads_here, 0)
        norm_here = lax.dynamic_slice_in_dim(
            normalizer[m, 0], span * heads_here, heads_here, 0
        ).reshape(heads_here, 1, head_dim)
        length = lengths[m]
        mixed_heads, dot_read, lse, new_memory, new_norm = attend(
            length, gate_here, projected, memory_here, norm_here
        )
        if m == 0:
            inner_near = lax.all_gather(
                after(near_units, all_rows[-1]),
                "seq",
                axis=0,
                tiled=True,
            )
        new_memories.append(new_memory)
        new_norms.append(new_norm.reshape(heads_here, head_dim))
        mixed = lax.all_to_all(
            mixed_heads.reshape(span_count, span_rows, block_rows),
            ("rep", "seq"),
            0,
            0,
            tiled=True,
        )
        mixed = jnp.swapaxes(mixed, 0, 1).reshape(span_rows, width)
        mixed_near = lax.dynamic_slice_in_dim(mixed, near_at, half_width, 1)
        mixed_far = lax.dynamic_slice_in_dim(mixed, far_at, half_width, 1)
        after_attn = (
            own_rows[m].astype(F32) + nt(mixed_near, out_near) + nt(mixed_far, out_far)
        )
        scale_two = lax.rsqrt(jnp.mean(after_attn * after_attn, axis=-1, keepdims=True) + EPSILON)
        normed_two = after_attn * scale_two
        hidden_two = (normed_two * gain_two).astype(BF16)
        rows_all = cube_gather(hidden_two, "dp")
        saved.append(
            dict(
                hidden_one=hidden_one,
                projected=projected,
                live=live,
                grads=grad_rows,
                memory=memory_here,
                norm=norm_here,
                length=length,
                dot_read=dot_read,
                lse=lse,
                mixed_heads=mixed_heads,
                mixed_near=mixed_near,
                mixed_far=mixed_far,
                after_attn=after_attn,
                scale_two=scale_two,
                normed_two=normed_two,
                rows=rows_all,
            )
        )

    down_near = lax.all_gather(
        after(near_downs, inner_near, *[s[n] for s in saved for n in ("rows", "grads")]),
        "seq",
        axis=0,
        tiled=True,
    )
    inner_far, down_far = swap(inner_near), swap(down_near)

    inner, down = (inner_near, inner_far), (down_near, down_far)
    last = None
    for s in saved:
        halves = []
        for half in range(2):
            halves.append(unit_pass(after(s["rows"], last), s["grads"], inner[half], down[half]))
            last = halves[-1][0]
        s["hidden"], s["grad_gates"], s["grad_ups"] = zip(*halves)

    def half_grads(left, right, half, earlier, extra=None):
        pairs = [(s[left][half], s[right]) for s in saved]
        pairs[0] = (after(pairs[0][0], earlier), pairs[0][1])
        return weight_pass(pairs, extra)

    def spread(values):
        return lax.psum_scatter(values, "seq", scatter_dimension=0, tiled=True)

    def rows_out(s, *earlier):
        gates = (after(s["grad_gates"][0], *earlier), s["grad_gates"][1])
        s["mlp_part"], s["grad_two_part"] = row_pass(
            s["hidden"], gates, s["grad_ups"], inner, down
        )
        return s["grad_two_part"]

    down_far_sum = half_grads("hidden", "grads", 1, last)
    gate_far_sum = half_grads("grad_gates", "rows", 1, down_far_sum)
    down_sum = half_grads("hidden", "grads", 0, gate_far_sum, swap(down_far_sum))
    down_mine = spread(down_sum)
    last = rows_out(saved[0], down_sum)
    up_far_sum = half_grads("grad_ups", "rows", 1, last)
    gate_sum = half_grads("grad_gates", "rows", 0, up_far_sum, swap(gate_far_sum))
    gate_mine = spread(gate_sum)
    last = gate_sum
    for s in saved[1:]:
        last = rows_out(s, last, down_mine)
    up_sum = half_grads("grad_ups", "rows", 0, last, swap(up_far_sum))
    up_mine = spread(up_sum)
    last = up_sum

    def rows_back(s, pins):
        grad_two = cube_scatter(s["grad_two_part"], "dp", pins)
        grad_scaled = grad_two * gain_two
        normed_two = s["normed_two"]
        s["grad_after"] = s["live"] + s["scale_two"] * (
            grad_scaled
            - normed_two * jnp.mean(grad_scaled * normed_two, axis=-1, keepdims=True)
        )
        s["grad_branch"] = s["grad_after"].astype(BF16)
        s["gains_two"] = jnp.sum(grad_two * normed_two, axis=0)
        grad_mixed_near = nn(s["grad_branch"], out_near).astype(BF16)
        grad_mixed_far = nn(s["grad_branch"], out_far).astype(BF16)
        grad_mixed = jnp.concatenate(
            [
                jnp.where(low_first, grad_mixed_near, grad_mixed_far),
                jnp.where(low_first, grad_mixed_far, grad_mixed_near),
            ],
            axis=1,
        )
        return lax.all_to_all(
            jnp.swapaxes(grad_mixed.reshape(span_rows, span_count, block_rows), 0, 1),
            ("rep", "seq"),
            0,
            0,
            tiled=True,
        ).reshape(total, block_rows)

    def heads_back(s, m, grad_heads):
        s["grad_projected"], gate_sums = attend_back(
            s["length"],
            gate_here,
            s["projected"],
            s["memory"],
            s["norm"],
            s["dot_read"],
            s["lse"],
            grad_heads,
        )
        s["gate"] = jnp.sum(gate_sums, axis=(1, 2))
        part_far, gains_far = project_back(
            1 - core, s["grad_projected"], head_weight, all_rows[m]
        )
        part_near, gains_near = project_back(
            core, after(s["grad_projected"], part_far), head_weight, all_rows[m]
        )
        s["gains_one"] = (gains_far + gains_near)[0]
        return part_near, add_low(part_near, swap(part_far))

    def tokens_back(s, m, grad_one):
        rows_float = own_rows[m].astype(F32)
        scale_one = lax.rsqrt(jnp.mean(rows_float * rows_float, axis=-1, keepdims=True) + EPSILON)
        normed_one = rows_float * scale_one
        grad_scaled = grad_one * gain_one
        return (
            s["grad_after"]
            + scale_one
            * (
                grad_scaled
                - normed_one * jnp.mean(grad_scaled * normed_one, axis=-1, keepdims=True)
            )
        ).astype(BF16)

    heads_grads = [rows_back(s, ()) for s in saved]
    earlier = (last, gate_mine)
    sums = []
    for m, s in enumerate(saved):
        last, part = heads_back(s, m, after(heads_grads[m], *earlier))
        sums.append(part)
        earlier = (last,)
    grad_ones = line_scatter(
        jnp.concatenate(
            [p.reshape(seq_count, span_rows, width) for p in sums], axis=1
        ).reshape(-1, width),
        "seq",
    )
    grad_tokens = [
        tokens_back(s, m, grad_ones[m * span_rows : (m + 1) * span_rows])
        for m, s in enumerate(saved)
    ]
    out_far_sum = weight_pass(
        [(after(s["grad_branch"], last, up_mine), s["mixed_far"]) for s in saved]
    )
    out_near_sum = weight_pass(
        [(after(s["grad_branch"], out_far_sum), s["mixed_near"]) for s in saved]
    )
    qkv_low = weight_pass(
        [(after(s["grad_projected"], out_near_sum), s["hidden_one"]) for s in saved]
    ).reshape(3, block_rows, width)
    for m, s in enumerate(saved):
        mlp_out = cube_scatter(s["mlp_part"], "dp")
        outputs.append((s["after_attn"] + mlp_out).astype(BF16))

    def joined(name):
        return functools.reduce(jnp.add, [s[name] for s in saved])

    def both_cores(mine, axis):
        other = swap(mine)
        size = mine.shape[axis]
        shape = list(mine.shape)
        shape[axis] = 2 * size
        whole = jnp.zeros(shape, F32)
        whole = lax.dynamic_update_slice_in_dim(whole, mine.astype(F32), core * size, axis)
        return lax.dynamic_update_slice_in_dim(
            whole, other.astype(F32), (1 - core) * size, axis
        )

    grad_down = both_cores(down_mine, 0)
    grad_inner = both_cores(jnp.concatenate([gate_mine, up_mine], axis=1), 0)

    out_mine = add_low(out_near_sum, swap(out_far_sum)).reshape(
        dp_count, column_out, half_width
    )
    pieces = []
    for side in range(2):
        for k in orders[side]:
            owned = lax.dynamic_index_in_dim(out_mine, column ^ k, 0, keepdims=False)
            pieces.append(owned[side * column_out // 2 : (side + 1) * column_out // 2])
    out_column = cube_scatter(jnp.concatenate(pieces, axis=0), "dp").astype(BF16)
    grad_out = both_cores(line_scatter(out_column, "seq").astype(BF16), 1)

    qkv_low = jnp.concatenate([qkv_low, jnp.zeros((1, block_rows, width), BF16)], axis=0)
    which = [3] * (span_count * dp_count)
    for part in range(3):
        for owner in range(span_count):
            which[owner * dp_count + (part * span_count + owner) // per_column] = part
    pieces = []
    for side in range(2):
        for k in orders[side]:
            part = pick(which, span * dp_count + (column ^ k))
            block = lax.dynamic_index_in_dim(qkv_low, part, 0, keepdims=False)
            pieces.append(block[side * half_block : (side + 1) * half_block])
    qkv_block = cube_scatter(jnp.concatenate(pieces, axis=0), "dp").astype(BF16)
    returned = jnp.zeros(((per_shard + 1) * unit, width), BF16)
    for group in rounds:
        send, slot, pairs = [0] * devices, [per_shard] * devices, []
        for c, col, source, target, from_unit, to_unit in group:
            a = device_number(c, col, target, dp_count, seq_count)
            b = device_number(c, col, source, dp_count, seq_count)
            send[a], slot[b] = to_unit, from_unit
            pairs.append((a, b))
        piece = lax.dynamic_slice_in_dim(qkv_block, pick(send, number) * unit, unit, 0)
        piece = lax.ppermute(piece, ALL, pairs)
        returned = lax.dynamic_update_slice_in_dim(returned, piece, pick(slot, number) * unit, 0)
    returned = returned[: per_shard * unit]
    grad_qkv = returned.astype(F32) + swap(returned).astype(F32)

    gate_terms = joined("gate") * gate_here * (1.0 - gate_here)
    gate_row = lax.dynamic_update_slice_in_dim(
        jnp.zeros((head_count,), F32), gate_terms, span * heads_here, 0
    )
    small = jnp.concatenate([joined("gains_one"), joined("gains_two"), gate_row])
    small = jnp.pad(small, (0, 8 * width - small.shape[0])).reshape(8, width)
    small = lax.all_gather(after(small, up_mine), ALL, axis=0, tiled=True)
    small = jnp.sum(small.reshape(devices, 8 * width)[:, : 3 * width], axis=0)
    gain_at = (column * seq_count + place) * shard_gain
    grad_gains = lax.dynamic_slice_in_dim(
        small[: 2 * width].reshape(2, width), gain_at, shard_gain, 1
    )
    grad_gate = small[2 * width : 2 * width + head_count]
    return (
        jnp.stack(outputs)[:, None],
        jnp.stack(new_memories)[:, None],
        jnp.stack(new_norms)[:, None],
        jnp.stack(grad_tokens)[:, None],
        grad_qkv,
        grad_out,
        grad_gains,
        grad_gate,
        grad_inner,
        grad_down,
    )


def solution(mesh):
    placed = (
        P(None, "dp", ("rep", "seq"), None),
        P(None, "dp"),
        P(None, "dp", None, None, None),
        P(None, "dp", None, None),
        P(("dp", "seq"), None),
        P(("dp", "seq"), None),
        P(None, ("dp", "seq")),
        P(),
        P(("dp", "seq"), None),
        P(("dp", "seq"), None),
        P(None, "dp", ("rep", "seq"), None),
    )
    return jax.shard_map(
        shards,
        mesh=mesh,
        in_specs=placed,
        out_specs=(
            P(None, "dp", ("rep", "seq"), None),
            P(None, "dp", ("rep", "seq"), None, None),
            P(None, "dp", ("rep", "seq"), None),
            P(None, "dp", ("rep", "seq"), None),
            P(("dp", "seq"), None),
            P(("dp", "seq"), None),
            P(None, ("dp", "seq")),
            P(),
            P(("dp", "seq"), None),
            P(("dp", "seq"), None),
        ),
        check_vma=False,
    )
```

```python
import functools
import math

import jax
import jax.numpy as jnp
from jax import lax
from jax.experimental import pallas as pl
from jax.experimental.pallas import tpu as pltpu
from jax.sharding import PartitionSpec as P

EPSILON = 1e-05
LOG2E = 1.4426950408889634
NEG = -1e30
F32 = jnp.float32
BF16 = jnp.bfloat16
ALL = ("rep", "dp", "seq")


def nt(left_side, right_side):
    return lax.dot_general(
        left_side, right_side, (((1,), (1,)), ((), ())), preferred_element_type=F32
    )


def nn(left_side, right_side):
    return lax.dot_general(
        left_side, right_side, (((1,), (0,)), ((), ())), preferred_element_type=F32
    )


def tn(left_side, right_side):
    return lax.dot_general(
        left_side, right_side, (((0,), (0,)), ((), ())), preferred_element_type=F32
    )


def elu_one(values):
    return jnp.where(values > 0.0, values + 1.0, jnp.exp(jnp.minimum(values, 0.0)))


def project_kernel(rows_ref, gain_ref, weight_ref, hidden_ref, projected_ref):
    rows = rows_ref[...].astype(F32)
    scale = lax.rsqrt(jnp.mean(rows * rows, axis=-1, keepdims=True) + EPSILON)
    hidden = (rows * scale * gain_ref[...]).astype(BF16)
    hidden_ref[...] = hidden
    projected_ref[...] = nt(hidden, weight_ref[...]).astype(BF16)


def project(rows, gain, weight):
    count, width = rows.shape
    outs = weight.shape[0]
    block = min(256, count)
    return pl.pallas_call(
        project_kernel,
        grid=(count // block,),
        in_specs=[
            pl.BlockSpec((block, width), lambda i: (i, 0)),
            pl.BlockSpec((1, width), lambda i: (0, 0)),
            pl.BlockSpec((outs, width), lambda i: (0, 0)),
        ],
        out_specs=[
            pl.BlockSpec((block, width), lambda i: (i, 0)),
            pl.BlockSpec((block, outs), lambda i: (i, 0)),
        ],
        out_shape=[
            jax.ShapeDtypeStruct((count, width), BF16),
            jax.ShapeDtypeStruct((count, outs), BF16),
        ],
        compiler_params=pltpu.CompilerParams(vmem_limit_bytes=32 << 20),
        cost_estimate=pl.CostEstimate(
            flops=2 * count * width * outs,
            bytes_accessed=4 * count * width + 2 * outs * (width + count),
            transcendentals=count,
        ),
        name="project",
    )(rows, gain, weight)


def attend_kernel(
    block,
    length_ref,
    gate_ref,
    q_ref,
    k_ref,
    v_ref,
    mem_ref,
    norm_ref,
    mixed_ref,
    dot_ref,
    lse_ref,
    new_mem_ref,
    new_norm_ref,
    v_turned,
):
    head, step = pl.program_id(0), pl.program_id(1)
    length = length_ref[0]
    total, width = k_ref.shape
    memory = mem_ref[0]
    norm_row = norm_ref[0]
    memory_low = memory.astype(BF16)

    @pl.when(step == 0)
    def _():
        v_turned[...] = v_ref[...].T
        key_sig = elu_one(k_ref[...].astype(F32))
        below = jnp.sum(key_sig * norm_row, axis=-1, keepdims=True)
        recalled = nn(key_sig.astype(BF16), memory_low) / below
        change = v_ref[...].astype(F32) - recalled
        live = lax.broadcasted_iota(jnp.int32, (total, width), 0) < length
        kept = jnp.where(live, key_sig, 0.0)
        new_mem_ref[0] = memory + tn(kept.astype(BF16), change.astype(BF16))
        new_norm_ref[0] = norm_row + jnp.sum(kept, axis=0, keepdims=True)

    queries = q_ref[...]
    factor = LOG2E * width ** (-0.5)

    def visit(at, carry, masked):
        high, mass, acc = carry
        start = pl.multiple_of(at * block, block)
        scores = nt(k_ref[pl.ds(start, block), :], queries) * factor
        if masked:
            key_at = start + lax.broadcasted_iota(jnp.int32, (block, block), 0)
            query_at = step * block + lax.broadcasted_iota(jnp.int32, (block, block), 1)
            scores = jnp.where((key_at <= query_at) & (key_at < length), scores, NEG)
        higher = jnp.maximum(high, jnp.max(scores, axis=0, keepdims=True))
        weights = jnp.exp2(scores - higher)
        shrink = jnp.exp2(high - higher)
        mass = mass * shrink + jnp.sum(weights, axis=0, keepdims=True)
        acc = acc * shrink + nn(v_turned[:, pl.ds(start, block)], weights.astype(BF16))
        return higher, mass, acc

    full = jnp.minimum(step, length // block)
    end = jnp.minimum(step + 1, (length + block - 1) // block)
    carry = (
        jnp.full((1, block), NEG, F32),
        jnp.zeros((1, block), F32),
        jnp.zeros((width, block), F32),
    )
    carry = lax.fori_loop(0, full, functools.partial(visit, masked=False), carry)
    high, mass, acc = lax.fori_loop(full, end, functools.partial(visit, masked=True), carry)
    dot_read = (acc / mass).T
    query_sig = elu_one(queries.astype(F32))
    below = jnp.sum(query_sig * norm_row, axis=-1, keepdims=True)
    mem_read = nn(query_sig.astype(BF16), memory_low) / below
    gate = gate_ref[head]
    mixed_ref[...] = (gate * mem_read + (1.0 - gate) * dot_read).astype(BF16)
    dot_ref[...] = dot_read
    lse_ref[0] = high + jnp.log2(mass)


def attend(length, gate, projected, memory, normalizer):
    total = projected.shape[0]
    heads, width = normalizer.shape[0], normalizer.shape[2]
    block = min(512, total)
    smem = pl.BlockSpec(memory_space=pltpu.SMEM)
    return pl.pallas_call(
        functools.partial(attend_kernel, block),
        grid=(heads, total // block),
        in_specs=[
            smem,
            smem,
            pl.BlockSpec((block, width), lambda h, i: (i, h)),
            pl.BlockSpec((total, width), lambda h, i: (0, heads + h)),
            pl.BlockSpec((total, width), lambda h, i: (0, 2 * heads + h)),
            pl.BlockSpec((1, width, width), lambda h, i: (h, 0, 0)),
            pl.BlockSpec((1, 1, width), lambda h, i: (h, 0, 0)),
        ],
        out_specs=[
            pl.BlockSpec((block, width), lambda h, i: (i, h)),
            pl.BlockSpec((block, width), lambda h, i: (i, h)),
            pl.BlockSpec((1, 1, block), lambda h, i: (h, 0, i)),
            pl.BlockSpec((1, width, width), lambda h, i: (h, 0, 0)),
            pl.BlockSpec((1, 1, width), lambda h, i: (h, 0, 0)),
        ],
        out_shape=[
            jax.ShapeDtypeStruct((total, heads * width), BF16),
            jax.ShapeDtypeStruct((total, heads * width), F32),
            jax.ShapeDtypeStruct((heads, 1, total), F32),
            jax.ShapeDtypeStruct((heads, width, width), F32),
            jax.ShapeDtypeStruct((heads, 1, width), F32),
        ],
        scratch_shapes=[pltpu.VMEM((width, total), BF16)],
        compiler_params=pltpu.CompilerParams(vmem_limit_bytes=40 << 20),
        cost_estimate=pl.CostEstimate(
            flops=4 * heads * total * total * width,
            bytes_accessed=heads * total * width * 12,
            transcendentals=heads * total * total,
        ),
        name="attend",
    )(length, gate, projected, projected, projected, memory, normalizer)


def attend_back_kernel(
    block,
    length_ref,
    gate_ref,
    q_ref,
    k_ref,
    v_ref,
    mem_ref,
    norm_ref,
    dot_ref,
    lse_ref,
    grad_ref,
    out_ref,
    gate_sum_ref,
    k_turned,
    k_sum,
    v_sum,
):
    head, step = pl.program_id(0), pl.program_id(1)
    heads, steps = pl.num_programs(0), pl.num_programs(1)
    length = length_ref[0]
    total, width = k_ref.shape
    gate = gate_ref[head]

    @pl.when(step == 0)
    def _():
        k_turned[...] = k_ref[...].T
        k_sum[...] = jnp.zeros_like(k_sum)
        v_sum[...] = jnp.zeros_like(v_sum)
        gate_sum_ref[...] = jnp.zeros_like(gate_sum_ref)

    queries = q_ref[...]
    query_float = queries.astype(F32)
    grad_mixed = grad_ref[...].astype(F32)
    grad_dot = ((1.0 - gate) * grad_mixed).astype(BF16)
    dot_read = dot_ref[...]
    offset = jnp.sum((grad_dot.astype(F32) * dot_read).T, axis=0, keepdims=True)
    lse = lse_ref[0]
    scale = width ** (-0.5)
    factor = LOG2E * scale

    def visit(at, acc, masked):
        start = pl.multiple_of(at * block, block)
        here = pl.ds(start, block)
        scores = nt(k_ref[here, :], queries) * factor
        weights = jnp.exp2(scores - lse)
        if masked:
            key_at = start + lax.broadcasted_iota(jnp.int32, (block, block), 0)
            query_at = step * block + lax.broadcasted_iota(jnp.int32, (block, block), 1)
            weights = jnp.where((key_at <= query_at) & (key_at < length), weights, 0.0)
        grad_probs = nt(v_ref[here, :], grad_dot)
        grad_scores = (weights * (grad_probs - offset) * scale).astype(BF16)
        v_sum[here, :] += nn(weights.astype(BF16), grad_dot)
        k_sum[here, :] += nn(grad_scores, queries)
        return acc + nn(k_turned[:, here], grad_scores)

    full = jnp.minimum(step, length // block)
    end = jnp.minimum(step + 1, (length + block - 1) // block)
    acc = jnp.zeros((width, block), F32)
    acc = lax.fori_loop(0, full, functools.partial(visit, masked=False), acc)
    acc = lax.fori_loop(full, end, functools.partial(visit, masked=True), acc)

    memory_low = mem_ref[0].astype(BF16)
    norm_row = norm_ref[0]
    query_sig = elu_one(query_float)
    below = jnp.sum(query_sig * norm_row, axis=-1, keepdims=True)
    numerator = nn(query_sig.astype(BF16), memory_low)
    inverse = 1.0 / below
    grad_read = gate * grad_mixed
    grad_below = -jnp.sum(grad_read * numerator, axis=-1, keepdims=True) * inverse * inverse
    grad_sig = nt((grad_read * inverse).astype(BF16), memory_low) + grad_below * norm_row
    slope = jnp.where(query_float > 0.0, 1.0, jnp.exp(jnp.minimum(query_float, 0.0)))
    rows = pl.ds(pl.multiple_of(step * block, block), block)
    out_ref[rows, pl.ds(pl.multiple_of(head * width, width), width)] = (
        acc.T + grad_sig * slope
    ).astype(BF16)
    gate_sum_ref[0] += jnp.sum(
        grad_mixed * (numerator * inverse - dot_read), axis=0, keepdims=True
    )

    @pl.when(step == steps - 1)
    def _():
        k_at = pl.multiple_of((heads + head) * width, width)
        v_at = pl.multiple_of((2 * heads + head) * width, width)
        out_ref[:, pl.ds(k_at, width)] = k_sum[...].astype(BF16)
        out_ref[:, pl.ds(v_at, width)] = v_sum[...].astype(BF16)


def attend_back(length, gate, projected, memory, normalizer, dot_read, lse, grad_mixed):
    total = projected.shape[0]
    heads, width = normalizer.shape[0], normalizer.shape[2]
    block = min(512, total)
    smem = pl.BlockSpec(memory_space=pltpu.SMEM)
    return pl.pallas_call(
        functools.partial(attend_back_kernel, block),
        grid=(heads, total // block),
        in_specs=[
            smem,
            smem,
            pl.BlockSpec((block, width), lambda h, i: (i, h)),
            pl.BlockSpec((total, width), lambda h, i: (0, heads + h)),
            pl.BlockSpec((total, width), lambda h, i: (0, 2 * heads + h)),
            pl.BlockSpec((1, width, width), lambda h, i: (h, 0, 0)),
            pl.BlockSpec((1, 1, width), lambda h, i: (h, 0, 0)),
            pl.BlockSpec((block, width), lambda h, i: (i, h)),
            pl.BlockSpec((1, 1, block), lambda h, i: (h, 0, i)),
            pl.BlockSpec((block, width), lambda h, i: (i, h)),
        ],
        out_specs=[
            pl.BlockSpec((total, 3 * heads * width), lambda h, i: (0, 0)),
            pl.BlockSpec((1, 1, width), lambda h, i: (h, 0, 0)),
        ],
        out_shape=[
            jax.ShapeDtypeStruct((total, 3 * heads * width), BF16),
            jax.ShapeDtypeStruct((heads, 1, width), F32),
        ],
        scratch_shapes=[
            pltpu.VMEM((width, total), BF16),
            pltpu.VMEM((total, width), F32),
            pltpu.VMEM((total, width), F32),
        ],
        compiler_params=pltpu.CompilerParams(vmem_limit_bytes=40 << 20),
        cost_estimate=pl.CostEstimate(
            flops=10 * heads * total * total * width,
            bytes_accessed=heads * total * width * 20,
            transcendentals=heads * total * total,
        ),
        name="attend_back",
    )(length, gate, projected, projected, projected, memory, normalizer, dot_read, lse, grad_mixed)


def unit_kernel(
    rows_ref, grad_ref, inner_ref, down_ref, hidden_ref, grad_gate_ref, grad_up_ref
):
    width = rows_ref.shape[1]
    rows = rows_ref[...]
    gates = nt(rows, inner_ref[:, :width])
    ups = nt(rows, inner_ref[:, width:])
    grad_hidden = nt(grad_ref[...], down_ref[...])
    sigmoid = 1.0 / (1.0 + jnp.exp(-gates))
    silu = gates * sigmoid
    hidden_ref[...] = (silu * ups).astype(BF16)
    grad_gate_ref[...] = (
        grad_hidden * ups * (sigmoid * (1.0 + gates * (1.0 - sigmoid)))
    ).astype(BF16)
    grad_up_ref[...] = (grad_hidden * silu).astype(BF16)


def unit_pass(rows, grads, inner, down):
    count, width = rows.shape
    units = inner.shape[0]
    tile = min(256, units)
    resident = pl.BlockSpec((count, width), lambda t: (0, 0), pipeline_mode=pl.Buffered(1))
    column = pl.BlockSpec((count, tile), lambda t: (0, t))
    unit_shape = jax.ShapeDtypeStruct((count, units), BF16)
    return pl.pallas_call(
        unit_kernel,
        grid=(units // tile,),
        in_specs=[
            resident,
            resident,
            pl.BlockSpec((tile, 2 * width), lambda t: (t, 0)),
            pl.BlockSpec((tile, width), lambda t: (t, 0)),
        ],
        out_specs=[column] * 3,
        out_shape=[unit_shape] * 3,
        compiler_params=pltpu.CompilerParams(vmem_limit_bytes=56 << 20),
        cost_estimate=pl.CostEstimate(
            flops=2 * 3 * count * width * units,
            bytes_accessed=units * (6 * width + 6 * count) + 4 * count * width,
            transcendentals=count * units,
        ),
        name="unit_pass",
    )(rows, grads, inner, down)


def row_kernel(starts_ref, *refs):
    hidden, gates, ups, gate_w, up_w, down_w = (refs[2 * i : 2 * i + 2] for i in range(6))
    out_ref, grad_two_ref = refs[12:]
    grad_two_ref[...] = (
        nn(gates[0][...], gate_w[0][...])
        + nn(gates[1][...], gate_w[1][...])
        + nn(ups[0][...], up_w[0][...])
        + nn(ups[1][...], up_w[1][...])
    ).astype(BF16)
    out = (
        nn(hidden[0][...], down_w[0][...]) + nn(hidden[1][...], down_w[1][...])
    ).astype(BF16)
    pieces = starts_ref.shape[0]
    size = out.shape[0] // pieces
    for i in range(pieces):
        start = pl.multiple_of(starts_ref[i], size)
        out_ref[pl.ds(start, size), :] = out[i * size : (i + 1) * size]


def row_pass(starts, hidden, grad_gates, grad_ups, inner, down):
    count, units = hidden[0].shape
    width = down[0].shape[1]
    tile = min(256, width)
    tiles = width // tile
    resident = pl.BlockSpec((count, units), lambda t: (0, 0), pipeline_mode=pl.Buffered(1))
    low = pl.BlockSpec((units, tile), lambda t: (0, t))
    high = pl.BlockSpec((units, tile), lambda t: (0, tiles + t))
    column = pl.BlockSpec((count, tile), lambda t: (0, t))
    row_shape = jax.ShapeDtypeStruct((count, width), BF16)
    return pl.pallas_call(
        row_kernel,
        grid=(tiles,),
        in_specs=[pl.BlockSpec(memory_space=pltpu.SMEM)]
        + [resident] * 6
        + [low, low, high, high, low, low],
        out_specs=[column] * 2,
        out_shape=[row_shape] * 2,
        compiler_params=pltpu.CompilerParams(vmem_limit_bytes=56 << 20),
        cost_estimate=pl.CostEstimate(
            flops=2 * 3 * count * width * 2 * units,
            bytes_accessed=12 * units * (width + count) + 4 * count * width,
            transcendentals=0,
        ),
        name="row_pass",
    )(starts, *hidden, *grad_gates, *grad_ups, *inner, *inner, *down)


def weight_kernel(pairs, *refs):
    out_ref = refs[-1]
    total = tn(refs[0][...], refs[1][...])
    for at in range(1, pairs):
        total += tn(refs[2 * at][...], refs[2 * at + 1][...])
    if len(refs) > 2 * pairs + 1:
        total += refs[2 * pairs][...].astype(F32)
    out_ref[...] = total.astype(BF16)


def weight_pass(pairs, extra=None):
    size, width = pairs[0][0].shape[1], pairs[0][1].shape[1]
    tile = min(256, size)
    in_specs, operands, flops, moved = [], [], 0, 2 * size * width
    for left, right in pairs:
        count = left.shape[0]
        in_specs.append(pl.BlockSpec((count, tile), lambda t: (0, t)))
        in_specs.append(
            pl.BlockSpec((count, width), lambda t: (0, 0), pipeline_mode=pl.Buffered(1))
        )
        operands += [left, right]
        flops += 2 * count * size * width
        moved += 2 * count * (size + width)
    if extra is not None:
        in_specs.append(pl.BlockSpec((tile, width), lambda t: (t, 0)))
        operands.append(extra)
        moved += 2 * size * width
    return pl.pallas_call(
        functools.partial(weight_kernel, len(pairs)),
        grid=(size // tile,),
        in_specs=in_specs,
        out_specs=pl.BlockSpec((tile, width), lambda t: (t, 0)),
        out_shape=jax.ShapeDtypeStruct((size, width), BF16),
        compiler_params=pltpu.CompilerParams(vmem_limit_bytes=56 << 20),
        cost_estimate=pl.CostEstimate(flops=flops, bytes_accessed=moved, transcendentals=0),
        name="weight_pass",
    )(*operands)


def back_kernel(half_ref, grad_ref, weight_ref, rows_ref, *refs):
    out_ref, gain_ref = refs[-2:]

    @pl.when(pl.program_id(0) == 0)
    def _():
        gain_ref[...] = jnp.zeros_like(gain_ref)

    part = nn(grad_ref[...], weight_ref[...])
    total = part + refs[0][...].astype(F32) if len(refs) > 2 else part
    out_ref[...] = total.astype(BF16)
    rows = rows_ref[...].astype(F32)
    scale = lax.rsqrt(jnp.mean(rows * rows, axis=-1, keepdims=True) + EPSILON)
    gain_ref[...] += jnp.sum(part * (rows * scale), axis=0, keepdims=True)


def project_back(half, grads, weight, rows, extra=None):
    count, outs = grads.shape[0] // 2, grads.shape[1]
    width = weight.shape[1]
    block = min(256, count)
    steps = count // block
    return pl.pallas_call(
        back_kernel,
        grid_spec=pltpu.PrefetchScalarGridSpec(
            num_scalar_prefetch=1,
            grid=(steps,),
            in_specs=[
                pl.BlockSpec((block, outs), lambda i, at: (at[0] * steps + i, 0)),
                pl.BlockSpec((outs, width), lambda i, at: (0, 0)),
                pl.BlockSpec((block, width), lambda i, at: (at[0] * steps + i, 0)),
            ]
            + [pl.BlockSpec((block, width), lambda i, at: (i, 0))] * (extra is not None),
            out_specs=[
                pl.BlockSpec((block, width), lambda i, at: (i, 0)),
                pl.BlockSpec((1, width), lambda i, at: (0, 0)),
            ],
        ),
        out_shape=[
            jax.ShapeDtypeStruct((count, width), BF16),
            jax.ShapeDtypeStruct((1, width), F32),
        ],
        compiler_params=pltpu.CompilerParams(vmem_limit_bytes=40 << 20),
        cost_estimate=pl.CostEstimate(
            flops=2 * count * width * outs,
            bytes_accessed=4 * count * width + 2 * outs * (width + count),
            transcendentals=count,
        ),
        name="project_back",
    )(
        jnp.reshape(half, (1,)).astype(jnp.int32),
        grads,
        weight,
        rows,
        *([] if extra is None else [extra]),
    )


def swap(values):
    return lax.ppermute(values, "rep", [(0, 1), (1, 0)])


def after(values, *earlier):
    earlier = [e for e in earlier if e is not None]
    return lax.optimization_barrier((values, *earlier))[0] if earlier else values


def add_low(left_side, right_side):
    return (left_side.astype(F32) + right_side.astype(F32)).astype(BF16)


def line_gather(values, axis):
    count = lax.axis_size(axis)
    here = lax.axis_index(axis)
    rows = values.shape[0]
    table = jnp.zeros(((3 * count - 2) * rows,) + values.shape[1:], values.dtype)

    def put(table, piece, origin):
        return lax.dynamic_update_slice_in_dim(table, piece, (origin + count - 1) * rows, 0)

    table = put(table, values, here)
    rising = falling = values
    for hop in range(1, count):
        rising = lax.ppermute(
            rising, axis, [(a, a + 1) for a in range(count - 1) if a >= hop - 1]
        )
        falling = lax.ppermute(
            falling, axis, [(a, a - 1) for a in range(1, count) if a + hop - 1 < count]
        )
        table = put(table, rising, here - hop)
        table = put(table, falling, here + hop)
    return table[(count - 1) * rows : (2 * count - 1) * rows]


def line_scatter(values, axis, pins=()):
    count = lax.axis_size(axis)
    here = lax.axis_index(axis)
    rows = values.shape[0] // count

    def block(owner):
        start = jnp.clip(owner, 0, count - 1) * rows
        return lax.dynamic_slice_in_dim(values, start, rows, 0).astype(F32)

    rising = falling = None
    for hop in range(1, count):
        reach = count - hop
        up, down = block(here + reach), block(here - reach)
        if rising is not None:
            up, down = up + rising.astype(F32), down + falling.astype(F32)
        rising = lax.ppermute(
            up.astype(BF16), axis, [(a, a + 1) for a in range(count) if a + reach < count]
        )
        falling = lax.ppermute(
            down.astype(BF16), axis, [(a, a - 1) for a in range(count) if a - reach >= 0]
        )
        if hop <= len(pins):
            rising, falling = after(rising, pins[hop - 1]), after(falling, pins[hop - 1])
    return block(here) + rising.astype(F32) + falling.astype(F32)


def cube_bits(count):
    bits = [1 << b for b in range(count.bit_length() - 1)]
    return bits, bits[::-1]


def cube_order(bits):
    order = [0]
    for bit in reversed(bits):
        order = order + [k | bit for k in order]
    return order


def cube_gather(values, axis):
    count = lax.axis_size(axis)
    half = values.shape[0] // 2
    parts = []
    for bits, start in zip(cube_bits(count), (0, half)):
        held = {0: values[start : start + half]}
        for bit in bits:
            pairs = [(a, a ^ bit) for a in range(count)]
            held.update({k ^ bit: lax.ppermute(v, axis, pairs) for k, v in list(held.items())})
        parts += [held[k] for k in cube_order(bits)]
    return jnp.concatenate(parts, axis=0)


def cube_scatter(values, axis, pins=()):
    count = lax.axis_size(axis)
    half = values.shape[0] // 2
    parts = []
    for bits, start in zip(cube_bits(count), (0, half)):
        held = values[start : start + half]
        for at, bit in enumerate(bits):
            pairs = [(a, a ^ bit) for a in range(count)]
            keep = held.shape[0] // 2
            got = lax.ppermute(held[keep:].astype(BF16), axis, pairs)
            if at < len(pins):
                got = after(got, pins[at])
            held = held[:keep].astype(F32) + got.astype(F32)
        parts.append(held)
    return jnp.concatenate(parts, axis=0)


def remote(source, target, sent, landed, device):
    return pltpu.make_async_remote_copy(
        src_ref=source,
        dst_ref=target,
        send_sem=sent,
        recv_sem=landed,
        device_id=device,
        device_id_type=pl.DeviceIdType.MESH,
    )


def greet(devices):
    barrier = pltpu.get_barrier_semaphore()
    for device in devices:
        pl.semaphore_signal(barrier, inc=1, device_id=device, device_id_type=pl.DeviceIdType.MESH)
    pl.semaphore_wait(barrier, len(devices))


def heads_kernel(
    sizes,
    qkv_ref,
    gain_ref,
    head_ref,
    gains_ref,
    landed,
    unit_sent,
    unit_here,
    block_sent,
    block_here,
    line_sent,
    line_here,
    cube_sent,
    cube_here,
    local,
):
    dp_count, seq_count, unit, per_shard, per_block, per_column = sizes
    span_count = 2 * seq_count
    block_rows = unit * per_block
    core, column, place = lax.axis_index("rep"), lax.axis_index("dp"), lax.axis_index("seq")
    span, shard = core * seq_count + place, column * seq_count + place
    line = [(core, column, (place + k) % seq_count) for k in range(1, seq_count)]
    cube = [(core, (column + k) % dp_count, place) for k in range(1, dp_count)]
    greet(line + cube)

    gains = []
    for k, device in enumerate(line):
        gains.append(
            remote(gain_ref, gains_ref.at[shard], line_sent.at[k], line_here.at[k], device)
        )
    for copy in gains:
        copy.start()
    own_gain = pltpu.make_async_copy(gain_ref, gains_ref.at[shard], local.at[0])
    own_gain.start()

    def rows(ref, at, size):
        return ref.at[pl.ds(pl.multiple_of(at * size, size), size)]

    def unit_copy(i):
        number = shard * per_shard + i
        owner = (number // per_block) % span_count
        source, target = rows(qkv_ref, i, unit), rows(landed, number % per_block, unit)
        far = remote(
            source,
            target,
            unit_sent.at[i],
            unit_here.at[number % per_block],
            (core, column, owner % seq_count),
        )
        near = pltpu.make_async_copy(source, target, local.at[1 + i])
        mine = owner // seq_count == core
        stays = owner % seq_count == place
        return far, near, mine & jnp.logical_not(stays), mine & stays

    for i in range(per_shard):
        far, near, leaves, stays = unit_copy(i)
        pl.when(leaves)(far.start)
        pl.when(stays)(near.start)
    for i in range(per_shard):
        _, near, _, stays = unit_copy(i)
        pl.when(stays)(near.wait)

    def block_copies(part):
        target = rows(head_ref, part, block_rows)
        far = [
            remote(landed, target, block_sent.at[k], block_here.at[part], device)
            for k, device in enumerate(cube)
        ]
        return far, pltpu.make_async_copy(landed, target, local.at[0])

    own_gain.wait()
    for part in range(3):
        number = part * span_count + span

        @pl.when(number // per_column == column)
        def _():
            for j in range(per_block):
                source = ((number * per_block + j) // per_shard) % seq_count

                @pl.when(source != place)
                def _():
                    here = rows(landed, j, unit)
                    remote(here, here, unit_sent.at[0], unit_here.at[j], line[0]).wait_recv()

            far, near = block_copies(part)
            for copy in far:
                copy.start()
            near.start()

    for copy in gains:
        copy.wait()
    mine = gains_ref.at[pl.ds(column * seq_count, seq_count)]
    gains = [
        remote(mine, mine, cube_sent.at[k], cube_here.at[k], device)
        for k, device in enumerate(cube)
    ]
    for copy in gains:
        copy.start()
    for part in range(3):
        number = part * span_count + span
        far, near = block_copies(part)

        @pl.when(number // per_column == column)
        def _():
            near.wait()
            for copy in far:
                copy.wait_send()

        @pl.when(number // per_column != column)
        def _():
            far[0].wait_recv()

    for k, copy in enumerate(gains):
        copy.wait_send()
        origin = (column + dp_count - k - 1) % dp_count
        theirs = gains_ref.at[pl.ds(origin * seq_count, seq_count)]
        remote(theirs, theirs, cube_sent.at[k], cube_here.at[k], cube[k]).wait_recv()
    for i in range(per_shard):
        far, _, leaves, _ = unit_copy(i)
        pl.when(leaves)(far.wait_send)


def gather_heads(qkv_weight, gains, sizes):
    dp_count, seq_count, unit, per_shard, per_block, _ = sizes
    width = qkv_weight.shape[1]
    block_rows = unit * per_block
    anywhere = pl.BlockSpec(memory_space=pl.ANY)
    dma = pltpu.SemaphoreType.DMA
    return pl.pallas_call(
        functools.partial(heads_kernel, sizes),
        in_specs=[anywhere, anywhere],
        out_specs=[anywhere, anywhere],
        out_shape=[
            jax.ShapeDtypeStruct((3 * block_rows, width), BF16),
            jax.ShapeDtypeStruct((dp_count * seq_count, *gains.shape), F32),
        ],
        scratch_shapes=[
            pltpu.VMEM((block_rows, width), BF16),
            dma((per_shard,)),
            dma((per_block,)),
            dma((dp_count - 1,)),
            dma((3,)),
            dma((seq_count - 1,)),
            dma((seq_count - 1,)),
            dma((dp_count - 1,)),
            dma((dp_count - 1,)),
            dma((1 + per_shard,)),
        ],
        compiler_params=pltpu.CompilerParams(
            collective_id=0, has_side_effects=True, vmem_limit_bytes=16 << 20
        ),
        cost_estimate=pl.CostEstimate(
            flops=0, bytes_accessed=64 * block_rows * width, transcendentals=0
        ),
        name="gather_heads",
    )(qkv_weight, gains)


def flipped(value, bits):
    bit = 1
    while bit <= bits:
        if bits & bit:
            value = value + bit - 2 * bit * ((value // bit) % 2)
        bit *= 2
    return value


def cot_copies(cot_ref, cot_all, cube, sent, here, local, first):
    count = len(cube) + 1
    half = cot_ref.shape[0] // 2
    stays, leaves = [], []
    for side, bits in enumerate(cube_bits(count)):
        order = cube_order(bits)
        source = cot_ref.at[pl.ds(side * half, half)]
        for k in range(count):
            target = cot_all.at[pl.ds((side * count + order.index(k)) * half, half)]
            if k == 0:
                stays.append(pltpu.make_async_copy(source, target, local.at[first + side]))
            else:
                at = side * (count - 1) + k - 1
                leaves.append(remote(source, target, sent.at[at], here.at[at], cube[k - 1]))
    return stays, leaves


def cot_kernel(count, cot_ref, cot_all, sent, here, local):
    core, column, place = lax.axis_index("rep"), lax.axis_index("dp"), lax.axis_index("seq")
    cube = [(core, flipped(column, k), place) for k in range(1, count)]
    greet(cube)
    stays, leaves = cot_copies(cot_ref, cot_all, cube, sent, here, local, 0)
    for copy in stays + leaves:
        copy.start()
    for copy in stays + leaves:
        copy.wait()


def gather_cot(cot, count):
    rows, width = cot.shape
    anywhere = pl.BlockSpec(memory_space=pl.ANY)
    dma = pltpu.SemaphoreType.DMA
    return pl.pallas_call(
        functools.partial(cot_kernel, count),
        in_specs=[anywhere],
        out_specs=anywhere,
        out_shape=jax.ShapeDtypeStruct((count * rows, width), BF16),
        scratch_shapes=[dma((2 * (count - 1),)), dma((2 * (count - 1),)), dma((2,))],
        compiler_params=pltpu.CompilerParams(collective_id=3, has_side_effects=True),
        cost_estimate=pl.CostEstimate(
            flops=0, bytes_accessed=8 * rows * width, transcendentals=0
        ),
        name="gather_cot",
    )(cot)


def rest_kernel(sizes, *refs):
    dp_count, seq_count = sizes
    out_ref, cot_ref, out_all, cot_all = refs[:4]
    line_sent, line_here, cube_sent, cube_here, cot_sent, cot_here, local = refs[4:]
    core, column, place = lax.axis_index("rep"), lax.axis_index("dp"), lax.axis_index("seq")
    line = [(core, column, (place + k) % seq_count) for k in range(1, seq_count)]
    cube = [(core, flipped(column, k), place) for k in range(1, dp_count)]
    greet(line + cube)
    shard_rows = out_ref.shape[0]
    column_rows = seq_count * shard_rows
    def out_rows(start, size):
        return out_all.at[pl.ds(pl.multiple_of(start, shard_rows), size)]

    mine = out_rows((column * seq_count + place) * shard_rows, shard_rows)
    lines = [
        remote(out_ref, mine, line_sent.at[k], line_here.at[k], device)
        for k, device in enumerate(line)
    ]
    own_out = pltpu.make_async_copy(out_ref, mine, local.at[0])

    own_cots, cots = cot_copies(cot_ref, cot_all, cube, cot_sent, cot_here, local, 1)
    for copy in lines + [own_out] + own_cots + cots:
        copy.start()
    own_out.wait()
    for copy in lines:
        copy.wait()
    mine = out_rows(column * column_rows, column_rows)
    cubes = [
        remote(mine, mine, cube_sent.at[k], cube_here.at[k], device)
        for k, device in enumerate(cube)
    ]
    for copy in cubes:
        copy.start()
    for copy in own_cots + cots:
        copy.wait()
    for k, copy in enumerate(cubes):
        copy.wait_send()
        theirs = out_rows(cube[k][1] * column_rows, column_rows)
        remote(theirs, theirs, cube_sent.at[k], cube_here.at[k], cube[k]).wait_recv()


def gather_rest(out_half, cot, sizes):
    dp_count, seq_count = sizes
    rows, width = cot.shape
    anywhere = pl.BlockSpec(memory_space=pl.ANY)
    dma = pltpu.SemaphoreType.DMA
    return pl.pallas_call(
        functools.partial(rest_kernel, sizes),
        in_specs=[anywhere] * 2,
        out_specs=[anywhere] * 2,
        out_shape=[
            jax.ShapeDtypeStruct(
                (dp_count * seq_count * out_half.shape[0], out_half.shape[1]), BF16
            ),
            jax.ShapeDtypeStruct((dp_count * rows, width), BF16),
        ],
        scratch_shapes=[
            dma((seq_count - 1,)),
            dma((seq_count - 1,)),
            dma((dp_count - 1,)),
            dma((dp_count - 1,)),
            dma((2 * (dp_count - 1),)),
            dma((2 * (dp_count - 1),)),
            dma((3,)),
        ],
        compiler_params=pltpu.CompilerParams(collective_id=2, has_side_effects=True),
        cost_estimate=pl.CostEstimate(
            flops=0, bytes_accessed=8 * rows * width, transcendentals=0
        ),
        name="gather_rest",
    )(out_half, cot)


def add_rows(out_ref, refs, size):
    def some(i, _):
        rows = pl.ds(pl.multiple_of(i * size, size), size)
        total = refs[0][rows, :].astype(F32)
        for ref in refs[1:]:
            total += ref[rows, :].astype(F32)
        out_ref[rows, :] = total.astype(out_ref.dtype)
        return 0

    lax.fori_loop(0, out_ref.shape[0] // size, some, 0)


def spread_kernel(
    sizes,
    micros,
    *refs,
):
    spread_body(sizes, refs[:micros], *refs[micros:])


def spread_body(
    sizes,
    line_refs,
    qkv_ref,
    out_ref,
    grad_ref,
    qkv_done,
    out_done,
    rising,
    falling,
    qkv_in,
    qkv_sum,
    out_in,
    out_part,
    out_line,
    rise_sent,
    rise_here,
    fall_sent,
    fall_here,
    qkv_sent,
    qkv_here,
    out_sent,
    out_here,
    unit_sent,
    unit_here,
    line_sent,
    line_here,
    swap_sent,
    swap_here,
    local,
):
    dp_count, seq_count, unit, per_shard, per_block, per_column = sizes
    span_count = 2 * seq_count
    micros = len(line_refs)
    core, column, place = lax.axis_index("rep"), lax.axis_index("dp"), lax.axis_index("seq")
    span = core * seq_count + place
    cube = [(core, (column + k) % dp_count, place) for k in range(1, dp_count)]
    line = [(core, column, (place + k) % seq_count) for k in range(1, seq_count)]
    across = [(1 - core, column, (place + k) % seq_count) for k in range(seq_count)]
    greet(cube + line + across)

    def part_at(part, col):
        return (part * span_count + span) // per_column == col

    def out_copy(k):
        target = cube[k]
        return remote(
            out_ref.at[target[1]], out_in.at[k], out_sent.at[k], out_here.at[k], target
        )

    def qkv_copy(k, part):
        return remote(
            qkv_ref.at[part], qkv_in.at[k], qkv_sent.at[k], qkv_here.at[k], cube[k]
        )

    def hop(number, m, up):
        reach = seq_count - number
        buffer, sent, here = (
            (rising, rise_sent, rise_here) if up else (falling, fall_sent, fall_here)
        )
        behind = place if up else seq_count - 1 - place
        owner = place + reach if up else place - reach
        owner = jnp.clip(owner, 0, seq_count - 1)
        next_place = jnp.clip(place + 1 if up else place - 1, 0, seq_count - 1)
        device = (core, column, next_place)
        at = (number - 1) * micros + m
        target = buffer.at[at]

        def send(source):
            remote(source, target, sent.at[at], here.at[at], device).start()

        own = line_refs[m].at[owner]
        if number == 1:
            pl.when(behind == 0)(lambda: send(own))
            return

        @pl.when(behind == 0)
        def _():
            send(own)

        @pl.when((behind >= 1) & (behind <= number - 1))
        def _():
            before = buffer.at[at - micros]
            remote(before, before, sent.at[0], here.at[at - micros], across[0]).wait_recv()
            add_rows(before, [before, own], 64)
            send(before)

    def hop_sent(number, m, up):
        sent = rise_sent if up else fall_sent
        buffer = rising if up else falling
        behind = place if up else seq_count - 1 - place
        at = (number - 1) * micros + m
        piece = buffer.at[at]

        @pl.when(behind <= number - 1)
        def _():
            remote(piece, piece, sent.at[at], sent.at[at], across[0]).wait_send()

    def hops(number):
        for m in range(micros):
            hop(number, m, True)
            hop(number, m, False)

    hops(1)
    for k in range(dp_count - 1):
        out_copy(k).start()
        for part in range(3):

            @pl.when(part_at(part, cube[k][1]))
            def _():
                qkv_copy(k, part).start()

    hops(2)

    for k in range(dp_count - 1):
        out_copy(k).wait_recv()
    for s in range(seq_count):
        add_rows(
            out_part.at[s],
            [out_ref.at[column, s]] + [out_in.at[k, s] for k in range(dp_count - 1)],
            32,
        )

    def line_copy(k):
        return remote(
            out_part.at[line[k][2]], out_line.at[k], line_sent.at[k], line_here.at[k], line[k]
        )

    for k in range(seq_count - 1):
        line_copy(k).start()

    def unit_copies(part, j):
        number = (part * span_count + span) * per_block + j
        owner = (number // per_shard) % seq_count
        source = qkv_sum.at[pl.ds(j * unit, unit)]
        target = qkv_done.at[pl.ds(pl.multiple_of((number % per_shard) * unit, unit), unit)]
        here = unit_here.at[number % per_shard]
        other = remote(
            source, target, unit_sent.at[2 * j], here, (1 - core, column, owner)
        )
        same = remote(source, target, unit_sent.at[2 * j + 1], here, (core, column, owner))
        stays = pltpu.make_async_copy(source, target, local.at[j])
        return owner, other, same, stays

    for part in range(3):

        @pl.when(part_at(part, column))
        def _():
            for k in range(dp_count - 1):
                qkv_copy(k, part).wait_recv()
            add_rows(
                qkv_sum, [qkv_ref.at[part]] + [qkv_in.at[k] for k in range(dp_count - 1)], 32
            )
            for j in range(per_block):
                owner, other, same, stays = unit_copies(part, j)
                other.start()
                pl.when(owner != place)(same.start)
                pl.when(owner == place)(stays.start)

    for number in range(3, seq_count):
        hops(number)

    for k in range(seq_count - 1):
        line_copy(k).wait_recv()
    add_rows(
        out_done.at[core],
        [out_part.at[place]] + [out_line.at[k] for k in range(seq_count - 1)],
        32,
    )
    mine = out_done.at[core]
    swapped = remote(mine, mine, swap_sent, swap_here, across[0])
    swapped.start()

    last = (seq_count - 2) * micros
    for m in range(micros):
        own = line_refs[m].at[place]
        up, down = rising.at[last + m], falling.at[last + m]

        @pl.when(place > 0)
        def _():
            remote(up, up, rise_sent.at[0], rise_here.at[last + m], across[0]).wait_recv()

        @pl.when(place < seq_count - 1)
        def _():
            remote(down, down, fall_sent.at[0], fall_here.at[last + m], across[0]).wait_recv()

        @pl.when(place == 0)
        def _():
            add_rows(grad_ref.at[m], [own, down], 64)

        @pl.when(place == seq_count - 1)
        def _():
            add_rows(grad_ref.at[m], [own, up], 64)

        @pl.when((place > 0) & (place < seq_count - 1))
        def _():
            add_rows(grad_ref.at[m], [own, up, down], 64)

    for number in range(1, seq_count):
        for m in range(micros):
            hop_sent(number, m, True)
            hop_sent(number, m, False)
    for k in range(dp_count - 1):
        out_copy(k).wait_send()
        for part in range(3):

            @pl.when(part_at(part, cube[k][1]))
            def _():
                qkv_copy(k, part).wait_send()

    for k in range(seq_count - 1):
        line_copy(k).wait_send()
    for part in range(3):

        @pl.when(part_at(part, column))
        def _():
            for j in range(per_block):
                owner, other, same, stays = unit_copies(part, j)
                other.wait_send()
                pl.when(owner != place)(same.wait_send)
                pl.when(owner == place)(stays.wait)

    for i in range(per_shard):
        number = (column * seq_count + place) * per_shard + i
        piece = qkv_done.at[pl.ds(i * unit, unit)]

        @pl.when((number // per_block) % span_count != span)
        def _():
            remote(piece, piece, unit_sent.at[0], unit_here.at[i], across[0]).wait_recv()

    swapped.wait_send()
    theirs = out_done.at[1 - core]
    remote(theirs, theirs, swap_sent, swap_here, across[0]).wait_recv()


def spread_sums(lines, qkv, out, sizes):
    dp_count, seq_count, unit, per_shard, per_block, _ = sizes
    micros = len(lines)
    _, rows, width = lines[0].shape
    shard_out, half_width = out.shape[2:]
    block_rows = unit * per_block
    hops = (seq_count - 1) * micros
    vmem = pl.BlockSpec(memory_space=pltpu.VMEM)
    dma = pltpu.SemaphoreType.DMA
    return pl.pallas_call(
        functools.partial(spread_kernel, sizes, micros),
        in_specs=[vmem] * (micros + 2),
        out_specs=[vmem] * 3,
        out_shape=[
            jax.ShapeDtypeStruct((micros, rows, width), F32),
            jax.ShapeDtypeStruct((per_shard * unit, width), BF16),
            jax.ShapeDtypeStruct((2, shard_out, half_width), BF16),
        ],
        scratch_shapes=[
            pltpu.VMEM((hops, rows, width), BF16),
            pltpu.VMEM((hops, rows, width), BF16),
            pltpu.VMEM((dp_count - 1, block_rows, width), BF16),
            pltpu.VMEM((block_rows, width), BF16),
            pltpu.VMEM((dp_count - 1, seq_count, shard_out, half_width), BF16),
            pltpu.VMEM((seq_count, shard_out, half_width), BF16),
            pltpu.VMEM((seq_count - 1, shard_out, half_width), BF16),
            dma((hops,)),
            dma((hops,)),
            dma((hops,)),
            dma((hops,)),
            dma((dp_count - 1,)),
            dma((dp_count - 1,)),
            dma((dp_count - 1,)),
            dma((dp_count - 1,)),
            dma((2 * per_block,)),
            dma((per_shard,)),
            dma((seq_count - 1,)),
            dma((seq_count - 1,)),
            dma,
            dma,
            dma((per_block,)),
        ],
        compiler_params=pltpu.CompilerParams(
            collective_id=1, has_side_effects=True, vmem_limit_bytes=56 << 20
        ),
        cost_estimate=pl.CostEstimate(
            flops=0, bytes_accessed=256 * rows * width, transcendentals=0
        ),
        name="spread_sums",
    )(*lines, qkv, out)


def pick(table, number):
    return jnp.asarray(table, jnp.int32)[number]


def shards(
    tokens,
    lengths,
    memory,
    normalizer,
    qkv_weight,
    out_weight,
    norm_gains,
    gate_logit,
    inner_weight,
    down_weight,
    cotangent,
):
    micros, _, span_rows, width = tokens.shape
    head_count = gate_logit.shape[0]
    head_dim = width // head_count
    dp_count, seq_count = lax.axis_size("dp"), lax.axis_size("seq")
    span_count = 2 * seq_count
    total = span_rows * span_count
    heads_here = head_count // span_count
    block_rows = heads_here * head_dim
    core, column, place = lax.axis_index("rep"), lax.axis_index("dp"), lax.axis_index("seq")
    span = core * seq_count + place
    inner_half = inner_weight.shape[0] // 2

    own_rows = [tokens[m, 0] for m in range(micros)]

    def gather_rows(rows):
        return lax.all_gather(rows, ("rep", "seq"), axis=0, tiled=True)

    all_rows = [gather_rows(own_rows[0])]

    unit = math.gcd(qkv_weight.shape[0], block_rows)
    per_shard, per_block = qkv_weight.shape[0] // unit, block_rows // unit
    per_column = 3 * span_count // dp_count
    devices = 2 * dp_count * seq_count
    shard_out, shard_gain = out_weight.shape[0], norm_gains.shape[1]
    lanes = -(-shard_gain // 128) * 128
    gain_tile = jnp.zeros((8, lanes), F32)
    gain_tile = lax.dynamic_update_slice(gain_tile, norm_gains.astype(F32), (0, 0))
    head_weight, gains_all = gather_heads(
        qkv_weight, gain_tile, (dp_count, seq_count, unit, per_shard, per_block, per_column)
    )
    gains_all = jnp.swapaxes(gains_all[:, :2, :shard_gain], 0, 1).reshape(2, width)
    gain_one, gain_two = gains_all[0:1], gains_all[1:2]
    half_width = width // 2
    positions = span * span_rows + jnp.arange(span_rows)
    lives = []
    for m in range(micros):
        live_rows = (positions < lengths[m, 0]).astype(F32)
        lives.append(cotangent[m, 0].astype(F32) * live_rows[:, None])
    for rows in own_rows[1:]:
        all_rows.append(gather_rows(after(rows, all_rows[-1], head_weight)))
    out_half = lax.dynamic_slice_in_dim(out_weight, core * half_width, half_width, 1)
    cots = [live.astype(BF16) for live in lives]
    out_near, cot_all = gather_rest(
        after(out_half, head_weight, all_rows[0]), cots[0], (dp_count, seq_count)
    )
    grads_all = [cot_all]
    for cot in cots[1:]:
        grads_all.append(gather_cot(after(cot, grads_all[-1], all_rows[-1]), dp_count))
    out_far = swap(out_near)

    gate_share = jax.nn.sigmoid(gate_logit)
    gate_here = lax.dynamic_slice_in_dim(gate_share, span * heads_here, heads_here, 0)
    near_at, far_at = core * half_width, (1 - core) * half_width
    low_first = core == 0

    saved = []
    outputs, new_memories, new_norms = [], [], []
    for m in range(micros):
        hidden_one, projected = project(
            after(all_rows[m], all_rows[-1], grads_all[-1]),
            gain_one,
            head_weight,
        )
        if m == 0:
            near_units, near_downs = (
                lax.dynamic_slice_in_dim(w, core * inner_half, inner_half, 0)
                for w in (inner_weight, down_weight)
            )
        memory_here = lax.dynamic_slice_in_dim(memory[m, 0], span * heads_here, heads_here, 0)
        norm_here = lax.dynamic_slice_in_dim(
            normalizer[m, 0], span * heads_here, heads_here, 0
        ).reshape(heads_here, 1, head_dim)
        length = lengths[m]
        mixed_heads, dot_read, lse, new_memory, new_norm = attend(
            length, gate_here, projected, memory_here, norm_here
        )
        if m == 0:
            inner_near = lax.all_gather(
                after(near_units, all_rows[-1], out_near),
                "seq",
                axis=0,
                tiled=True,
            )
        new_memories.append(new_memory)
        new_norms.append(new_norm.reshape(heads_here, head_dim))
        mixed = lax.all_to_all(
            mixed_heads.reshape(span_count, span_rows, block_rows),
            ("rep", "seq"),
            0,
            0,
            tiled=True,
        )
        mixed = jnp.swapaxes(mixed, 0, 1).reshape(span_rows, width)
        mixed_near = lax.dynamic_slice_in_dim(mixed, near_at, half_width, 1)
        mixed_far = lax.dynamic_slice_in_dim(mixed, far_at, half_width, 1)
        after_attn = (
            own_rows[m].astype(F32)
            + nt(mixed_near, out_near)
            + nt(mixed_far, out_far)
        )
        scale_two = lax.rsqrt(jnp.mean(after_attn * after_attn, axis=-1, keepdims=True) + EPSILON)
        normed_two = after_attn * scale_two
        hidden_two = (normed_two * gain_two).astype(BF16)
        if m + 1 == micros:
            hidden_two = after(hidden_two, inner_near)
        rows_all = cube_gather(hidden_two, "dp")
        saved.append(
            dict(
                hidden_one=hidden_one,
                projected=projected,
                live=lives[m],
                grads=grads_all[m],
                memory=memory_here,
                norm=norm_here,
                length=length,
                dot_read=dot_read,
                lse=lse,
                mixed_heads=mixed_heads,
                mixed_near=mixed_near,
                mixed_far=mixed_far,
                after_attn=after_attn,
                scale_two=scale_two,
                normed_two=normed_two,
                rows=rows_all,
            )
        )

    down_near = lax.all_gather(
        near_downs,
        "seq",
        axis=0,
        tiled=True,
    )
    inner_far, down_far = swap(inner_near), swap(down_near)

    inner, down = (inner_near, inner_far), (down_near, down_far)
    last = None
    for s in saved:
        halves = []
        for half in range(2):
            halves.append(unit_pass(after(s["rows"], last), s["grads"], inner[half], down[half]))
            last = halves[-1][0]
        s["hidden"], s["grad_gates"], s["grad_ups"] = zip(*halves)

    def half_grads(left, right, half, earlier, extra=None):
        pairs = [(s[left][half], s[right]) for s in saved]
        pairs[0] = (after(pairs[0][0], earlier), pairs[0][1])
        return weight_pass(pairs, extra)

    def spread(values):
        return lax.psum_scatter(values, "seq", scatter_dimension=0, tiled=True)

    starts = jnp.stack(
        [
            (column ^ k) * span_rows + side * (span_rows // 2)
            for side, bits in enumerate(cube_bits(dp_count))
            for k in cube_order(bits)
        ]
    ).astype(jnp.int32)

    def rows_out(s, *earlier):
        gates = (after(s["grad_gates"][0], *earlier), s["grad_gates"][1])
        s["mlp_part"], s["grad_two_part"] = row_pass(
            starts, s["hidden"], gates, s["grad_ups"], inner, down
        )
        return s["grad_two_part"]

    down_far_sum = half_grads("hidden", "grads", 1, last)
    gate_far_sum = half_grads("grad_gates", "rows", 1, down_far_sum)
    down_sum = half_grads("hidden", "grads", 0, gate_far_sum, swap(down_far_sum))
    down_mine = spread(down_sum)
    last = rows_out(saved[0], down_sum)
    up_far_sum = half_grads("grad_ups", "rows", 1, last)
    gate_sum = half_grads("grad_gates", "rows", 0, up_far_sum, swap(gate_far_sum))
    gate_mine = spread(gate_sum)
    def rows_back(s, pins):
        grad_two = cube_scatter(s["grad_two_part"], "dp", pins)
        grad_scaled = grad_two * gain_two
        normed_two = s["normed_two"]
        s["grad_after"] = s["live"] + s["scale_two"] * (
            grad_scaled
            - normed_two * jnp.mean(grad_scaled * normed_two, axis=-1, keepdims=True)
        )
        s["grad_branch"] = s["grad_after"].astype(BF16)
        s["gains_two"] = jnp.sum(grad_two * normed_two, axis=0)
        grad_mixed_near = nn(s["grad_branch"], out_near).astype(BF16)
        grad_mixed_far = nn(s["grad_branch"], out_far).astype(BF16)
        grad_mixed = jnp.concatenate(
            [
                jnp.where(low_first, grad_mixed_near, grad_mixed_far),
                jnp.where(low_first, grad_mixed_far, grad_mixed_near),
            ],
            axis=1,
        )
        return lax.all_to_all(
            jnp.swapaxes(grad_mixed.reshape(span_rows, span_count, block_rows), 0, 1),
            ("rep", "seq"),
            0,
            0,
            tiled=True,
        ).reshape(total, block_rows)

    def heads_back(s, m, grad_heads):
        s["grad_projected"], gate_sums = attend_back(
            s["length"],
            gate_here,
            s["projected"],
            s["memory"],
            s["norm"],
            s["dot_read"],
            s["lse"],
            grad_heads,
        )
        s["gate"] = jnp.sum(gate_sums, axis=(1, 2))
        part_far, gains_far = project_back(
            1 - core, s["grad_projected"], head_weight, all_rows[m]
        )
        part_near, gains_near = project_back(
            core, s["grad_projected"], head_weight, all_rows[m], swap(part_far)
        )
        s["gains_one"] = (gains_far + gains_near)[0]
        return part_near

    def tokens_back(s, m, grad_one):
        rows_float = own_rows[m].astype(F32)
        scale_one = lax.rsqrt(jnp.mean(rows_float * rows_float, axis=-1, keepdims=True) + EPSILON)
        normed_one = rows_float * scale_one
        grad_scaled = grad_one * gain_one
        return (
            s["grad_after"]
            + scale_one
            * (
                grad_scaled
                - normed_one * jnp.mean(grad_scaled * normed_one, axis=-1, keepdims=True)
            )
        ).astype(BF16)

    heads_grads = [rows_back(saved[0], ())]
    last = gate_sum
    for m, s in enumerate(saved[1:]):
        last = rows_out(s, last, down_mine)
        heads_grads.append(rows_back(s, ()))

    def spread_out(s, *earlier):
        return lax.psum_scatter(
            after(s["mlp_part"], *earlier), "dp", scatter_dimension=0, tiled=True
        )

    mlp_outs, sums = [spread_out(saved[0], saved[-1]["grad_branch"])], []
    last = after(last, gate_mine)
    for m, s in enumerate(saved):
        sums.append(heads_back(s, m, after(heads_grads[m], last)))
        if m == 0:
            up_sum = half_grads("grad_ups", "rows", 0, s["grad_projected"], swap(up_far_sum))
            up_mine = spread(up_sum)
            last = after(up_sum, mlp_outs[0])
        else:
            mlp_outs.append(spread_out(s, up_sum))
    out_far_sum = weight_pass([(s["grad_branch"], s["mixed_far"]) for s in saved])
    out_sum = weight_pass(
        [(s["grad_branch"], s["mixed_near"]) for s in saved], swap(out_far_sum)
    )
    qkv_low = weight_pass([(s["grad_projected"], s["hidden_one"]) for s in saved]).reshape(
        3, block_rows, width
    )

    grad_ones, qkv_done, out_done = spread_sums(
        [after(p, up_mine, *mlp_outs).reshape(seq_count, span_rows, width) for p in sums],
        qkv_low,
        out_sum.reshape(dp_count, seq_count, shard_out, half_width),
        (dp_count, seq_count, unit, per_shard, per_block, per_column),
    )
    grad_tokens = [tokens_back(s, m, grad_ones[m]) for m, s in enumerate(saved)]
    grad_qkv = qkv_done.astype(F32)
    grad_out = jnp.swapaxes(out_done, 0, 1).reshape(shard_out, width).astype(F32)
    for s, mlp_out in zip(saved, mlp_outs):
        outputs.append((s["after_attn"] + mlp_out.astype(F32)).astype(BF16))

    def joined(name):
        return functools.reduce(jnp.add, [s[name] for s in saved])

    def both_cores(mine, axis):
        other = swap(mine)
        size = mine.shape[axis]
        shape = list(mine.shape)
        shape[axis] = 2 * size
        whole = jnp.zeros(shape, F32)
        whole = lax.dynamic_update_slice_in_dim(whole, mine.astype(F32), core * size, axis)
        return lax.dynamic_update_slice_in_dim(
            whole, other.astype(F32), (1 - core) * size, axis
        )

    grad_down = both_cores(down_mine, 0)
    grad_inner = both_cores(jnp.concatenate([gate_mine, up_mine], axis=1), 0)

    gate_terms = joined("gate") * gate_here * (1.0 - gate_here)
    gate_row = lax.dynamic_update_slice_in_dim(
        jnp.zeros((head_count,), F32), gate_terms, span * heads_here, 0
    )
    small = jnp.concatenate([joined("gains_one"), joined("gains_two"), gate_row])
    small = jnp.pad(small, (0, 8 * width - small.shape[0])).reshape(8, width)
    small = lax.all_gather(after(small, up_mine), ALL, axis=0, tiled=True)
    small = jnp.sum(small.reshape(devices, 8 * width)[:, : 3 * width], axis=0)
    gain_at = (column * seq_count + place) * shard_gain
    grad_gains = lax.dynamic_slice_in_dim(
        small[: 2 * width].reshape(2, width), gain_at, shard_gain, 1
    )
    grad_gate = small[2 * width : 2 * width + head_count]
    return (
        jnp.stack(outputs)[:, None],
        jnp.stack(new_memories)[:, None],
        jnp.stack(new_norms)[:, None],
        jnp.stack(grad_tokens)[:, None],
        grad_qkv,
        grad_out,
        grad_gains,
        grad_gate,
        grad_inner,
        grad_down,
    )


def solution(mesh):
    placed = (
        P(None, "dp", ("rep", "seq"), None),
        P(None, "dp"),
        P(None, "dp", None, None, None),
        P(None, "dp", None, None),
        P(("dp", "seq"), None),
        P(("dp", "seq"), None),
        P(None, ("dp", "seq")),
        P(),
        P(("dp", "seq"), None),
        P(("dp", "seq"), None),
        P(None, "dp", ("rep", "seq"), None),
    )
    return jax.shard_map(
        shards,
        mesh=mesh,
        in_specs=placed,
        out_specs=(
            P(None, "dp", ("rep", "seq"), None),
            P(None, "dp", ("rep", "seq"), None, None),
            P(None, "dp", ("rep", "seq"), None),
            P(None, "dp", ("rep", "seq"), None),
            P(("dp", "seq"), None),
            P(("dp", "seq"), None),
            P(None, ("dp", "seq")),
            P(),
            P(("dp", "seq"), None),
            P(("dp", "seq"), None),
        ),
        check_vma=False,
    )
```

```python
import functools
import math

import jax
import jax.numpy as jnp
from jax import lax
from jax.experimental import pallas as pl
from jax.experimental.pallas import tpu as pltpu
from jax.sharding import PartitionSpec as P

EPSILON = 1e-05
LOG2E = 1.4426950408889634
NEG = -1e30
F32 = jnp.float32
BF16 = jnp.bfloat16
ALL = ("rep", "dp", "seq")


def nt(left_side, right_side):
    return lax.dot_general(
        left_side, right_side, (((1,), (1,)), ((), ())), preferred_element_type=F32
    )


def nn(left_side, right_side):
    return lax.dot_general(
        left_side, right_side, (((1,), (0,)), ((), ())), preferred_element_type=F32
    )


def tn(left_side, right_side):
    return lax.dot_general(
        left_side, right_side, (((0,), (0,)), ((), ())), preferred_element_type=F32
    )


def elu_one(values):
    return jnp.where(values > 0.0, values + 1.0, jnp.exp(jnp.minimum(values, 0.0)))


def project_kernel(rows_ref, gain_ref, weight_ref, hidden_ref, projected_ref):
    rows = rows_ref[...].astype(F32)
    scale = lax.rsqrt(jnp.mean(rows * rows, axis=-1, keepdims=True) + EPSILON)
    hidden = (rows * scale * gain_ref[...]).astype(BF16)
    hidden_ref[...] = hidden
    projected_ref[...] = nt(hidden, weight_ref[...]).astype(BF16)


def project(rows, gain, weight):
    count, width = rows.shape
    outs = weight.shape[0]
    block = min(256, count)
    return pl.pallas_call(
        project_kernel,
        grid=(count // block,),
        in_specs=[
            pl.BlockSpec((block, width), lambda i: (i, 0)),
            pl.BlockSpec((1, width), lambda i: (0, 0)),
            pl.BlockSpec((outs, width), lambda i: (0, 0)),
        ],
        out_specs=[
            pl.BlockSpec((block, width), lambda i: (i, 0)),
            pl.BlockSpec((block, outs), lambda i: (i, 0)),
        ],
        out_shape=[
            jax.ShapeDtypeStruct((count, width), BF16),
            jax.ShapeDtypeStruct((count, outs), BF16),
        ],
        compiler_params=pltpu.CompilerParams(vmem_limit_bytes=32 << 20),
        cost_estimate=pl.CostEstimate(
            flops=2 * count * width * outs,
            bytes_accessed=4 * count * width + 2 * outs * (width + count),
            transcendentals=count,
        ),
        name="project",
    )(rows, gain, weight)


def attend_kernel(
    block,
    length_ref,
    gate_ref,
    q_ref,
    k_ref,
    v_ref,
    mem_ref,
    norm_ref,
    mixed_ref,
    dot_ref,
    lse_ref,
    new_mem_ref,
    new_norm_ref,
    v_turned,
):
    head, step = pl.program_id(0), pl.program_id(1)
    length = length_ref[0]
    total, width = k_ref.shape
    memory = mem_ref[0]
    norm_row = norm_ref[0]
    memory_low = memory.astype(BF16)

    @pl.when(step == 0)
    def _():
        v_turned[...] = v_ref[...].T
        key_sig = elu_one(k_ref[...].astype(F32))
        below = jnp.sum(key_sig * norm_row, axis=-1, keepdims=True)
        recalled = nn(key_sig.astype(BF16), memory_low) / below
        change = v_ref[...].astype(F32) - recalled
        live = lax.broadcasted_iota(jnp.int32, (total, width), 0) < length
        kept = jnp.where(live, key_sig, 0.0)
        new_mem_ref[0] = memory + tn(kept.astype(BF16), change.astype(BF16))
        new_norm_ref[0] = norm_row + jnp.sum(kept, axis=0, keepdims=True)

    queries = q_ref[...]
    factor = LOG2E * width ** (-0.5)

    def visit(at, carry, masked):
        high, mass, acc = carry
        start = pl.multiple_of(at * block, block)
        scores = nt(k_ref[pl.ds(start, block), :], queries) * factor
        if masked:
            key_at = start + lax.broadcasted_iota(jnp.int32, (block, block), 0)
            query_at = step * block + lax.broadcasted_iota(jnp.int32, (block, block), 1)
            scores = jnp.where((key_at <= query_at) & (key_at < length), scores, NEG)
        higher = jnp.maximum(high, jnp.max(scores, axis=0, keepdims=True))
        weights = jnp.exp2(scores - higher)
        shrink = jnp.exp2(high - higher)
        mass = mass * shrink + jnp.sum(weights, axis=0, keepdims=True)
        acc = acc * shrink + nn(v_turned[:, pl.ds(start, block)], weights.astype(BF16))
        return higher, mass, acc

    full = jnp.minimum(step, length // block)
    end = jnp.minimum(step + 1, (length + block - 1) // block)
    carry = (
        jnp.full((1, block), NEG, F32),
        jnp.zeros((1, block), F32),
        jnp.zeros((width, block), F32),
    )
    carry = lax.fori_loop(0, full, functools.partial(visit, masked=False), carry)
    high, mass, acc = lax.fori_loop(full, end, functools.partial(visit, masked=True), carry)
    dot_read = (acc / mass).T
    query_sig = elu_one(queries.astype(F32))
    below = jnp.sum(query_sig * norm_row, axis=-1, keepdims=True)
    mem_read = nn(query_sig.astype(BF16), memory_low) / below
    gate = gate_ref[head]
    mixed_ref[...] = (gate * mem_read + (1.0 - gate) * dot_read).astype(BF16)
    dot_ref[...] = dot_read
    lse_ref[0] = high + jnp.log2(mass)


def attend(length, gate, projected, memory, normalizer):
    total = projected.shape[0]
    heads, width = normalizer.shape[0], normalizer.shape[2]
    block = min(512, total)
    smem = pl.BlockSpec(memory_space=pltpu.SMEM)
    return pl.pallas_call(
        functools.partial(attend_kernel, block),
        grid=(heads, total // block),
        in_specs=[
            smem,
            smem,
            pl.BlockSpec((block, width), lambda h, i: (i, h)),
            pl.BlockSpec((total, width), lambda h, i: (0, heads + h)),
            pl.BlockSpec((total, width), lambda h, i: (0, 2 * heads + h)),
            pl.BlockSpec((1, width, width), lambda h, i: (h, 0, 0)),
            pl.BlockSpec((1, 1, width), lambda h, i: (h, 0, 0)),
        ],
        out_specs=[
            pl.BlockSpec((block, width), lambda h, i: (i, h)),
            pl.BlockSpec((block, width), lambda h, i: (i, h)),
            pl.BlockSpec((1, 1, block), lambda h, i: (h, 0, i)),
            pl.BlockSpec((1, width, width), lambda h, i: (h, 0, 0)),
            pl.BlockSpec((1, 1, width), lambda h, i: (h, 0, 0)),
        ],
        out_shape=[
            jax.ShapeDtypeStruct((total, heads * width), BF16),
            jax.ShapeDtypeStruct((total, heads * width), F32),
            jax.ShapeDtypeStruct((heads, 1, total), F32),
            jax.ShapeDtypeStruct((heads, width, width), F32),
            jax.ShapeDtypeStruct((heads, 1, width), F32),
        ],
        scratch_shapes=[pltpu.VMEM((width, total), BF16)],
        compiler_params=pltpu.CompilerParams(vmem_limit_bytes=40 << 20),
        cost_estimate=pl.CostEstimate(
            flops=4 * heads * total * total * width,
            bytes_accessed=heads * total * width * 12,
            transcendentals=heads * total * total,
        ),
        name="attend",
    )(length, gate, projected, projected, projected, memory, normalizer)


def attend_back_kernel(
    block,
    length_ref,
    gate_ref,
    q_ref,
    k_ref,
    v_ref,
    mem_ref,
    norm_ref,
    dot_ref,
    lse_ref,
    grad_ref,
    out_ref,
    gate_sum_ref,
    k_turned,
    k_sum,
    v_sum,
):
    head, step = pl.program_id(0), pl.program_id(1)
    heads, steps = pl.num_programs(0), pl.num_programs(1)
    length = length_ref[0]
    total, width = k_ref.shape
    gate = gate_ref[head]

    @pl.when(step == 0)
    def _():
        k_turned[...] = k_ref[...].T
        k_sum[...] = jnp.zeros_like(k_sum)
        v_sum[...] = jnp.zeros_like(v_sum)
        gate_sum_ref[...] = jnp.zeros_like(gate_sum_ref)

    queries = q_ref[...]
    query_float = queries.astype(F32)
    grad_mixed = grad_ref[...].astype(F32)
    grad_dot = ((1.0 - gate) * grad_mixed).astype(BF16)
    dot_read = dot_ref[...]
    offset = jnp.sum((grad_dot.astype(F32) * dot_read).T, axis=0, keepdims=True)
    lse = lse_ref[0]
    scale = width ** (-0.5)
    factor = LOG2E * scale

    def visit(at, acc, masked):
        start = pl.multiple_of(at * block, block)
        here = pl.ds(start, block)
        scores = nt(k_ref[here, :], queries) * factor
        weights = jnp.exp2(scores - lse)
        if masked:
            key_at = start + lax.broadcasted_iota(jnp.int32, (block, block), 0)
            query_at = step * block + lax.broadcasted_iota(jnp.int32, (block, block), 1)
            weights = jnp.where((key_at <= query_at) & (key_at < length), weights, 0.0)
        grad_probs = nt(v_ref[here, :], grad_dot)
        grad_scores = (weights * (grad_probs - offset) * scale).astype(BF16)
        v_sum[here, :] += nn(weights.astype(BF16), grad_dot)
        k_sum[here, :] += nn(grad_scores, queries)
        return acc + nn(k_turned[:, here], grad_scores)

    full = jnp.minimum(step, length // block)
    end = jnp.minimum(step + 1, (length + block - 1) // block)
    acc = jnp.zeros((width, block), F32)
    acc = lax.fori_loop(0, full, functools.partial(visit, masked=False), acc)
    acc = lax.fori_loop(full, end, functools.partial(visit, masked=True), acc)

    memory_low = mem_ref[0].astype(BF16)
    norm_row = norm_ref[0]
    query_sig = elu_one(query_float)
    below = jnp.sum(query_sig * norm_row, axis=-1, keepdims=True)
    numerator = nn(query_sig.astype(BF16), memory_low)
    inverse = 1.0 / below
    grad_read = gate * grad_mixed
    grad_below = -jnp.sum(grad_read * numerator, axis=-1, keepdims=True) * inverse * inverse
    grad_sig = nt((grad_read * inverse).astype(BF16), memory_low) + grad_below * norm_row
    slope = jnp.where(query_float > 0.0, 1.0, jnp.exp(jnp.minimum(query_float, 0.0)))
    rows = pl.ds(pl.multiple_of(step * block, block), block)
    out_ref[rows, pl.ds(pl.multiple_of(head * width, width), width)] = (
        acc.T + grad_sig * slope
    ).astype(BF16)
    gate_sum_ref[0] += jnp.sum(
        grad_mixed * (numerator * inverse - dot_read), axis=0, keepdims=True
    )

    @pl.when(step == steps - 1)
    def _():
        k_at = pl.multiple_of((heads + head) * width, width)
        v_at = pl.multiple_of((2 * heads + head) * width, width)
        out_ref[:, pl.ds(k_at, width)] = k_sum[...].astype(BF16)
        out_ref[:, pl.ds(v_at, width)] = v_sum[...].astype(BF16)


def attend_back(length, gate, projected, memory, normalizer, dot_read, lse, grad_mixed):
    total = projected.shape[0]
    heads, width = normalizer.shape[0], normalizer.shape[2]
    block = min(512, total)
    smem = pl.BlockSpec(memory_space=pltpu.SMEM)
    return pl.pallas_call(
        functools.partial(attend_back_kernel, block),
        grid=(heads, total // block),
        in_specs=[
            smem,
            smem,
            pl.BlockSpec((block, width), lambda h, i: (i, h)),
            pl.BlockSpec((total, width), lambda h, i: (0, heads + h)),
            pl.BlockSpec((total, width), lambda h, i: (0, 2 * heads + h)),
            pl.BlockSpec((1, width, width), lambda h, i: (h, 0, 0)),
            pl.BlockSpec((1, 1, width), lambda h, i: (h, 0, 0)),
            pl.BlockSpec((block, width), lambda h, i: (i, h)),
            pl.BlockSpec((1, 1, block), lambda h, i: (h, 0, i)),
            pl.BlockSpec((block, width), lambda h, i: (i, h)),
        ],
        out_specs=[
            pl.BlockSpec((total, 3 * heads * width), lambda h, i: (0, 0)),
            pl.BlockSpec((1, 1, width), lambda h, i: (h, 0, 0)),
        ],
        out_shape=[
            jax.ShapeDtypeStruct((total, 3 * heads * width), BF16),
            jax.ShapeDtypeStruct((heads, 1, width), F32),
        ],
        scratch_shapes=[
            pltpu.VMEM((width, total), BF16),
            pltpu.VMEM((total, width), F32),
            pltpu.VMEM((total, width), F32),
        ],
        compiler_params=pltpu.CompilerParams(vmem_limit_bytes=40 << 20),
        cost_estimate=pl.CostEstimate(
            flops=10 * heads * total * total * width,
            bytes_accessed=heads * total * width * 20,
            transcendentals=heads * total * total,
        ),
        name="attend_back",
    )(length, gate, projected, projected, projected, memory, normalizer, dot_read, lse, grad_mixed)


def unit_kernel(
    rows_ref, grad_ref, inner_ref, down_ref, hidden_ref, grad_gate_ref, grad_up_ref
):
    width = rows_ref.shape[1]
    rows = rows_ref[...]
    gates = nt(rows, inner_ref[:, :width])
    ups = nt(rows, inner_ref[:, width:])
    grad_hidden = nt(grad_ref[...], down_ref[...])
    sigmoid = 1.0 / (1.0 + jnp.exp(-gates))
    silu = gates * sigmoid
    hidden_ref[...] = (silu * ups).astype(BF16)
    grad_gate_ref[...] = (
        grad_hidden * ups * (sigmoid * (1.0 + gates * (1.0 - sigmoid)))
    ).astype(BF16)
    grad_up_ref[...] = (grad_hidden * silu).astype(BF16)


def unit_pass(rows, grads, inner, down):
    count, width = rows.shape
    units = inner.shape[0]
    tile = min(256, units)
    resident = pl.BlockSpec((count, width), lambda t: (0, 0), pipeline_mode=pl.Buffered(1))
    column = pl.BlockSpec((count, tile), lambda t: (0, t))
    unit_shape = jax.ShapeDtypeStruct((count, units), BF16)
    return pl.pallas_call(
        unit_kernel,
        grid=(units // tile,),
        in_specs=[
            resident,
            resident,
            pl.BlockSpec((tile, 2 * width), lambda t: (t, 0)),
            pl.BlockSpec((tile, width), lambda t: (t, 0)),
        ],
        out_specs=[column] * 3,
        out_shape=[unit_shape] * 3,
        compiler_params=pltpu.CompilerParams(vmem_limit_bytes=56 << 20),
        cost_estimate=pl.CostEstimate(
            flops=2 * 3 * count * width * units,
            bytes_accessed=units * (6 * width + 6 * count) + 4 * count * width,
            transcendentals=count * units,
        ),
        name="unit_pass",
    )(rows, grads, inner, down)


def weight_kernel(pairs, *refs):
    out_ref = refs[-1]
    total = tn(refs[0][...], refs[1][...])
    for at in range(1, pairs):
        total += tn(refs[2 * at][...], refs[2 * at + 1][...])
    if len(refs) > 2 * pairs + 1:
        total += refs[2 * pairs][...].astype(F32)
    out_ref[...] = total.astype(BF16)


def weight_pass(pairs, extra=None):
    size, width = pairs[0][0].shape[1], pairs[0][1].shape[1]
    tile = min(256, size)
    in_specs, operands, flops, moved = [], [], 0, 2 * size * width
    for left, right in pairs:
        count = left.shape[0]
        in_specs.append(pl.BlockSpec((count, tile), lambda t: (0, t)))
        in_specs.append(
            pl.BlockSpec((count, width), lambda t: (0, 0), pipeline_mode=pl.Buffered(1))
        )
        operands += [left, right]
        flops += 2 * count * size * width
        moved += 2 * count * (size + width)
    if extra is not None:
        in_specs.append(pl.BlockSpec((tile, width), lambda t: (t, 0)))
        operands.append(extra)
        moved += 2 * size * width
    return pl.pallas_call(
        functools.partial(weight_kernel, len(pairs)),
        grid=(size // tile,),
        in_specs=in_specs,
        out_specs=pl.BlockSpec((tile, width), lambda t: (t, 0)),
        out_shape=jax.ShapeDtypeStruct((size, width), BF16),
        compiler_params=pltpu.CompilerParams(vmem_limit_bytes=56 << 20),
        cost_estimate=pl.CostEstimate(flops=flops, bytes_accessed=moved, transcendentals=0),
        name="weight_pass",
    )(*operands)


def back_kernel(half_ref, grad_ref, weight_ref, rows_ref, *refs):
    out_ref, gain_ref = refs[-2:]

    @pl.when(pl.program_id(0) == 0)
    def _():
        gain_ref[...] = jnp.zeros_like(gain_ref)

    part = nn(grad_ref[...], weight_ref[...])
    total = part + refs[0][...].astype(F32) if len(refs) > 2 else part
    out_ref[...] = total.astype(BF16)
    rows = rows_ref[...].astype(F32)
    scale = lax.rsqrt(jnp.mean(rows * rows, axis=-1, keepdims=True) + EPSILON)
    gain_ref[...] += jnp.sum(part * (rows * scale), axis=0, keepdims=True)


def project_back(half, grads, weight, rows, extra=None):
    count, outs = grads.shape[0] // 2, grads.shape[1]
    width = weight.shape[1]
    block = min(256, count)
    steps = count // block
    return pl.pallas_call(
        back_kernel,
        grid_spec=pltpu.PrefetchScalarGridSpec(
            num_scalar_prefetch=1,
            grid=(steps,),
            in_specs=[
                pl.BlockSpec((block, outs), lambda i, at: (at[0] * steps + i, 0)),
                pl.BlockSpec((outs, width), lambda i, at: (0, 0)),
                pl.BlockSpec((block, width), lambda i, at: (at[0] * steps + i, 0)),
            ]
            + [pl.BlockSpec((block, width), lambda i, at: (i, 0))] * (extra is not None),
            out_specs=[
                pl.BlockSpec((block, width), lambda i, at: (i, 0)),
                pl.BlockSpec((1, width), lambda i, at: (0, 0)),
            ],
        ),
        out_shape=[
            jax.ShapeDtypeStruct((count, width), BF16),
            jax.ShapeDtypeStruct((1, width), F32),
        ],
        compiler_params=pltpu.CompilerParams(vmem_limit_bytes=40 << 20),
        cost_estimate=pl.CostEstimate(
            flops=2 * count * width * outs,
            bytes_accessed=4 * count * width + 2 * outs * (width + count),
            transcendentals=count,
        ),
        name="project_back",
    )(
        jnp.reshape(half, (1,)).astype(jnp.int32),
        grads,
        weight,
        rows,
        *([] if extra is None else [extra]),
    )


def swap(values):
    return lax.ppermute(values, "rep", [(0, 1), (1, 0)])


def after(values, *earlier):
    earlier = [e for e in earlier if e is not None]
    return lax.optimization_barrier((values, *earlier))[0] if earlier else values


def add_low(left_side, right_side):
    return (left_side.astype(F32) + right_side.astype(F32)).astype(BF16)


def line_gather(values, axis):
    count = lax.axis_size(axis)
    here = lax.axis_index(axis)
    rows = values.shape[0]
    table = jnp.zeros(((3 * count - 2) * rows,) + values.shape[1:], values.dtype)

    def put(table, piece, origin):
        return lax.dynamic_update_slice_in_dim(table, piece, (origin + count - 1) * rows, 0)

    table = put(table, values, here)
    rising = falling = values
    for hop in range(1, count):
        rising = lax.ppermute(
            rising, axis, [(a, a + 1) for a in range(count - 1) if a >= hop - 1]
        )
        falling = lax.ppermute(
            falling, axis, [(a, a - 1) for a in range(1, count) if a + hop - 1 < count]
        )
        table = put(table, rising, here - hop)
        table = put(table, falling, here + hop)
    return table[(count - 1) * rows : (2 * count - 1) * rows]


def line_scatter(values, axis, pins=()):
    count = lax.axis_size(axis)
    here = lax.axis_index(axis)
    rows = values.shape[0] // count

    def block(owner):
        start = jnp.clip(owner, 0, count - 1) * rows
        return lax.dynamic_slice_in_dim(values, start, rows, 0).astype(F32)

    rising = falling = None
    for hop in range(1, count):
        reach = count - hop
        up, down = block(here + reach), block(here - reach)
        if rising is not None:
            up, down = up + rising.astype(F32), down + falling.astype(F32)
        rising = lax.ppermute(
            up.astype(BF16), axis, [(a, a + 1) for a in range(count) if a + reach < count]
        )
        falling = lax.ppermute(
            down.astype(BF16), axis, [(a, a - 1) for a in range(count) if a - reach >= 0]
        )
        if hop <= len(pins):
            rising, falling = after(rising, pins[hop - 1]), after(falling, pins[hop - 1])
    return block(here) + rising.astype(F32) + falling.astype(F32)


def cube_bits(count):
    bits = [1 << b for b in range(count.bit_length() - 1)]
    return bits, bits[::-1]


def cube_order(bits):
    order = [0]
    for bit in reversed(bits):
        order = order + [k | bit for k in order]
    return order


def cube_gather(values, axis):
    count = lax.axis_size(axis)
    half = values.shape[0] // 2
    parts = []
    for bits, start in zip(cube_bits(count), (0, half)):
        held = {0: values[start : start + half]}
        for bit in bits:
            pairs = [(a, a ^ bit) for a in range(count)]
            held.update({k ^ bit: lax.ppermute(v, axis, pairs) for k, v in list(held.items())})
        parts += [held[k] for k in cube_order(bits)]
    return jnp.concatenate(parts, axis=0)


def cube_scatter(values, axis, pins=()):
    count = lax.axis_size(axis)
    half = values.shape[0] // 2
    parts = []
    for bits, start in zip(cube_bits(count), (0, half)):
        held = values[start : start + half]
        for at, bit in enumerate(bits):
            pairs = [(a, a ^ bit) for a in range(count)]
            keep = held.shape[0] // 2
            got = lax.ppermute(held[keep:].astype(BF16), axis, pairs)
            if at < len(pins):
                got = after(got, pins[at])
            held = held[:keep].astype(F32) + got.astype(F32)
        parts.append(held)
    return jnp.concatenate(parts, axis=0)


def remote(source, target, sent, landed, device):
    return pltpu.make_async_remote_copy(
        src_ref=source,
        dst_ref=target,
        send_sem=sent,
        recv_sem=landed,
        device_id=device,
        device_id_type=pl.DeviceIdType.MESH,
    )


def greet(devices):
    barrier = pltpu.get_barrier_semaphore()
    for device in devices:
        pl.semaphore_signal(barrier, inc=1, device_id=device, device_id_type=pl.DeviceIdType.MESH)
    pl.semaphore_wait(barrier, len(devices))


def heads_kernel(
    sizes,
    qkv_ref,
    gain_ref,
    head_ref,
    gains_ref,
    landed,
    unit_sent,
    unit_here,
    block_sent,
    block_here,
    line_sent,
    line_here,
    cube_sent,
    cube_here,
    local,
):
    dp_count, seq_count, unit, per_shard, per_block, per_column = sizes
    span_count = 2 * seq_count
    block_rows = unit * per_block
    core, column, place = lax.axis_index("rep"), lax.axis_index("dp"), lax.axis_index("seq")
    span, shard = core * seq_count + place, column * seq_count + place
    line = [(core, column, (place + k) % seq_count) for k in range(1, seq_count)]
    cube = [(core, (column + k) % dp_count, place) for k in range(1, dp_count)]
    greet(line + cube)

    gains = []
    for k, device in enumerate(line):
        gains.append(
            remote(gain_ref, gains_ref.at[shard], line_sent.at[k], line_here.at[k], device)
        )
    for copy in gains:
        copy.start()
    own_gain = pltpu.make_async_copy(gain_ref, gains_ref.at[shard], local.at[0])
    own_gain.start()

    def rows(ref, at, size):
        return ref.at[pl.ds(pl.multiple_of(at * size, size), size)]

    def unit_copy(i):
        number = shard * per_shard + i
        owner = (number // per_block) % span_count
        source, target = rows(qkv_ref, i, unit), rows(landed, number % per_block, unit)
        far = remote(
            source,
            target,
            unit_sent.at[i],
            unit_here.at[number % per_block],
            (core, column, owner % seq_count),
        )
        near = pltpu.make_async_copy(source, target, local.at[1 + i])
        mine = owner // seq_count == core
        stays = owner % seq_count == place
        return far, near, mine & jnp.logical_not(stays), mine & stays

    for i in range(per_shard):
        far, near, leaves, stays = unit_copy(i)
        pl.when(leaves)(far.start)
        pl.when(stays)(near.start)
    for i in range(per_shard):
        _, near, _, stays = unit_copy(i)
        pl.when(stays)(near.wait)

    def block_copies(part):
        target = rows(head_ref, part, block_rows)
        far = [
            remote(landed, target, block_sent.at[k], block_here.at[part], device)
            for k, device in enumerate(cube)
        ]
        return far, pltpu.make_async_copy(landed, target, local.at[0])

    own_gain.wait()
    for part in range(3):
        number = part * span_count + span

        @pl.when(number // per_column == column)
        def _():
            for j in range(per_block):
                source = ((number * per_block + j) // per_shard) % seq_count

                @pl.when(source != place)
                def _():
                    here = rows(landed, j, unit)
                    remote(here, here, unit_sent.at[0], unit_here.at[j], line[0]).wait_recv()

            far, near = block_copies(part)
            for copy in far:
                copy.start()
            near.start()

    for copy in gains:
        copy.wait()
    mine = gains_ref.at[pl.ds(column * seq_count, seq_count)]
    gains = [
        remote(mine, mine, cube_sent.at[k], cube_here.at[k], device)
        for k, device in enumerate(cube)
    ]
    for copy in gains:
        copy.start()
    for part in range(3):
        number = part * span_count + span
        far, near = block_copies(part)

        @pl.when(number // per_column == column)
        def _():
            near.wait()
            for copy in far:
                copy.wait_send()

        @pl.when(number // per_column != column)
        def _():
            far[0].wait_recv()

    for k, copy in enumerate(gains):
        copy.wait_send()
        origin = (column + dp_count - k - 1) % dp_count
        theirs = gains_ref.at[pl.ds(origin * seq_count, seq_count)]
        remote(theirs, theirs, cube_sent.at[k], cube_here.at[k], cube[k]).wait_recv()
    for i in range(per_shard):
        far, _, leaves, _ = unit_copy(i)
        pl.when(leaves)(far.wait_send)


def gather_heads(qkv_weight, gains, sizes):
    dp_count, seq_count, unit, per_shard, per_block, _ = sizes
    width = qkv_weight.shape[1]
    block_rows = unit * per_block
    anywhere = pl.BlockSpec(memory_space=pl.ANY)
    dma = pltpu.SemaphoreType.DMA
    return pl.pallas_call(
        functools.partial(heads_kernel, sizes),
        in_specs=[anywhere, anywhere],
        out_specs=[anywhere, anywhere],
        out_shape=[
            jax.ShapeDtypeStruct((3 * block_rows, width), BF16),
            jax.ShapeDtypeStruct((dp_count * seq_count, *gains.shape), F32),
        ],
        scratch_shapes=[
            pltpu.VMEM((block_rows, width), BF16),
            dma((per_shard,)),
            dma((per_block,)),
            dma((dp_count - 1,)),
            dma((3,)),
            dma((seq_count - 1,)),
            dma((seq_count - 1,)),
            dma((dp_count - 1,)),
            dma((dp_count - 1,)),
            dma((1 + per_shard,)),
        ],
        compiler_params=pltpu.CompilerParams(
            collective_id=0, has_side_effects=True, vmem_limit_bytes=16 << 20
        ),
        cost_estimate=pl.CostEstimate(
            flops=0, bytes_accessed=64 * block_rows * width, transcendentals=0
        ),
        name="gather_heads",
    )(qkv_weight, gains)


def flipped(value, bits):
    bit = 1
    while bit <= bits:
        if bits & bit:
            value = value + bit - 2 * bit * ((value // bit) % 2)
        bit *= 2
    return value


def cot_copies(cot_ref, cot_all, cube, sent, here, local, first):
    count = len(cube) + 1
    half = cot_ref.shape[0] // 2
    stays, leaves = [], []
    for side, bits in enumerate(cube_bits(count)):
        order = cube_order(bits)
        source = cot_ref.at[pl.ds(side * half, half)]
        for k in range(count):
            target = cot_all.at[pl.ds((side * count + order.index(k)) * half, half)]
            if k == 0:
                stays.append(pltpu.make_async_copy(source, target, local.at[first + side]))
            else:
                at = side * (count - 1) + k - 1
                leaves.append(remote(source, target, sent.at[at], here.at[at], cube[k - 1]))
    return stays, leaves


def cot_kernel(count, cot_ref, cot_all, sent, here, local):
    core, column, place = lax.axis_index("rep"), lax.axis_index("dp"), lax.axis_index("seq")
    cube = [(core, flipped(column, k), place) for k in range(1, count)]
    greet(cube)
    stays, leaves = cot_copies(cot_ref, cot_all, cube, sent, here, local, 0)
    for copy in stays + leaves:
        copy.start()
    for copy in stays + leaves:
        copy.wait()


def gather_cot(cot, count):
    rows, width = cot.shape
    anywhere = pl.BlockSpec(memory_space=pl.ANY)
    dma = pltpu.SemaphoreType.DMA
    return pl.pallas_call(
        functools.partial(cot_kernel, count),
        in_specs=[anywhere],
        out_specs=anywhere,
        out_shape=jax.ShapeDtypeStruct((count * rows, width), BF16),
        scratch_shapes=[dma((2 * (count - 1),)), dma((2 * (count - 1),)), dma((2,))],
        compiler_params=pltpu.CompilerParams(collective_id=3, has_side_effects=True),
        cost_estimate=pl.CostEstimate(
            flops=0, bytes_accessed=8 * rows * width, transcendentals=0
        ),
        name="gather_cot",
    )(cot)


def rest_kernel(sizes, *refs):
    dp_count, seq_count = sizes
    out_ref, cot_ref, out_all, cot_all = refs[:4]
    line_sent, line_here, cube_sent, cube_here, cot_sent, cot_here, local = refs[4:]
    core, column, place = lax.axis_index("rep"), lax.axis_index("dp"), lax.axis_index("seq")
    line = [(core, column, (place + k) % seq_count) for k in range(1, seq_count)]
    cube = [(core, flipped(column, k), place) for k in range(1, dp_count)]
    greet(line + cube)
    shard_rows = out_ref.shape[0]
    column_rows = seq_count * shard_rows
    def out_rows(start, size):
        return out_all.at[pl.ds(pl.multiple_of(start, shard_rows), size)]

    mine = out_rows((column * seq_count + place) * shard_rows, shard_rows)
    lines = [
        remote(out_ref, mine, line_sent.at[k], line_here.at[k], device)
        for k, device in enumerate(line)
    ]
    own_out = pltpu.make_async_copy(out_ref, mine, local.at[0])

    own_cots, cots = cot_copies(cot_ref, cot_all, cube, cot_sent, cot_here, local, 1)
    for copy in lines + [own_out] + own_cots + cots:
        copy.start()
    own_out.wait()
    for copy in lines:
        copy.wait()
    mine = out_rows(column * column_rows, column_rows)
    cubes = [
        remote(mine, mine, cube_sent.at[k], cube_here.at[k], device)
        for k, device in enumerate(cube)
    ]
    for copy in cubes:
        copy.start()
    for copy in own_cots + cots:
        copy.wait()
    for k, copy in enumerate(cubes):
        copy.wait_send()
        theirs = out_rows(cube[k][1] * column_rows, column_rows)
        remote(theirs, theirs, cube_sent.at[k], cube_here.at[k], cube[k]).wait_recv()


def gather_rest(out_half, cot, sizes):
    dp_count, seq_count = sizes
    rows, width = cot.shape
    anywhere = pl.BlockSpec(memory_space=pl.ANY)
    dma = pltpu.SemaphoreType.DMA
    return pl.pallas_call(
        functools.partial(rest_kernel, sizes),
        in_specs=[anywhere] * 2,
        out_specs=[anywhere] * 2,
        out_shape=[
            jax.ShapeDtypeStruct(
                (dp_count * seq_count * out_half.shape[0], out_half.shape[1]), BF16
            ),
            jax.ShapeDtypeStruct((dp_count * rows, width), BF16),
        ],
        scratch_shapes=[
            dma((seq_count - 1,)),
            dma((seq_count - 1,)),
            dma((dp_count - 1,)),
            dma((dp_count - 1,)),
            dma((2 * (dp_count - 1),)),
            dma((2 * (dp_count - 1),)),
            dma((3,)),
        ],
        compiler_params=pltpu.CompilerParams(collective_id=2, has_side_effects=True),
        cost_estimate=pl.CostEstimate(
            flops=0, bytes_accessed=8 * rows * width, transcendentals=0
        ),
        name="gather_rest",
    )(out_half, cot)


def row_kernel(count, *refs):
    hidden, gates, ups, gate_w, up_w, down_w = (refs[2 * i : 2 * i + 2] for i in range(6))
    out_ref, grad_ref, parts, landed, sent, here = refs[12:]
    step, steps = pl.program_id(0), pl.num_programs(0)
    core, column, place = lax.axis_index("rep"), lax.axis_index("dp"), lax.axis_index("seq")
    cube = [(core, flipped(column, k), place) for k in range(1, count)]

    @pl.when(step == 0)
    def _():
        greet(cube)

    size = out_ref.shape[0] // (2 * count)
    spots = [
        (side, at, order_k)
        for side, bits in enumerate(cube_bits(count))
        for at, order_k in enumerate(cube_order(bits))
    ]

    def piece(side, at):
        return pl.ds((side * count + at) * size, size)

    def leaving(t, side, at, k):
        number = side * (count - 1) + k - 1
        flat = t * (2 * (count - 1)) + number
        return remote(
            parts.at[t, piece(side, at)],
            landed.at[t, number],
            sent.at[flat],
            here.at[flat],
            cube[k - 1],
        )

    parts[step] = (
        nn(gates[0][...], gate_w[0][...])
        + nn(gates[1][...], gate_w[1][...])
        + nn(ups[0][...], up_w[0][...])
        + nn(ups[1][...], up_w[1][...])
    ).astype(BF16)
    for side, at, k in spots:
        if k:
            leaving(step, side, at, k).start()
    out = (
        nn(hidden[0][...], down_w[0][...]) + nn(hidden[1][...], down_w[1][...])
    ).astype(BF16)
    for side, at, k in spots:
        owner = flipped(column, k) if k else column
        start = pl.multiple_of((2 * owner + side) * size, size)
        out_ref[pl.ds(start, size), :] = out[(side * count + at) * size :][:size]

    @pl.when(step == steps - 1)
    def _():
        width = parts.shape[2]

        def finish(t, _):
            for side, at, k in spots:
                if k:
                    leaving(t, side, at, k).wait()
            columns = pl.ds(pl.multiple_of(t * width, width), width)
            for side in range(2):
                total = parts[t, piece(side, 0), :].astype(F32)
                for k in range(1, count):
                    total += landed[t, side * (count - 1) + k - 1].astype(F32)
                grad_ref[side * size : (side + 1) * size, columns] = total
            return 0

        lax.fori_loop(0, steps, finish, 0)


def row_pass(hidden, grad_gates, grad_ups, inner, down, dp_count):
    count, units = hidden[0].shape
    width = down[0].shape[1]
    tile = min(256, width)
    tiles = width // tile
    pieces = 2 * (dp_count - 1)
    size = count // (2 * dp_count)
    resident = pl.BlockSpec((count, units), lambda t: (0, 0), pipeline_mode=pl.Buffered(1))
    low = pl.BlockSpec((units, tile), lambda t: (0, t))
    high = pl.BlockSpec((units, tile), lambda t: (0, tiles + t))
    dma = pltpu.SemaphoreType.DMA
    return pl.pallas_call(
        functools.partial(row_kernel, dp_count),
        grid=(tiles,),
        in_specs=[resident] * 6 + [low, low, high, high, low, low],
        out_specs=[
            pl.BlockSpec((count, tile), lambda t: (0, t)),
            pl.BlockSpec((2 * size, width), lambda t: (0, 0)),
        ],
        out_shape=[
            jax.ShapeDtypeStruct((count, width), BF16),
            jax.ShapeDtypeStruct((2 * size, width), F32),
        ],
        scratch_shapes=[
            pltpu.VMEM((tiles, count, tile), BF16),
            pltpu.VMEM((tiles, pieces, size, tile), BF16),
            dma((tiles * pieces,)),
            dma((tiles * pieces,)),
        ],
        compiler_params=pltpu.CompilerParams(
            collective_id=4, has_side_effects=True, vmem_limit_bytes=56 << 20
        ),
        cost_estimate=pl.CostEstimate(
            flops=2 * 3 * count * width * 2 * units,
            bytes_accessed=12 * units * (width + count) + 4 * count * width,
            transcendentals=0,
        ),
        name="row_pass",
    )(*hidden, *grad_gates, *grad_ups, *inner, *inner, *down)


def add_rows(out_ref, refs, size):
    def some(i, _):
        rows = pl.ds(pl.multiple_of(i * size, size), size)
        total = refs[0][rows, :].astype(F32)
        for ref in refs[1:]:
            total += ref[rows, :].astype(F32)
        out_ref[rows, :] = total.astype(out_ref.dtype)
        return 0

    lax.fori_loop(0, out_ref.shape[0] // size, some, 0)


def spread_kernel(
    sizes,
    micros,
    *refs,
):
    spread_body(sizes, refs[:micros], *refs[micros:])


def spread_body(
    sizes,
    line_refs,
    qkv_ref,
    out_ref,
    grad_ref,
    qkv_done,
    out_done,
    rising,
    falling,
    qkv_in,
    qkv_sum,
    out_in,
    out_part,
    out_line,
    rise_sent,
    rise_here,
    fall_sent,
    fall_here,
    qkv_sent,
    qkv_here,
    out_sent,
    out_here,
    unit_sent,
    unit_here,
    line_sent,
    line_here,
    swap_sent,
    swap_here,
    local,
):
    dp_count, seq_count, unit, per_shard, per_block, per_column = sizes
    span_count = 2 * seq_count
    micros = len(line_refs)
    core, column, place = lax.axis_index("rep"), lax.axis_index("dp"), lax.axis_index("seq")
    span = core * seq_count + place
    cube = [(core, (column + k) % dp_count, place) for k in range(1, dp_count)]
    line = [(core, column, (place + k) % seq_count) for k in range(1, seq_count)]
    across = [(1 - core, column, (place + k) % seq_count) for k in range(seq_count)]
    greet(cube + line + across)

    def part_at(part, col):
        return (part * span_count + span) // per_column == col

    def out_copy(k):
        target = cube[k]
        return remote(
            out_ref.at[target[1]], out_in.at[k], out_sent.at[k], out_here.at[k], target
        )

    def qkv_copy(k, part):
        return remote(
            qkv_ref.at[part], qkv_in.at[k], qkv_sent.at[k], qkv_here.at[k], cube[k]
        )

    def hop(number, m, up):
        reach = seq_count - number
        buffer, sent, here = (
            (rising, rise_sent, rise_here) if up else (falling, fall_sent, fall_here)
        )
        behind = place if up else seq_count - 1 - place
        owner = place + reach if up else place - reach
        owner = jnp.clip(owner, 0, seq_count - 1)
        next_place = jnp.clip(place + 1 if up else place - 1, 0, seq_count - 1)
        device = (core, column, next_place)
        at = (number - 1) * micros + m
        target = buffer.at[at]

        def send(source):
            remote(source, target, sent.at[at], here.at[at], device).start()

        own = line_refs[m].at[owner]
        if number == 1:
            pl.when(behind == 0)(lambda: send(own))
            return

        @pl.when(behind == 0)
        def _():
            send(own)

        @pl.when((behind >= 1) & (behind <= number - 1))
        def _():
            before = buffer.at[at - micros]
            remote(before, before, sent.at[0], here.at[at - micros], across[0]).wait_recv()
            add_rows(before, [before, own], 64)
            send(before)

    def hop_sent(number, m, up):
        sent = rise_sent if up else fall_sent
        buffer = rising if up else falling
        behind = place if up else seq_count - 1 - place
        at = (number - 1) * micros + m
        piece = buffer.at[at]

        @pl.when(behind <= number - 1)
        def _():
            remote(piece, piece, sent.at[at], sent.at[at], across[0]).wait_send()

    def hops(number):
        for m in range(micros):
            hop(number, m, True)
            hop(number, m, False)

    hops(1)
    for k in range(dp_count - 1):
        out_copy(k).start()
        for part in range(3):

            @pl.when(part_at(part, cube[k][1]))
            def _():
                qkv_copy(k, part).start()

    hops(2)

    for k in range(dp_count - 1):
        out_copy(k).wait_recv()
    for s in range(seq_count):
        add_rows(
            out_part.at[s],
            [out_ref.at[column, s]] + [out_in.at[k, s] for k in range(dp_count - 1)],
            32,
        )

    def line_copy(k):
        return remote(
            out_part.at[line[k][2]], out_line.at[k], line_sent.at[k], line_here.at[k], line[k]
        )

    for k in range(seq_count - 1):
        line_copy(k).start()

    def unit_copies(part, j):
        number = (part * span_count + span) * per_block + j
        owner = (number // per_shard) % seq_count
        source = qkv_sum.at[pl.ds(j * unit, unit)]
        target = qkv_done.at[pl.ds(pl.multiple_of((number % per_shard) * unit, unit), unit)]
        here = unit_here.at[number % per_shard]
        other = remote(
            source, target, unit_sent.at[2 * j], here, (1 - core, column, owner)
        )
        same = remote(source, target, unit_sent.at[2 * j + 1], here, (core, column, owner))
        stays = pltpu.make_async_copy(source, target, local.at[j])
        return owner, other, same, stays

    for part in range(3):

        @pl.when(part_at(part, column))
        def _():
            for k in range(dp_count - 1):
                qkv_copy(k, part).wait_recv()
            add_rows(
                qkv_sum, [qkv_ref.at[part]] + [qkv_in.at[k] for k in range(dp_count - 1)], 32
            )
            for j in range(per_block):
                owner, other, same, stays = unit_copies(part, j)
                other.start()
                pl.when(owner != place)(same.start)
                pl.when(owner == place)(stays.start)

    for number in range(3, seq_count):
        hops(number)

    for k in range(seq_count - 1):
        line_copy(k).wait_recv()
    add_rows(
        out_done.at[core],
        [out_part.at[place]] + [out_line.at[k] for k in range(seq_count - 1)],
        32,
    )
    mine = out_done.at[core]
    swapped = remote(mine, mine, swap_sent, swap_here, across[0])
    swapped.start()

    last = (seq_count - 2) * micros
    for m in range(micros):
        own = line_refs[m].at[place]
        up, down = rising.at[last + m], falling.at[last + m]

        @pl.when(place > 0)
        def _():
            remote(up, up, rise_sent.at[0], rise_here.at[last + m], across[0]).wait_recv()

        @pl.when(place < seq_count - 1)
        def _():
            remote(down, down, fall_sent.at[0], fall_here.at[last + m], across[0]).wait_recv()

        @pl.when(place == 0)
        def _():
            add_rows(grad_ref.at[m], [own, down], 64)

        @pl.when(place == seq_count - 1)
        def _():
            add_rows(grad_ref.at[m], [own, up], 64)

        @pl.when((place > 0) & (place < seq_count - 1))
        def _():
            add_rows(grad_ref.at[m], [own, up, down], 64)

    for number in range(1, seq_count):
        for m in range(micros):
            hop_sent(number, m, True)
            hop_sent(number, m, False)
    for k in range(dp_count - 1):
        out_copy(k).wait_send()
        for part in range(3):

            @pl.when(part_at(part, cube[k][1]))
            def _():
                qkv_copy(k, part).wait_send()

    for k in range(seq_count - 1):
        line_copy(k).wait_send()
    for part in range(3):

        @pl.when(part_at(part, column))
        def _():
            for j in range(per_block):
                owner, other, same, stays = unit_copies(part, j)
                other.wait_send()
                pl.when(owner != place)(same.wait_send)
                pl.when(owner == place)(stays.wait)

    for i in range(per_shard):
        number = (column * seq_count + place) * per_shard + i
        piece = qkv_done.at[pl.ds(i * unit, unit)]

        @pl.when((number // per_block) % span_count != span)
        def _():
            remote(piece, piece, unit_sent.at[0], unit_here.at[i], across[0]).wait_recv()

    swapped.wait_send()
    theirs = out_done.at[1 - core]
    remote(theirs, theirs, swap_sent, swap_here, across[0]).wait_recv()


def spread_sums(lines, qkv, out, sizes):
    dp_count, seq_count, unit, per_shard, per_block, _ = sizes
    micros = len(lines)
    _, rows, width = lines[0].shape
    shard_out, half_width = out.shape[2:]
    block_rows = unit * per_block
    hops = (seq_count - 1) * micros
    vmem = pl.BlockSpec(memory_space=pltpu.VMEM)
    dma = pltpu.SemaphoreType.DMA
    return pl.pallas_call(
        functools.partial(spread_kernel, sizes, micros),
        in_specs=[vmem] * (micros + 2),
        out_specs=[vmem] * 3,
        out_shape=[
            jax.ShapeDtypeStruct((micros, rows, width), F32),
            jax.ShapeDtypeStruct((per_shard * unit, width), BF16),
            jax.ShapeDtypeStruct((2, shard_out, half_width), BF16),
        ],
        scratch_shapes=[
            pltpu.VMEM((hops, rows, width), BF16),
            pltpu.VMEM((hops, rows, width), BF16),
            pltpu.VMEM((dp_count - 1, block_rows, width), BF16),
            pltpu.VMEM((block_rows, width), BF16),
            pltpu.VMEM((dp_count - 1, seq_count, shard_out, half_width), BF16),
            pltpu.VMEM((seq_count, shard_out, half_width), BF16),
            pltpu.VMEM((seq_count - 1, shard_out, half_width), BF16),
            dma((hops,)),
            dma((hops,)),
            dma((hops,)),
            dma((hops,)),
            dma((dp_count - 1,)),
            dma((dp_count - 1,)),
            dma((dp_count - 1,)),
            dma((dp_count - 1,)),
            dma((2 * per_block,)),
            dma((per_shard,)),
            dma((seq_count - 1,)),
            dma((seq_count - 1,)),
            dma,
            dma,
            dma((per_block,)),
        ],
        compiler_params=pltpu.CompilerParams(
            collective_id=1, has_side_effects=True, vmem_limit_bytes=56 << 20
        ),
        cost_estimate=pl.CostEstimate(
            flops=0, bytes_accessed=256 * rows * width, transcendentals=0
        ),
        name="spread_sums",
    )(*lines, qkv, out)


def pick(table, number):
    return jnp.asarray(table, jnp.int32)[number]


def shards(
    tokens,
    lengths,
    memory,
    normalizer,
    qkv_weight,
    out_weight,
    norm_gains,
    gate_logit,
    inner_weight,
    down_weight,
    cotangent,
):
    micros, _, span_rows, width = tokens.shape
    head_count = gate_logit.shape[0]
    head_dim = width // head_count
    dp_count, seq_count = lax.axis_size("dp"), lax.axis_size("seq")
    span_count = 2 * seq_count
    total = span_rows * span_count
    heads_here = head_count // span_count
    block_rows = heads_here * head_dim
    core, column, place = lax.axis_index("rep"), lax.axis_index("dp"), lax.axis_index("seq")
    span = core * seq_count + place
    inner_half = inner_weight.shape[0] // 2

    own_rows = [tokens[m, 0] for m in range(micros)]

    def gather_rows(rows):
        return lax.all_gather(rows, ("rep", "seq"), axis=0, tiled=True)

    all_rows = [gather_rows(own_rows[0])]

    unit = math.gcd(qkv_weight.shape[0], block_rows)
    per_shard, per_block = qkv_weight.shape[0] // unit, block_rows // unit
    per_column = 3 * span_count // dp_count
    devices = 2 * dp_count * seq_count
    shard_out, shard_gain = out_weight.shape[0], norm_gains.shape[1]
    lanes = -(-shard_gain // 128) * 128
    gain_tile = jnp.zeros((8, lanes), F32)
    gain_tile = lax.dynamic_update_slice(gain_tile, norm_gains.astype(F32), (0, 0))
    head_weight, gains_all = gather_heads(
        qkv_weight, gain_tile, (dp_count, seq_count, unit, per_shard, per_block, per_column)
    )
    gains_all = jnp.swapaxes(gains_all[:, :2, :shard_gain], 0, 1).reshape(2, width)
    gain_one, gain_two = gains_all[0:1], gains_all[1:2]
    half_width = width // 2
    positions = span * span_rows + jnp.arange(span_rows)
    lives = []
    for m in range(micros):
        live_rows = (positions < lengths[m, 0]).astype(F32)
        lives.append(cotangent[m, 0].astype(F32) * live_rows[:, None])
    for rows in own_rows[1:]:
        all_rows.append(gather_rows(after(rows, all_rows[-1], head_weight)))
    out_half = lax.dynamic_slice_in_dim(out_weight, core * half_width, half_width, 1)
    cots = [live.astype(BF16) for live in lives]
    out_near, cot_all = gather_rest(
        after(out_half, head_weight, all_rows[0]), cots[0], (dp_count, seq_count)
    )
    grads_all = [cot_all]
    for cot in cots[1:]:
        grads_all.append(gather_cot(after(cot, grads_all[-1], all_rows[-1]), dp_count))
    out_far = swap(out_near)

    gate_share = jax.nn.sigmoid(gate_logit)
    gate_here = lax.dynamic_slice_in_dim(gate_share, span * heads_here, heads_here, 0)
    near_at, far_at = core * half_width, (1 - core) * half_width
    low_first = core == 0

    saved = []
    outputs, new_memories, new_norms = [], [], []
    for m in range(micros):
        hidden_one, projected = project(
            after(all_rows[m], all_rows[-1], grads_all[-1]),
            gain_one,
            head_weight,
        )
        if m == 0:
            near_units, near_downs = (
                lax.dynamic_slice_in_dim(w, core * inner_half, inner_half, 0)
                for w in (inner_weight, down_weight)
            )
        memory_here = lax.dynamic_slice_in_dim(memory[m, 0], span * heads_here, heads_here, 0)
        norm_here = lax.dynamic_slice_in_dim(
            normalizer[m, 0], span * heads_here, heads_here, 0
        ).reshape(heads_here, 1, head_dim)
        length = lengths[m]
        mixed_heads, dot_read, lse, new_memory, new_norm = attend(
            length, gate_here, projected, memory_here, norm_here
        )
        if m == 0:
            inner_near = lax.all_gather(
                after(near_units, all_rows[-1], out_near),
                "seq",
                axis=0,
                tiled=True,
            )
        new_memories.append(new_memory)
        new_norms.append(new_norm.reshape(heads_here, head_dim))
        mixed = lax.all_to_all(
            mixed_heads.reshape(span_count, span_rows, block_rows),
            ("rep", "seq"),
            0,
            0,
            tiled=True,
        )
        mixed = jnp.swapaxes(mixed, 0, 1).reshape(span_rows, width)
        mixed_near = lax.dynamic_slice_in_dim(mixed, near_at, half_width, 1)
        mixed_far = lax.dynamic_slice_in_dim(mixed, far_at, half_width, 1)
        after_attn = (
            own_rows[m].astype(F32)
            + nt(mixed_near, out_near)
            + nt(mixed_far, out_far)
        )
        scale_two = lax.rsqrt(jnp.mean(after_attn * after_attn, axis=-1, keepdims=True) + EPSILON)
        normed_two = after_attn * scale_two
        hidden_two = (normed_two * gain_two).astype(BF16)
        if m + 1 == micros:
            hidden_two = after(hidden_two, inner_near)
        rows_all = cube_gather(hidden_two, "dp")
        saved.append(
            dict(
                hidden_one=hidden_one,
                projected=projected,
                live=lives[m],
                grads=grads_all[m],
                memory=memory_here,
                norm=norm_here,
                length=length,
                dot_read=dot_read,
                lse=lse,
                mixed_heads=mixed_heads,
                mixed_near=mixed_near,
                mixed_far=mixed_far,
                after_attn=after_attn,
                scale_two=scale_two,
                normed_two=normed_two,
                rows=rows_all,
            )
        )

    down_near = after(
        lax.all_gather(near_downs, "seq", axis=0, tiled=True), *[s["rows"] for s in saved]
    )
    inner_far, down_far = swap(inner_near), swap(down_near)

    inner, down = (inner_near, inner_far), (down_near, down_far)
    last = None
    for s in saved:
        halves = []
        for half in range(2):
            halves.append(unit_pass(after(s["rows"], last), s["grads"], inner[half], down[half]))
            last = halves[-1][0]
        s["hidden"], s["grad_gates"], s["grad_ups"] = zip(*halves)

    def half_grads(left, right, half, extra, *earlier):
        pairs = [(s[left][half], s[right]) for s in saved]
        pairs[0] = (after(pairs[0][0], *earlier), pairs[0][1])
        return weight_pass(pairs, extra)

    def spread(values):
        return lax.psum_scatter(values, "seq", scatter_dimension=0, tiled=True)

    def rows_out(s, *earlier):
        gates = (after(s["grad_gates"][0], *earlier), s["grad_gates"][1])
        s["mlp_part"], s["grad_two"] = row_pass(
            s["hidden"], gates, s["grad_ups"], inner, down, dp_count
        )
        return s["grad_two"]

    down_far_sum = half_grads("hidden", "grads", 1, None, last)
    gate_far_sum = half_grads("grad_gates", "rows", 1, None, down_far_sum)
    down_sum = half_grads("hidden", "grads", 0, swap(down_far_sum), gate_far_sum)
    down_mine = spread(down_sum)
    last = rows_out(saved[0], down_sum)
    up_far_sum = half_grads("grad_ups", "rows", 1, None, last)
    gate_sum = half_grads("grad_gates", "rows", 0, swap(gate_far_sum), up_far_sum)
    gate_mine = spread(gate_sum)
    def rows_back(s):
        grad_two = s["grad_two"]
        grad_scaled = grad_two * gain_two
        normed_two = s["normed_two"]
        s["grad_after"] = s["live"] + s["scale_two"] * (
            grad_scaled
            - normed_two * jnp.mean(grad_scaled * normed_two, axis=-1, keepdims=True)
        )
        s["grad_branch"] = s["grad_after"].astype(BF16)
        s["gains_two"] = jnp.sum(grad_two * normed_two, axis=0)
        grad_mixed_near = nn(s["grad_branch"], out_near).astype(BF16)
        grad_mixed_far = nn(s["grad_branch"], out_far).astype(BF16)
        grad_mixed = jnp.concatenate(
            [
                jnp.where(low_first, grad_mixed_near, grad_mixed_far),
                jnp.where(low_first, grad_mixed_far, grad_mixed_near),
            ],
            axis=1,
        )
        s["grad_mixed"] = jnp.swapaxes(
            grad_mixed.reshape(span_rows, span_count, block_rows), 0, 1
        )
        return lax.all_to_all(s["grad_mixed"], ("rep", "seq"), 0, 0, tiled=True).reshape(
            total, block_rows
        )

    def heads_back(s, m, grad_heads):
        s["grad_projected"], gate_sums = attend_back(
            s["length"],
            gate_here,
            s["projected"],
            s["memory"],
            s["norm"],
            s["dot_read"],
            s["lse"],
            grad_heads,
        )
        s["gate"] = jnp.sum(gate_sums, axis=(1, 2))
        part_far, gains_far = project_back(
            1 - core, s["grad_projected"], head_weight, all_rows[m]
        )
        part_near, gains_near = project_back(
            core, s["grad_projected"], head_weight, all_rows[m], swap(part_far)
        )
        s["gains_one"] = (gains_far + gains_near)[0]
        return part_near

    def tokens_back(s, m, grad_one):
        rows_float = own_rows[m].astype(F32)
        scale_one = lax.rsqrt(jnp.mean(rows_float * rows_float, axis=-1, keepdims=True) + EPSILON)
        normed_one = rows_float * scale_one
        grad_scaled = grad_one * gain_one
        return (
            s["grad_after"]
            + scale_one
            * (
                grad_scaled
                - normed_one * jnp.mean(grad_scaled * normed_one, axis=-1, keepdims=True)
            )
        ).astype(BF16)

    heads_grads = [rows_back(saved[0])]
    last = gate_sum
    for m, s in enumerate(saved[1:]):
        last = rows_out(s, last, down_mine)
        heads_grads.append(rows_back(s))

    def spread_out(s, *earlier):
        return lax.psum_scatter(
            after(s["mlp_part"], *earlier), "dp", scatter_dimension=0, tiled=True
        )

    mlp_outs, sums = [spread_out(saved[0], saved[-1]["grad_branch"])], []
    earlier = (saved[-1]["grad_mixed"], gate_mine)
    for m, s in enumerate(saved):
        sums.append(heads_back(s, m, after(heads_grads[m], *earlier)))
        if m == 0:
            up_sum = half_grads(
                "grad_ups", "rows", 0, swap(up_far_sum), s["grad_projected"], heads_grads[-1]
            )
            up_mine = spread(up_sum)
            earlier = (up_sum, mlp_outs[0])
        else:
            mlp_outs.append(spread_out(s, up_sum))
    out_far_sum = weight_pass([(s["grad_branch"], s["mixed_far"]) for s in saved])
    out_sum = weight_pass(
        [(s["grad_branch"], s["mixed_near"]) for s in saved], swap(out_far_sum)
    )
    qkv_low = weight_pass([(s["grad_projected"], s["hidden_one"]) for s in saved]).reshape(
        3, block_rows, width
    )

    grad_ones, qkv_done, out_done = spread_sums(
        [after(p, up_mine, mlp_outs[0]).reshape(seq_count, span_rows, width) for p in sums],
        qkv_low,
        out_sum.reshape(dp_count, seq_count, shard_out, half_width),
        (dp_count, seq_count, unit, per_shard, per_block, per_column),
    )
    grad_tokens = [tokens_back(s, m, grad_ones[m]) for m, s in enumerate(saved)]
    grad_qkv = qkv_done.astype(F32)
    grad_out = jnp.swapaxes(out_done, 0, 1).reshape(shard_out, width).astype(F32)
    for s, mlp_out in zip(saved, mlp_outs):
        outputs.append((s["after_attn"] + mlp_out.astype(F32)).astype(BF16))

    def joined(name):
        return functools.reduce(jnp.add, [s[name] for s in saved])

    def both_cores(mine, axis):
        other = swap(mine)
        size = mine.shape[axis]
        shape = list(mine.shape)
        shape[axis] = 2 * size
        whole = jnp.zeros(shape, F32)
        whole = lax.dynamic_update_slice_in_dim(whole, mine.astype(F32), core * size, axis)
        return lax.dynamic_update_slice_in_dim(
            whole, other.astype(F32), (1 - core) * size, axis
        )

    grad_down = both_cores(down_mine, 0)
    grad_inner = both_cores(jnp.concatenate([gate_mine, up_mine], axis=1), 0)

    gate_terms = joined("gate") * gate_here * (1.0 - gate_here)
    gate_row = lax.dynamic_update_slice_in_dim(
        jnp.zeros((head_count,), F32), gate_terms, span * heads_here, 0
    )
    small = jnp.concatenate([joined("gains_one"), joined("gains_two"), gate_row])
    small = jnp.pad(small, (0, 8 * width - small.shape[0])).reshape(8, width)
    small = lax.all_gather(after(small, up_mine), ALL, axis=0, tiled=True)
    small = jnp.sum(small.reshape(devices, 8 * width)[:, : 3 * width], axis=0)
    gain_at = (column * seq_count + place) * shard_gain
    grad_gains = lax.dynamic_slice_in_dim(
        small[: 2 * width].reshape(2, width), gain_at, shard_gain, 1
    )
    grad_gate = small[2 * width : 2 * width + head_count]
    return (
        jnp.stack(outputs)[:, None],
        jnp.stack(new_memories)[:, None],
        jnp.stack(new_norms)[:, None],
        jnp.stack(grad_tokens)[:, None],
        grad_qkv,
        grad_out,
        grad_gains,
        grad_gate,
        grad_inner,
        grad_down,
    )


def solution(mesh):
    placed = (
        P(None, "dp", ("rep", "seq"), None),
        P(None, "dp"),
        P(None, "dp", None, None, None),
        P(None, "dp", None, None),
        P(("dp", "seq"), None),
        P(("dp", "seq"), None),
        P(None, ("dp", "seq")),
        P(),
        P(("dp", "seq"), None),
        P(("dp", "seq"), None),
        P(None, "dp", ("rep", "seq"), None),
    )
    return jax.shard_map(
        shards,
        mesh=mesh,
        in_specs=placed,
        out_specs=(
            P(None, "dp", ("rep", "seq"), None),
            P(None, "dp", ("rep", "seq"), None, None),
            P(None, "dp", ("rep", "seq"), None),
            P(None, "dp", ("rep", "seq"), None),
            P(("dp", "seq"), None),
            P(("dp", "seq"), None),
            P(None, ("dp", "seq")),
            P(),
            P(("dp", "seq"), None),
            P(("dp", "seq"), None),
        ),
        check_vma=False,
    )
```

```python
import functools
import math

import jax
import jax.numpy as jnp
from jax import lax
from jax.experimental import pallas as pl
from jax.experimental.pallas import tpu as pltpu
from jax.sharding import PartitionSpec as P

EPSILON = 1e-05
LOG2E = 1.4426950408889634
NEG = -1e30
F32 = jnp.float32
BF16 = jnp.bfloat16
ALL = ("rep", "dp", "seq")


def nt(left_side, right_side):
    return lax.dot_general(
        left_side, right_side, (((1,), (1,)), ((), ())), preferred_element_type=F32
    )


def nn(left_side, right_side):
    return lax.dot_general(
        left_side, right_side, (((1,), (0,)), ((), ())), preferred_element_type=F32
    )


def tn(left_side, right_side):
    return lax.dot_general(
        left_side, right_side, (((0,), (0,)), ((), ())), preferred_element_type=F32
    )


def elu_one(values):
    return jnp.where(values > 0.0, values + 1.0, jnp.exp(jnp.minimum(values, 0.0)))


def project_kernel(rows_ref, gain_ref, weight_ref, hidden_ref, projected_ref):
    rows = rows_ref[...].astype(F32)
    scale = lax.rsqrt(jnp.mean(rows * rows, axis=-1, keepdims=True) + EPSILON)
    hidden = (rows * scale * gain_ref[...]).astype(BF16)
    hidden_ref[...] = hidden
    projected_ref[...] = nt(hidden, weight_ref[...]).astype(BF16)


def project(rows, gain, weight):
    count, width = rows.shape
    outs = weight.shape[0]
    block = min(256, count)
    return pl.pallas_call(
        project_kernel,
        grid=(count // block,),
        in_specs=[
            pl.BlockSpec((block, width), lambda i: (i, 0)),
            pl.BlockSpec((1, width), lambda i: (0, 0)),
            pl.BlockSpec((outs, width), lambda i: (0, 0)),
        ],
        out_specs=[
            pl.BlockSpec((block, width), lambda i: (i, 0)),
            pl.BlockSpec((block, outs), lambda i: (i, 0)),
        ],
        out_shape=[
            jax.ShapeDtypeStruct((count, width), BF16),
            jax.ShapeDtypeStruct((count, outs), BF16),
        ],
        compiler_params=pltpu.CompilerParams(vmem_limit_bytes=32 << 20),
        cost_estimate=pl.CostEstimate(
            flops=2 * count * width * outs,
            bytes_accessed=4 * count * width + 2 * outs * (width + count),
            transcendentals=count,
        ),
        name="project",
    )(rows, gain, weight)


def attend_kernel(
    block,
    length_ref,
    gate_ref,
    q_ref,
    k_ref,
    v_ref,
    mem_ref,
    norm_ref,
    mixed_ref,
    dot_ref,
    lse_ref,
    new_mem_ref,
    new_norm_ref,
    v_turned,
):
    head, step = pl.program_id(0), pl.program_id(1)
    length = length_ref[0]
    total, width = k_ref.shape
    memory = mem_ref[0]
    norm_row = norm_ref[0]
    memory_low = memory.astype(BF16)

    @pl.when(step == 0)
    def _():
        v_turned[...] = v_ref[...].T
        key_sig = elu_one(k_ref[...].astype(F32))
        below = jnp.sum(key_sig * norm_row, axis=-1, keepdims=True)
        recalled = nn(key_sig.astype(BF16), memory_low) / below
        change = v_ref[...].astype(F32) - recalled
        live = lax.broadcasted_iota(jnp.int32, (total, width), 0) < length
        kept = jnp.where(live, key_sig, 0.0)
        new_mem_ref[0] = memory + tn(kept.astype(BF16), change.astype(BF16))
        new_norm_ref[0] = norm_row + jnp.sum(kept, axis=0, keepdims=True)

    queries = q_ref[...]
    factor = LOG2E * width ** (-0.5)

    def visit(at, carry, masked):
        high, mass, acc = carry
        start = pl.multiple_of(at * block, block)
        scores = nt(k_ref[pl.ds(start, block), :], queries) * factor
        if masked:
            key_at = start + lax.broadcasted_iota(jnp.int32, (block, block), 0)
            query_at = step * block + lax.broadcasted_iota(jnp.int32, (block, block), 1)
            scores = jnp.where((key_at <= query_at) & (key_at < length), scores, NEG)
        higher = jnp.maximum(high, jnp.max(scores, axis=0, keepdims=True))
        weights = jnp.exp2(scores - higher)
        shrink = jnp.exp2(high - higher)
        mass = mass * shrink + jnp.sum(weights, axis=0, keepdims=True)
        acc = acc * shrink + nn(v_turned[:, pl.ds(start, block)], weights.astype(BF16))
        return higher, mass, acc

    full = jnp.minimum(step, length // block)
    end = jnp.minimum(step + 1, (length + block - 1) // block)
    carry = (
        jnp.full((1, block), NEG, F32),
        jnp.zeros((1, block), F32),
        jnp.zeros((width, block), F32),
    )
    carry = lax.fori_loop(0, full, functools.partial(visit, masked=False), carry)
    high, mass, acc = lax.fori_loop(full, end, functools.partial(visit, masked=True), carry)
    dot_read = (acc / mass).T
    query_sig = elu_one(queries.astype(F32))
    below = jnp.sum(query_sig * norm_row, axis=-1, keepdims=True)
    mem_read = nn(query_sig.astype(BF16), memory_low) / below
    gate = gate_ref[head]
    mixed_ref[...] = (gate * mem_read + (1.0 - gate) * dot_read).astype(BF16)
    dot_ref[...] = dot_read
    lse_ref[0] = high + jnp.log2(mass)


def attend(length, gate, projected, memory, normalizer):
    total = projected.shape[0]
    heads, width = normalizer.shape[0], normalizer.shape[2]
    block = min(512, total)
    smem = pl.BlockSpec(memory_space=pltpu.SMEM)
    return pl.pallas_call(
        functools.partial(attend_kernel, block),
        grid=(heads, total // block),
        in_specs=[
            smem,
            smem,
            pl.BlockSpec((block, width), lambda h, i: (i, h)),
            pl.BlockSpec((total, width), lambda h, i: (0, heads + h)),
            pl.BlockSpec((total, width), lambda h, i: (0, 2 * heads + h)),
            pl.BlockSpec((1, width, width), lambda h, i: (h, 0, 0)),
            pl.BlockSpec((1, 1, width), lambda h, i: (h, 0, 0)),
        ],
        out_specs=[
            pl.BlockSpec((block, width), lambda h, i: (i, h)),
            pl.BlockSpec((block, width), lambda h, i: (i, h)),
            pl.BlockSpec((1, 1, block), lambda h, i: (h, 0, i)),
            pl.BlockSpec((1, width, width), lambda h, i: (h, 0, 0)),
            pl.BlockSpec((1, 1, width), lambda h, i: (h, 0, 0)),
        ],
        out_shape=[
            jax.ShapeDtypeStruct((total, heads * width), BF16),
            jax.ShapeDtypeStruct((total, heads * width), F32),
            jax.ShapeDtypeStruct((heads, 1, total), F32),
            jax.ShapeDtypeStruct((heads, width, width), F32),
            jax.ShapeDtypeStruct((heads, 1, width), F32),
        ],
        scratch_shapes=[pltpu.VMEM((width, total), BF16)],
        compiler_params=pltpu.CompilerParams(vmem_limit_bytes=40 << 20),
        cost_estimate=pl.CostEstimate(
            flops=4 * heads * total * total * width,
            bytes_accessed=heads * total * width * 12,
            transcendentals=heads * total * total,
        ),
        name="attend",
    )(length, gate, projected, projected, projected, memory, normalizer)


def attend_back_kernel(
    block,
    length_ref,
    gate_ref,
    q_ref,
    k_ref,
    v_ref,
    mem_ref,
    norm_ref,
    dot_ref,
    lse_ref,
    grad_ref,
    out_ref,
    gate_sum_ref,
    k_turned,
    k_sum,
    v_sum,
):
    head, step = pl.program_id(0), pl.program_id(1)
    heads, steps = pl.num_programs(0), pl.num_programs(1)
    length = length_ref[0]
    total, width = k_ref.shape
    gate = gate_ref[head]

    @pl.when(step == 0)
    def _():
        k_turned[...] = k_ref[...].T
        k_sum[...] = jnp.zeros_like(k_sum)
        v_sum[...] = jnp.zeros_like(v_sum)
        gate_sum_ref[...] = jnp.zeros_like(gate_sum_ref)

    queries = q_ref[...]
    query_float = queries.astype(F32)
    grad_mixed = grad_ref[...].astype(F32)
    grad_dot = ((1.0 - gate) * grad_mixed).astype(BF16)
    dot_read = dot_ref[...]
    offset = jnp.sum((grad_dot.astype(F32) * dot_read).T, axis=0, keepdims=True)
    lse = lse_ref[0]
    scale = width ** (-0.5)
    factor = LOG2E * scale

    def visit(at, acc, masked):
        start = pl.multiple_of(at * block, block)
        here = pl.ds(start, block)
        scores = nt(k_ref[here, :], queries) * factor
        weights = jnp.exp2(scores - lse)
        if masked:
            key_at = start + lax.broadcasted_iota(jnp.int32, (block, block), 0)
            query_at = step * block + lax.broadcasted_iota(jnp.int32, (block, block), 1)
            weights = jnp.where((key_at <= query_at) & (key_at < length), weights, 0.0)
        grad_probs = nt(v_ref[here, :], grad_dot)
        grad_scores = (weights * (grad_probs - offset) * scale).astype(BF16)
        v_sum[here, :] += nn(weights.astype(BF16), grad_dot)
        k_sum[here, :] += nn(grad_scores, queries)
        return acc + nn(k_turned[:, here], grad_scores)

    full = jnp.minimum(step, length // block)
    end = jnp.minimum(step + 1, (length + block - 1) // block)
    acc = jnp.zeros((width, block), F32)
    acc = lax.fori_loop(0, full, functools.partial(visit, masked=False), acc)
    acc = lax.fori_loop(full, end, functools.partial(visit, masked=True), acc)

    memory_low = mem_ref[0].astype(BF16)
    norm_row = norm_ref[0]
    query_sig = elu_one(query_float)
    below = jnp.sum(query_sig * norm_row, axis=-1, keepdims=True)
    numerator = nn(query_sig.astype(BF16), memory_low)
    inverse = 1.0 / below
    grad_read = gate * grad_mixed
    grad_below = -jnp.sum(grad_read * numerator, axis=-1, keepdims=True) * inverse * inverse
    grad_sig = nt((grad_read * inverse).astype(BF16), memory_low) + grad_below * norm_row
    slope = jnp.where(query_float > 0.0, 1.0, jnp.exp(jnp.minimum(query_float, 0.0)))
    rows = pl.ds(pl.multiple_of(step * block, block), block)
    out_ref[rows, pl.ds(pl.multiple_of(head * width, width), width)] = (
        acc.T + grad_sig * slope
    ).astype(BF16)
    gate_sum_ref[0] += jnp.sum(
        grad_mixed * (numerator * inverse - dot_read), axis=0, keepdims=True
    )

    @pl.when(step == steps - 1)
    def _():
        k_at = pl.multiple_of((heads + head) * width, width)
        v_at = pl.multiple_of((2 * heads + head) * width, width)
        out_ref[:, pl.ds(k_at, width)] = k_sum[...].astype(BF16)
        out_ref[:, pl.ds(v_at, width)] = v_sum[...].astype(BF16)


def attend_back(length, gate, projected, memory, normalizer, dot_read, lse, grad_mixed):
    total = projected.shape[0]
    heads, width = normalizer.shape[0], normalizer.shape[2]
    block = min(512, total)
    smem = pl.BlockSpec(memory_space=pltpu.SMEM)
    return pl.pallas_call(
        functools.partial(attend_back_kernel, block),
        grid=(heads, total // block),
        in_specs=[
            smem,
            smem,
            pl.BlockSpec((block, width), lambda h, i: (i, h)),
            pl.BlockSpec((total, width), lambda h, i: (0, heads + h)),
            pl.BlockSpec((total, width), lambda h, i: (0, 2 * heads + h)),
            pl.BlockSpec((1, width, width), lambda h, i: (h, 0, 0)),
            pl.BlockSpec((1, 1, width), lambda h, i: (h, 0, 0)),
            pl.BlockSpec((block, width), lambda h, i: (i, h)),
            pl.BlockSpec((1, 1, block), lambda h, i: (h, 0, i)),
            pl.BlockSpec((block, width), lambda h, i: (i, h)),
        ],
        out_specs=[
            pl.BlockSpec((total, 3 * heads * width), lambda h, i: (0, 0)),
            pl.BlockSpec((1, 1, width), lambda h, i: (h, 0, 0)),
        ],
        out_shape=[
            jax.ShapeDtypeStruct((total, 3 * heads * width), BF16),
            jax.ShapeDtypeStruct((heads, 1, width), F32),
        ],
        scratch_shapes=[
            pltpu.VMEM((width, total), BF16),
            pltpu.VMEM((total, width), F32),
            pltpu.VMEM((total, width), F32),
        ],
        compiler_params=pltpu.CompilerParams(vmem_limit_bytes=40 << 20),
        cost_estimate=pl.CostEstimate(
            flops=10 * heads * total * total * width,
            bytes_accessed=heads * total * width * 20,
            transcendentals=heads * total * total,
        ),
        name="attend_back",
    )(length, gate, projected, projected, projected, memory, normalizer, dot_read, lse, grad_mixed)


def unit_kernel(
    rows_ref, grad_ref, inner_ref, down_ref, hidden_ref, grad_gate_ref, grad_up_ref
):
    width = rows_ref.shape[1]
    rows = rows_ref[...]
    gates = nt(rows, inner_ref[:, :width])
    ups = nt(rows, inner_ref[:, width:])
    grad_hidden = nt(grad_ref[...], down_ref[...])
    sigmoid = 1.0 / (1.0 + jnp.exp(-gates))
    silu = gates * sigmoid
    hidden_ref[...] = (silu * ups).astype(BF16)
    grad_gate_ref[...] = (
        grad_hidden * ups * (sigmoid * (1.0 + gates * (1.0 - sigmoid)))
    ).astype(BF16)
    grad_up_ref[...] = (grad_hidden * silu).astype(BF16)


def unit_pass(rows, grads, inner, down):
    count, width = rows.shape
    units = inner.shape[0]
    tile = min(256, units)
    resident = pl.BlockSpec((count, width), lambda t: (0, 0), pipeline_mode=pl.Buffered(1))
    column = pl.BlockSpec((count, tile), lambda t: (0, t))
    unit_shape = jax.ShapeDtypeStruct((count, units), BF16)
    return pl.pallas_call(
        unit_kernel,
        grid=(units // tile,),
        in_specs=[
            resident,
            resident,
            pl.BlockSpec((tile, 2 * width), lambda t: (t, 0)),
            pl.BlockSpec((tile, width), lambda t: (t, 0)),
        ],
        out_specs=[column] * 3,
        out_shape=[unit_shape] * 3,
        compiler_params=pltpu.CompilerParams(vmem_limit_bytes=56 << 20),
        cost_estimate=pl.CostEstimate(
            flops=2 * 3 * count * width * units,
            bytes_accessed=units * (6 * width + 6 * count) + 4 * count * width,
            transcendentals=count * units,
        ),
        name="unit_pass",
    )(rows, grads, inner, down)


def weight_kernel(pairs, *refs):
    out_ref = refs[-1]
    total = tn(refs[0][...], refs[1][...])
    for at in range(1, pairs):
        total += tn(refs[2 * at][...], refs[2 * at + 1][...])
    if len(refs) > 2 * pairs + 1:
        total += refs[2 * pairs][...].astype(F32)
    out_ref[...] = total.astype(BF16)


def weight_pass(pairs, extra=None):
    size, width = pairs[0][0].shape[1], pairs[0][1].shape[1]
    tile = min(256, size)
    in_specs, operands, flops, moved = [], [], 0, 2 * size * width
    for left, right in pairs:
        count = left.shape[0]
        in_specs.append(pl.BlockSpec((count, tile), lambda t: (0, t)))
        in_specs.append(
            pl.BlockSpec((count, width), lambda t: (0, 0), pipeline_mode=pl.Buffered(1))
        )
        operands += [left, right]
        flops += 2 * count * size * width
        moved += 2 * count * (size + width)
    if extra is not None:
        in_specs.append(pl.BlockSpec((tile, width), lambda t: (t, 0)))
        operands.append(extra)
        moved += 2 * size * width
    return pl.pallas_call(
        functools.partial(weight_kernel, len(pairs)),
        grid=(size // tile,),
        in_specs=in_specs,
        out_specs=pl.BlockSpec((tile, width), lambda t: (t, 0)),
        out_shape=jax.ShapeDtypeStruct((size, width), BF16),
        compiler_params=pltpu.CompilerParams(vmem_limit_bytes=56 << 20),
        cost_estimate=pl.CostEstimate(flops=flops, bytes_accessed=moved, transcendentals=0),
        name="weight_pass",
    )(*operands)


def back_kernel(half_ref, grad_ref, weight_ref, rows_ref, *refs):
    out_ref, gain_ref = refs[-2:]

    @pl.when(pl.program_id(0) == 0)
    def _():
        gain_ref[...] = jnp.zeros_like(gain_ref)

    part = nn(grad_ref[...], weight_ref[...])
    total = part + refs[0][...].astype(F32) if len(refs) > 2 else part
    out_ref[...] = total.astype(BF16)
    rows = rows_ref[...].astype(F32)
    scale = lax.rsqrt(jnp.mean(rows * rows, axis=-1, keepdims=True) + EPSILON)
    gain_ref[...] += jnp.sum(part * (rows * scale), axis=0, keepdims=True)


def project_back(half, grads, weight, rows, extra=None):
    count, outs = grads.shape[0] // 2, grads.shape[1]
    width = weight.shape[1]
    block = min(256, count)
    steps = count // block
    return pl.pallas_call(
        back_kernel,
        grid_spec=pltpu.PrefetchScalarGridSpec(
            num_scalar_prefetch=1,
            grid=(steps,),
            in_specs=[
                pl.BlockSpec((block, outs), lambda i, at: (at[0] * steps + i, 0)),
                pl.BlockSpec((outs, width), lambda i, at: (0, 0)),
                pl.BlockSpec((block, width), lambda i, at: (at[0] * steps + i, 0)),
            ]
            + [pl.BlockSpec((block, width), lambda i, at: (i, 0))] * (extra is not None),
            out_specs=[
                pl.BlockSpec((block, width), lambda i, at: (i, 0)),
                pl.BlockSpec((1, width), lambda i, at: (0, 0)),
            ],
        ),
        out_shape=[
            jax.ShapeDtypeStruct((count, width), BF16),
            jax.ShapeDtypeStruct((1, width), F32),
        ],
        compiler_params=pltpu.CompilerParams(vmem_limit_bytes=40 << 20),
        cost_estimate=pl.CostEstimate(
            flops=2 * count * width * outs,
            bytes_accessed=4 * count * width + 2 * outs * (width + count),
            transcendentals=count,
        ),
        name="project_back",
    )(
        jnp.reshape(half, (1,)).astype(jnp.int32),
        grads,
        weight,
        rows,
        *([] if extra is None else [extra]),
    )


def swap(values):
    return lax.ppermute(values, "rep", [(0, 1), (1, 0)])


def after(values, *earlier):
    earlier = [e for e in earlier if e is not None]
    return lax.optimization_barrier((values, *earlier))[0] if earlier else values


def add_low(left_side, right_side):
    return (left_side.astype(F32) + right_side.astype(F32)).astype(BF16)


def line_gather(values, axis):
    count = lax.axis_size(axis)
    here = lax.axis_index(axis)
    rows = values.shape[0]
    table = jnp.zeros(((3 * count - 2) * rows,) + values.shape[1:], values.dtype)

    def put(table, piece, origin):
        return lax.dynamic_update_slice_in_dim(table, piece, (origin + count - 1) * rows, 0)

    table = put(table, values, here)
    rising = falling = values
    for hop in range(1, count):
        rising = lax.ppermute(
            rising, axis, [(a, a + 1) for a in range(count - 1) if a >= hop - 1]
        )
        falling = lax.ppermute(
            falling, axis, [(a, a - 1) for a in range(1, count) if a + hop - 1 < count]
        )
        table = put(table, rising, here - hop)
        table = put(table, falling, here + hop)
    return table[(count - 1) * rows : (2 * count - 1) * rows]


def line_scatter(values, axis, pins=()):
    count = lax.axis_size(axis)
    here = lax.axis_index(axis)
    rows = values.shape[0] // count

    def block(owner):
        start = jnp.clip(owner, 0, count - 1) * rows
        return lax.dynamic_slice_in_dim(values, start, rows, 0).astype(F32)

    rising = falling = None
    for hop in range(1, count):
        reach = count - hop
        up, down = block(here + reach), block(here - reach)
        if rising is not None:
            up, down = up + rising.astype(F32), down + falling.astype(F32)
        rising = lax.ppermute(
            up.astype(BF16), axis, [(a, a + 1) for a in range(count) if a + reach < count]
        )
        falling = lax.ppermute(
            down.astype(BF16), axis, [(a, a - 1) for a in range(count) if a - reach >= 0]
        )
        if hop <= len(pins):
            rising, falling = after(rising, pins[hop - 1]), after(falling, pins[hop - 1])
    return block(here) + rising.astype(F32) + falling.astype(F32)


def cube_bits(count):
    bits = [1 << b for b in range(count.bit_length() - 1)]
    return bits, bits[::-1]


def cube_order(bits):
    order = [0]
    for bit in reversed(bits):
        order = order + [k | bit for k in order]
    return order


def cube_gather(values, axis):
    count = lax.axis_size(axis)
    half = values.shape[0] // 2
    parts = []
    for bits, start in zip(cube_bits(count), (0, half)):
        held = {0: values[start : start + half]}
        for bit in bits:
            pairs = [(a, a ^ bit) for a in range(count)]
            held.update({k ^ bit: lax.ppermute(v, axis, pairs) for k, v in list(held.items())})
        parts += [held[k] for k in cube_order(bits)]
    return jnp.concatenate(parts, axis=0)


def cube_scatter(values, axis, pins=()):
    count = lax.axis_size(axis)
    half = values.shape[0] // 2
    parts = []
    for bits, start in zip(cube_bits(count), (0, half)):
        held = values[start : start + half]
        for at, bit in enumerate(bits):
            pairs = [(a, a ^ bit) for a in range(count)]
            keep = held.shape[0] // 2
            got = lax.ppermute(held[keep:].astype(BF16), axis, pairs)
            if at < len(pins):
                got = after(got, pins[at])
            held = held[:keep].astype(F32) + got.astype(F32)
        parts.append(held)
    return jnp.concatenate(parts, axis=0)


def remote(source, target, sent, landed, device):
    return pltpu.make_async_remote_copy(
        src_ref=source,
        dst_ref=target,
        send_sem=sent,
        recv_sem=landed,
        device_id=device,
        device_id_type=pl.DeviceIdType.MESH,
    )


def greet(devices):
    barrier = pltpu.get_barrier_semaphore()
    for device in devices:
        pl.semaphore_signal(barrier, inc=1, device_id=device, device_id_type=pl.DeviceIdType.MESH)
    pl.semaphore_wait(barrier, len(devices))


def heads_kernel(
    sizes,
    qkv_ref,
    gain_ref,
    head_ref,
    gains_ref,
    landed,
    unit_sent,
    unit_here,
    block_sent,
    block_here,
    line_sent,
    line_here,
    cube_sent,
    cube_here,
    local,
):
    dp_count, seq_count, unit, per_shard, per_block, per_column = sizes
    span_count = 2 * seq_count
    block_rows = unit * per_block
    core, column, place = lax.axis_index("rep"), lax.axis_index("dp"), lax.axis_index("seq")
    span, shard = core * seq_count + place, column * seq_count + place
    line = [(core, column, (place + k) % seq_count) for k in range(1, seq_count)]
    cube = [(core, (column + k) % dp_count, place) for k in range(1, dp_count)]
    greet(line + cube)

    gains = []
    for k, device in enumerate(line):
        gains.append(
            remote(gain_ref, gains_ref.at[shard], line_sent.at[k], line_here.at[k], device)
        )
    for copy in gains:
        copy.start()
    own_gain = pltpu.make_async_copy(gain_ref, gains_ref.at[shard], local.at[0])
    own_gain.start()

    def rows(ref, at, size):
        return ref.at[pl.ds(pl.multiple_of(at * size, size), size)]

    def unit_copy(i):
        number = shard * per_shard + i
        owner = (number // per_block) % span_count
        source, target = rows(qkv_ref, i, unit), rows(landed, number % per_block, unit)
        far = remote(
            source,
            target,
            unit_sent.at[i],
            unit_here.at[number % per_block],
            (core, column, owner % seq_count),
        )
        near = pltpu.make_async_copy(source, target, local.at[1 + i])
        mine = owner // seq_count == core
        stays = owner % seq_count == place
        return far, near, mine & jnp.logical_not(stays), mine & stays

    for i in range(per_shard):
        far, near, leaves, stays = unit_copy(i)
        pl.when(leaves)(far.start)
        pl.when(stays)(near.start)
    for i in range(per_shard):
        _, near, _, stays = unit_copy(i)
        pl.when(stays)(near.wait)

    def block_copies(part):
        target = rows(head_ref, part, block_rows)
        far = [
            remote(landed, target, block_sent.at[k], block_here.at[part], device)
            for k, device in enumerate(cube)
        ]
        return far, pltpu.make_async_copy(landed, target, local.at[0])

    own_gain.wait()
    for part in range(3):
        number = part * span_count + span

        @pl.when(number // per_column == column)
        def _():
            for j in range(per_block):
                source = ((number * per_block + j) // per_shard) % seq_count

                @pl.when(source != place)
                def _():
                    here = rows(landed, j, unit)
                    remote(here, here, unit_sent.at[0], unit_here.at[j], line[0]).wait_recv()

            far, near = block_copies(part)
            for copy in far:
                copy.start()
            near.start()

    for copy in gains:
        copy.wait()
    mine = gains_ref.at[pl.ds(column * seq_count, seq_count)]
    gains = [
        remote(mine, mine, cube_sent.at[k], cube_here.at[k], device)
        for k, device in enumerate(cube)
    ]
    for copy in gains:
        copy.start()
    for part in range(3):
        number = part * span_count + span
        far, near = block_copies(part)

        @pl.when(number // per_column == column)
        def _():
            near.wait()
            for copy in far:
                copy.wait_send()

        @pl.when(number // per_column != column)
        def _():
            far[0].wait_recv()

    for k, copy in enumerate(gains):
        copy.wait_send()
        origin = (column + dp_count - k - 1) % dp_count
        theirs = gains_ref.at[pl.ds(origin * seq_count, seq_count)]
        remote(theirs, theirs, cube_sent.at[k], cube_here.at[k], cube[k]).wait_recv()
    for i in range(per_shard):
        far, _, leaves, _ = unit_copy(i)
        pl.when(leaves)(far.wait_send)


def gather_heads(qkv_weight, gains, sizes):
    dp_count, seq_count, unit, per_shard, per_block, _ = sizes
    width = qkv_weight.shape[1]
    block_rows = unit * per_block
    anywhere = pl.BlockSpec(memory_space=pl.ANY)
    dma = pltpu.SemaphoreType.DMA
    return pl.pallas_call(
        functools.partial(heads_kernel, sizes),
        in_specs=[anywhere, anywhere],
        out_specs=[anywhere, anywhere],
        out_shape=[
            jax.ShapeDtypeStruct((3 * block_rows, width), BF16),
            jax.ShapeDtypeStruct((dp_count * seq_count, *gains.shape), F32),
        ],
        scratch_shapes=[
            pltpu.VMEM((block_rows, width), BF16),
            dma((per_shard,)),
            dma((per_block,)),
            dma((dp_count - 1,)),
            dma((3,)),
            dma((seq_count - 1,)),
            dma((seq_count - 1,)),
            dma((dp_count - 1,)),
            dma((dp_count - 1,)),
            dma((1 + per_shard,)),
        ],
        compiler_params=pltpu.CompilerParams(
            collective_id=0, has_side_effects=True, vmem_limit_bytes=16 << 20
        ),
        cost_estimate=pl.CostEstimate(
            flops=0, bytes_accessed=64 * block_rows * width, transcendentals=0
        ),
        name="gather_heads",
    )(qkv_weight, gains)


def flipped(value, bits):
    bit = 1
    while bit <= bits:
        if bits & bit:
            value = value + bit - 2 * bit * ((value // bit) % 2)
        bit *= 2
    return value


def cot_copies(cot_ref, cot_all, cube, sent, here, local, first):
    count = len(cube) + 1
    half = cot_ref.shape[0] // 2
    stays, leaves = [], []
    for side, bits in enumerate(cube_bits(count)):
        order = cube_order(bits)
        source = cot_ref.at[pl.ds(side * half, half)]
        for k in range(count):
            target = cot_all.at[pl.ds((side * count + order.index(k)) * half, half)]
            if k == 0:
                stays.append(pltpu.make_async_copy(source, target, local.at[first + side]))
            else:
                at = side * (count - 1) + k - 1
                leaves.append(remote(source, target, sent.at[at], here.at[at], cube[k - 1]))
    return stays, leaves


def cot_kernel(count, cot_ref, cot_all, sent, here, local):
    core, column, place = lax.axis_index("rep"), lax.axis_index("dp"), lax.axis_index("seq")
    cube = [(core, flipped(column, k), place) for k in range(1, count)]
    greet(cube)
    stays, leaves = cot_copies(cot_ref, cot_all, cube, sent, here, local, 0)
    for copy in stays + leaves:
        copy.start()
    for copy in stays + leaves:
        copy.wait()


def gather_cot(cot, count):
    rows, width = cot.shape
    anywhere = pl.BlockSpec(memory_space=pl.ANY)
    dma = pltpu.SemaphoreType.DMA
    return pl.pallas_call(
        functools.partial(cot_kernel, count),
        in_specs=[anywhere],
        out_specs=anywhere,
        out_shape=jax.ShapeDtypeStruct((count * rows, width), BF16),
        scratch_shapes=[dma((2 * (count - 1),)), dma((2 * (count - 1),)), dma((2,))],
        compiler_params=pltpu.CompilerParams(collective_id=3, has_side_effects=True),
        cost_estimate=pl.CostEstimate(
            flops=0, bytes_accessed=8 * rows * width, transcendentals=0
        ),
        name="gather_cot",
    )(cot)


def rest_kernel(sizes, *refs):
    dp_count, seq_count = sizes
    out_ref, cot_ref, out_all, cot_all = refs[:4]
    line_sent, line_here, cube_sent, cube_here, cot_sent, cot_here, local = refs[4:]
    core, column, place = lax.axis_index("rep"), lax.axis_index("dp"), lax.axis_index("seq")
    line = [(core, column, (place + k) % seq_count) for k in range(1, seq_count)]
    cube = [(core, flipped(column, k), place) for k in range(1, dp_count)]
    greet(line + cube)
    shard_rows = out_ref.shape[0]
    column_rows = seq_count * shard_rows
    def out_rows(start, size):
        return out_all.at[pl.ds(pl.multiple_of(start, shard_rows), size)]

    mine = out_rows((column * seq_count + place) * shard_rows, shard_rows)
    lines = [
        remote(out_ref, mine, line_sent.at[k], line_here.at[k], device)
        for k, device in enumerate(line)
    ]
    own_out = pltpu.make_async_copy(out_ref, mine, local.at[0])

    own_cots, cots = cot_copies(cot_ref, cot_all, cube, cot_sent, cot_here, local, 1)
    for copy in lines + [own_out] + own_cots + cots:
        copy.start()
    own_out.wait()
    for copy in lines:
        copy.wait()
    mine = out_rows(column * column_rows, column_rows)
    cubes = [
        remote(mine, mine, cube_sent.at[k], cube_here.at[k], device)
        for k, device in enumerate(cube)
    ]
    for copy in cubes:
        copy.start()
    for copy in own_cots + cots:
        copy.wait()
    for k, copy in enumerate(cubes):
        copy.wait_send()
        theirs = out_rows(cube[k][1] * column_rows, column_rows)
        remote(theirs, theirs, cube_sent.at[k], cube_here.at[k], cube[k]).wait_recv()


def gather_rest(out_half, cot, sizes):
    dp_count, seq_count = sizes
    rows, width = cot.shape
    anywhere = pl.BlockSpec(memory_space=pl.ANY)
    dma = pltpu.SemaphoreType.DMA
    return pl.pallas_call(
        functools.partial(rest_kernel, sizes),
        in_specs=[anywhere] * 2,
        out_specs=[anywhere] * 2,
        out_shape=[
            jax.ShapeDtypeStruct(
                (dp_count * seq_count * out_half.shape[0], out_half.shape[1]), BF16
            ),
            jax.ShapeDtypeStruct((dp_count * rows, width), BF16),
        ],
        scratch_shapes=[
            dma((seq_count - 1,)),
            dma((seq_count - 1,)),
            dma((dp_count - 1,)),
            dma((dp_count - 1,)),
            dma((2 * (dp_count - 1),)),
            dma((2 * (dp_count - 1),)),
            dma((3,)),
        ],
        compiler_params=pltpu.CompilerParams(collective_id=2, has_side_effects=True),
        cost_estimate=pl.CostEstimate(
            flops=0, bytes_accessed=8 * rows * width, transcendentals=0
        ),
        name="gather_rest",
    )(out_half, cot)


def row_kernel(count, *refs):
    hidden, gates, ups, gate_w, up_w, down_w = (refs[2 * i : 2 * i + 2] for i in range(6))
    out_ref, grad_ref, parts, sent, here = refs[12:17]
    landed = refs[17:]
    stages = len(landed)
    step, steps = pl.program_id(0), pl.num_programs(0)
    core, column, place = lax.axis_index("rep"), lax.axis_index("dp"), lax.axis_index("seq")
    width = parts.shape[2]
    size = out_ref.shape[0] // (2 * count)

    @pl.when(step == 0)
    def _():
        greet([(core, flipped(column, bit), place) for bit in cube_bits(count)[0]])

    def copy(t, stage, side):
        keep = (count >> (stage + 1)) * size
        flat = (t * stages + stage) * 2 + side
        return remote(
            parts.at[t, pl.ds(side * count * size + keep, keep)],
            landed[stage].at[t, side],
            sent.at[flat],
            here.at[flat],
            (core, flipped(column, cube_bits(count)[side][stage]), place),
        )

    def send(t, stage):
        for side in range(2):
            copy(t, stage, side).start()

    def take(t, stage):
        keep = (count >> (stage + 1)) * size
        for side in range(2):
            copy(t, stage, side).wait()
            rows = pl.ds(side * count * size, keep)
            total = parts[t, rows, :].astype(F32) + landed[stage][t, side].astype(F32)
            if stage + 1 < stages:
                parts[t, rows, :] = total.astype(BF16)
            else:
                columns = pl.ds(pl.multiple_of(t * width, width), width)
                grad_ref[side * size : (side + 1) * size, columns] = total
        if stage + 1 < stages:
            send(t, stage + 1)

    parts[step] = (
        nn(gates[0][...], gate_w[0][...])
        + nn(gates[1][...], gate_w[1][...])
        + nn(ups[0][...], up_w[0][...])
        + nn(ups[1][...], up_w[1][...])
    ).astype(BF16)
    send(step, 0)
    out = (
        nn(hidden[0][...], down_w[0][...]) + nn(hidden[1][...], down_w[1][...])
    ).astype(BF16)
    for side, bits in enumerate(cube_bits(count)):
        for at, k in enumerate(cube_order(bits)):
            owner = flipped(column, k) if k else column
            start = pl.multiple_of((2 * owner + side) * size, size)
            out_ref[pl.ds(start, size), :] = out[(side * count + at) * size :][:size]

    for stage in reversed(range(stages)):

        @pl.when(step >= 2 * (stage + 1))
        def _():
            take(step - 2 * (stage + 1), stage)

    @pl.when(step == steps - 1)
    def _():
        for stage in range(stages):
            for back in reversed(range(2 * (stage + 1))):
                take(steps - 1 - back, stage)


def row_pass(hidden, grad_gates, grad_ups, inner, down, dp_count):
    count, units = hidden[0].shape
    width = down[0].shape[1]
    tile = min(256, width)
    tiles = width // tile
    size = count // (2 * dp_count)
    stages = dp_count.bit_length() - 1
    resident = pl.BlockSpec((count, units), lambda t: (0, 0), pipeline_mode=pl.Buffered(1))
    low = pl.BlockSpec((units, tile), lambda t: (0, t))
    high = pl.BlockSpec((units, tile), lambda t: (0, tiles + t))
    dma = pltpu.SemaphoreType.DMA
    return pl.pallas_call(
        functools.partial(row_kernel, dp_count),
        grid=(tiles,),
        in_specs=[resident] * 6 + [low, low, high, high, low, low],
        out_specs=[
            pl.BlockSpec((count, tile), lambda t: (0, t)),
            pl.BlockSpec((2 * size, width), lambda t: (0, 0)),
        ],
        out_shape=[
            jax.ShapeDtypeStruct((count, width), BF16),
            jax.ShapeDtypeStruct((2 * size, width), F32),
        ],
        scratch_shapes=[
            pltpu.VMEM((tiles, count, tile), BF16),
            dma((tiles * stages * 2,)),
            dma((tiles * stages * 2,)),
        ]
        + [
            pltpu.VMEM((tiles, 2, (dp_count >> (j + 1)) * size, tile), BF16)
            for j in range(stages)
        ],
        compiler_params=pltpu.CompilerParams(
            collective_id=4, has_side_effects=True, vmem_limit_bytes=56 << 20
        ),
        cost_estimate=pl.CostEstimate(
            flops=2 * 3 * count * width * 2 * units,
            bytes_accessed=12 * units * (width + count) + 4 * count * width,
            transcendentals=0,
        ),
        name="row_pass",
    )(*hidden, *grad_gates, *grad_ups, *inner, *inner, *down)


def add_rows(out_ref, refs, size):
    def some(i, _):
        rows = pl.ds(pl.multiple_of(i * size, size), size)
        total = refs[0][rows, :].astype(F32)
        for ref in refs[1:]:
            total += ref[rows, :].astype(F32)
        out_ref[rows, :] = total.astype(out_ref.dtype)
        return 0

    lax.fori_loop(0, out_ref.shape[0] // size, some, 0)


def spread_kernel(
    sizes,
    micros,
    *refs,
):
    spread_body(sizes, refs[:micros], *refs[micros:])


def spread_body(
    sizes,
    line_refs,
    qkv_ref,
    out_ref,
    grad_ref,
    qkv_done,
    out_done,
    rising,
    falling,
    qkv_in,
    qkv_sum,
    out_in,
    out_part,
    out_line,
    rise_sent,
    rise_here,
    fall_sent,
    fall_here,
    qkv_sent,
    qkv_here,
    out_sent,
    out_here,
    unit_sent,
    unit_here,
    line_sent,
    line_here,
    swap_sent,
    swap_here,
    local,
):
    dp_count, seq_count, unit, per_shard, per_block, per_column = sizes
    span_count = 2 * seq_count
    micros = len(line_refs)
    core, column, place = lax.axis_index("rep"), lax.axis_index("dp"), lax.axis_index("seq")
    span = core * seq_count + place
    cube = [(core, (column + k) % dp_count, place) for k in range(1, dp_count)]
    line = [(core, column, (place + k) % seq_count) for k in range(1, seq_count)]
    across = [(1 - core, column, (place + k) % seq_count) for k in range(seq_count)]
    greet(cube + line + across)

    def part_at(part, col):
        return (part * span_count + span) // per_column == col

    def out_copy(k):
        target = cube[k]
        return remote(
            out_ref.at[target[1]], out_in.at[k], out_sent.at[k], out_here.at[k], target
        )

    def qkv_copy(k, part):
        return remote(
            qkv_ref.at[part], qkv_in.at[k], qkv_sent.at[k], qkv_here.at[k], cube[k]
        )

    def hop(number, m, up):
        reach = seq_count - number
        buffer, sent, here = (
            (rising, rise_sent, rise_here) if up else (falling, fall_sent, fall_here)
        )
        behind = place if up else seq_count - 1 - place
        owner = place + reach if up else place - reach
        owner = jnp.clip(owner, 0, seq_count - 1)
        next_place = jnp.clip(place + 1 if up else place - 1, 0, seq_count - 1)
        device = (core, column, next_place)
        at = (number - 1) * micros + m
        target = buffer.at[at]

        def send(source):
            remote(source, target, sent.at[at], here.at[at], device).start()

        own = line_refs[m].at[owner]
        if number == 1:
            pl.when(behind == 0)(lambda: send(own))
            return

        @pl.when(behind == 0)
        def _():
            send(own)

        @pl.when((behind >= 1) & (behind <= number - 1))
        def _():
            before = buffer.at[at - micros]
            remote(before, before, sent.at[0], here.at[at - micros], across[0]).wait_recv()
            add_rows(before, [before, own], 64)
            send(before)

    def hop_sent(number, m, up):
        sent = rise_sent if up else fall_sent
        buffer = rising if up else falling
        behind = place if up else seq_count - 1 - place
        at = (number - 1) * micros + m
        piece = buffer.at[at]

        @pl.when(behind <= number - 1)
        def _():
            remote(piece, piece, sent.at[at], sent.at[at], across[0]).wait_send()

    def hops(number):
        for m in range(micros):
            hop(number, m, True)
            hop(number, m, False)

    hops(1)
    for k in range(dp_count - 1):
        out_copy(k).start()
        for part in range(3):

            @pl.when(part_at(part, cube[k][1]))
            def _():
                qkv_copy(k, part).start()

    hops(2)

    for k in range(dp_count - 1):
        out_copy(k).wait_recv()
    for s in range(seq_count):
        add_rows(
            out_part.at[s],
            [out_ref.at[column, s]] + [out_in.at[k, s] for k in range(dp_count - 1)],
            32,
        )

    def line_copy(k):
        return remote(
            out_part.at[line[k][2]], out_line.at[k], line_sent.at[k], line_here.at[k], line[k]
        )

    for k in range(seq_count - 1):
        line_copy(k).start()

    def unit_copies(part, j):
        number = (part * span_count + span) * per_block + j
        owner = (number // per_shard) % seq_count
        source = qkv_sum.at[pl.ds(j * unit, unit)]
        target = qkv_done.at[pl.ds(pl.multiple_of((number % per_shard) * unit, unit), unit)]
        here = unit_here.at[number % per_shard]
        other = remote(
            source, target, unit_sent.at[2 * j], here, (1 - core, column, owner)
        )
        same = remote(source, target, unit_sent.at[2 * j + 1], here, (core, column, owner))
        stays = pltpu.make_async_copy(source, target, local.at[j])
        return owner, other, same, stays

    for part in range(3):

        @pl.when(part_at(part, column))
        def _():
            for k in range(dp_count - 1):
                qkv_copy(k, part).wait_recv()
            add_rows(
                qkv_sum, [qkv_ref.at[part]] + [qkv_in.at[k] for k in range(dp_count - 1)], 32
            )
            for j in range(per_block):
                owner, other, same, stays = unit_copies(part, j)
                other.start()
                pl.when(owner != place)(same.start)
                pl.when(owner == place)(stays.start)

    for number in range(3, seq_count):
        hops(number)

    for k in range(seq_count - 1):
        line_copy(k).wait_recv()
    add_rows(
        out_done.at[core],
        [out_part.at[place]] + [out_line.at[k] for k in range(seq_count - 1)],
        32,
    )
    mine = out_done.at[core]
    swapped = remote(mine, mine, swap_sent, swap_here, across[0])
    swapped.start()

    last = (seq_count - 2) * micros
    for m in range(micros):
        own = line_refs[m].at[place]
        up, down = rising.at[last + m], falling.at[last + m]

        @pl.when(place > 0)
        def _():
            remote(up, up, rise_sent.at[0], rise_here.at[last + m], across[0]).wait_recv()

        @pl.when(place < seq_count - 1)
        def _():
            remote(down, down, fall_sent.at[0], fall_here.at[last + m], across[0]).wait_recv()

        @pl.when(place == 0)
        def _():
            add_rows(grad_ref.at[m], [own, down], 64)

        @pl.when(place == seq_count - 1)
        def _():
            add_rows(grad_ref.at[m], [own, up], 64)

        @pl.when((place > 0) & (place < seq_count - 1))
        def _():
            add_rows(grad_ref.at[m], [own, up, down], 64)

    for number in range(1, seq_count):
        for m in range(micros):
            hop_sent(number, m, True)
            hop_sent(number, m, False)
    for k in range(dp_count - 1):
        out_copy(k).wait_send()
        for part in range(3):

            @pl.when(part_at(part, cube[k][1]))
            def _():
                qkv_copy(k, part).wait_send()

    for k in range(seq_count - 1):
        line_copy(k).wait_send()
    for part in range(3):

        @pl.when(part_at(part, column))
        def _():
            for j in range(per_block):
                owner, other, same, stays = unit_copies(part, j)
                other.wait_send()
                pl.when(owner != place)(same.wait_send)
                pl.when(owner == place)(stays.wait)

    for i in range(per_shard):
        number = (column * seq_count + place) * per_shard + i
        piece = qkv_done.at[pl.ds(i * unit, unit)]

        @pl.when((number // per_block) % span_count != span)
        def _():
            remote(piece, piece, unit_sent.at[0], unit_here.at[i], across[0]).wait_recv()

    swapped.wait_send()
    theirs = out_done.at[1 - core]
    remote(theirs, theirs, swap_sent, swap_here, across[0]).wait_recv()


def spread_sums(lines, qkv, out, sizes):
    dp_count, seq_count, unit, per_shard, per_block, _ = sizes
    micros = len(lines)
    _, rows, width = lines[0].shape
    shard_out, half_width = out.shape[2:]
    block_rows = unit * per_block
    hops = (seq_count - 1) * micros
    vmem = pl.BlockSpec(memory_space=pltpu.VMEM)
    dma = pltpu.SemaphoreType.DMA
    return pl.pallas_call(
        functools.partial(spread_kernel, sizes, micros),
        in_specs=[vmem] * (micros + 2),
        out_specs=[vmem] * 3,
        out_shape=[
            jax.ShapeDtypeStruct((micros, rows, width), F32),
            jax.ShapeDtypeStruct((per_shard * unit, width), BF16),
            jax.ShapeDtypeStruct((2, shard_out, half_width), BF16),
        ],
        scratch_shapes=[
            pltpu.VMEM((hops, rows, width), BF16),
            pltpu.VMEM((hops, rows, width), BF16),
            pltpu.VMEM((dp_count - 1, block_rows, width), BF16),
            pltpu.VMEM((block_rows, width), BF16),
            pltpu.VMEM((dp_count - 1, seq_count, shard_out, half_width), BF16),
            pltpu.VMEM((seq_count, shard_out, half_width), BF16),
            pltpu.VMEM((seq_count - 1, shard_out, half_width), BF16),
            dma((hops,)),
            dma((hops,)),
            dma((hops,)),
            dma((hops,)),
            dma((dp_count - 1,)),
            dma((dp_count - 1,)),
            dma((dp_count - 1,)),
            dma((dp_count - 1,)),
            dma((2 * per_block,)),
            dma((per_shard,)),
            dma((seq_count - 1,)),
            dma((seq_count - 1,)),
            dma,
            dma,
            dma((per_block,)),
        ],
        compiler_params=pltpu.CompilerParams(
            collective_id=1, has_side_effects=True, vmem_limit_bytes=56 << 20
        ),
        cost_estimate=pl.CostEstimate(
            flops=0, bytes_accessed=256 * rows * width, transcendentals=0
        ),
        name="spread_sums",
    )(*lines, qkv, out)


def pick(table, number):
    return jnp.asarray(table, jnp.int32)[number]


def shards(
    tokens,
    lengths,
    memory,
    normalizer,
    qkv_weight,
    out_weight,
    norm_gains,
    gate_logit,
    inner_weight,
    down_weight,
    cotangent,
):
    micros, _, span_rows, width = tokens.shape
    head_count = gate_logit.shape[0]
    head_dim = width // head_count
    dp_count, seq_count = lax.axis_size("dp"), lax.axis_size("seq")
    span_count = 2 * seq_count
    total = span_rows * span_count
    heads_here = head_count // span_count
    block_rows = heads_here * head_dim
    core, column, place = lax.axis_index("rep"), lax.axis_index("dp"), lax.axis_index("seq")
    span = core * seq_count + place
    inner_half = inner_weight.shape[0] // 2

    own_rows = [tokens[m, 0] for m in range(micros)]

    def gather_rows(rows):
        return lax.all_gather(rows, ("rep", "seq"), axis=0, tiled=True)

    all_rows = [gather_rows(own_rows[0])]

    unit = math.gcd(qkv_weight.shape[0], block_rows)
    per_shard, per_block = qkv_weight.shape[0] // unit, block_rows // unit
    per_column = 3 * span_count // dp_count
    devices = 2 * dp_count * seq_count
    shard_out, shard_gain = out_weight.shape[0], norm_gains.shape[1]
    lanes = -(-shard_gain // 128) * 128
    gain_tile = jnp.zeros((8, lanes), F32)
    gain_tile = lax.dynamic_update_slice(gain_tile, norm_gains.astype(F32), (0, 0))
    head_weight, gains_all = gather_heads(
        qkv_weight, gain_tile, (dp_count, seq_count, unit, per_shard, per_block, per_column)
    )
    gains_all = jnp.swapaxes(gains_all[:, :2, :shard_gain], 0, 1).reshape(2, width)
    gain_one, gain_two = gains_all[0:1], gains_all[1:2]
    half_width = width // 2
    positions = span * span_rows + jnp.arange(span_rows)
    lives = []
    for m in range(micros):
        live_rows = (positions < lengths[m, 0]).astype(F32)
        lives.append(cotangent[m, 0].astype(F32) * live_rows[:, None])
    for rows in own_rows[1:]:
        all_rows.append(gather_rows(after(rows, all_rows[-1], head_weight)))
    out_half = lax.dynamic_slice_in_dim(out_weight, core * half_width, half_width, 1)
    cots = [live.astype(BF16) for live in lives]
    out_near, cot_all = gather_rest(
        after(out_half, head_weight, all_rows[0]), cots[0], (dp_count, seq_count)
    )
    grads_all = [cot_all]
    for cot in cots[1:]:
        grads_all.append(gather_cot(after(cot, grads_all[-1], all_rows[-1]), dp_count))
    out_far = swap(out_near)

    gate_share = jax.nn.sigmoid(gate_logit)
    gate_here = lax.dynamic_slice_in_dim(gate_share, span * heads_here, heads_here, 0)
    near_at, far_at = core * half_width, (1 - core) * half_width
    low_first = core == 0

    saved = []
    outputs, new_memories, new_norms = [], [], []
    for m in range(micros):
        hidden_one, projected = project(
            after(all_rows[m], all_rows[-1], grads_all[-1]),
            gain_one,
            head_weight,
        )
        if m == 0:
            near_units, near_downs = (
                lax.dynamic_slice_in_dim(w, core * inner_half, inner_half, 0)
                for w in (inner_weight, down_weight)
            )
        memory_here = lax.dynamic_slice_in_dim(memory[m, 0], span * heads_here, heads_here, 0)
        norm_here = lax.dynamic_slice_in_dim(
            normalizer[m, 0], span * heads_here, heads_here, 0
        ).reshape(heads_here, 1, head_dim)
        length = lengths[m]
        mixed_heads, dot_read, lse, new_memory, new_norm = attend(
            length, gate_here, projected, memory_here, norm_here
        )
        if m == 0:
            inner_near = lax.all_gather(
                after(near_units, all_rows[-1], out_near),
                "seq",
                axis=0,
                tiled=True,
            )
        new_memories.append(new_memory)
        new_norms.append(new_norm.reshape(heads_here, head_dim))
        mixed = lax.all_to_all(
            mixed_heads.reshape(span_count, span_rows, block_rows),
            ("rep", "seq"),
            0,
            0,
            tiled=True,
        )
        mixed = jnp.swapaxes(mixed, 0, 1).reshape(span_rows, width)
        mixed_near = lax.dynamic_slice_in_dim(mixed, near_at, half_width, 1)
        mixed_far = lax.dynamic_slice_in_dim(mixed, far_at, half_width, 1)
        after_attn = (
            own_rows[m].astype(F32)
            + nt(mixed_near, out_near)
            + nt(mixed_far, out_far)
        )
        scale_two = lax.rsqrt(jnp.mean(after_attn * after_attn, axis=-1, keepdims=True) + EPSILON)
        normed_two = after_attn * scale_two
        hidden_two = (normed_two * gain_two).astype(BF16)
        if m + 1 == micros:
            hidden_two = after(hidden_two, inner_near)
        rows_all = cube_gather(hidden_two, "dp")
        saved.append(
            dict(
                hidden_one=hidden_one,
                projected=projected,
                live=lives[m],
                grads=grads_all[m],
                memory=memory_here,
                norm=norm_here,
                length=length,
                dot_read=dot_read,
                lse=lse,
                mixed_heads=mixed_heads,
                mixed_near=mixed_near,
                mixed_far=mixed_far,
                after_attn=after_attn,
                scale_two=scale_two,
                normed_two=normed_two,
                rows=rows_all,
            )
        )

    down_near = after(
        lax.all_gather(near_downs, "seq", axis=0, tiled=True), *[s["rows"] for s in saved]
    )
    inner_far, down_far = swap(inner_near), swap(down_near)

    inner, down = (inner_near, inner_far), (down_near, down_far)
    last = None
    for s in saved:
        halves = []
        for half in range(2):
            halves.append(unit_pass(after(s["rows"], last), s["grads"], inner[half], down[half]))
            last = halves[-1][0]
        s["hidden"], s["grad_gates"], s["grad_ups"] = zip(*halves)

    def half_grads(left, right, half, extra, *earlier):
        pairs = [(s[left][half], s[right]) for s in saved]
        pairs[0] = (after(pairs[0][0], *earlier), pairs[0][1])
        return weight_pass(pairs, extra)

    def spread(values):
        return lax.psum_scatter(values, "seq", scatter_dimension=0, tiled=True)

    def rows_out(s, *earlier):
        gates = (after(s["grad_gates"][0], *earlier), s["grad_gates"][1])
        s["mlp_part"], s["grad_two"] = row_pass(
            s["hidden"], gates, s["grad_ups"], inner, down, dp_count
        )
        return s["grad_two"]

    down_far_sum = half_grads("hidden", "grads", 1, None, last)
    gate_far_sum = half_grads("grad_gates", "rows", 1, None, down_far_sum)
    down_sum = half_grads("hidden", "grads", 0, swap(down_far_sum), gate_far_sum)
    down_mine = spread(down_sum)
    last = rows_out(saved[0], down_sum)
    up_far_sum = half_grads("grad_ups", "rows", 1, None, last)
    gate_sum = half_grads("grad_gates", "rows", 0, swap(gate_far_sum), up_far_sum)
    gate_mine = spread(gate_sum)
    def rows_back(s):
        grad_two = s["grad_two"]
        grad_scaled = grad_two * gain_two
        normed_two = s["normed_two"]
        s["grad_after"] = s["live"] + s["scale_two"] * (
            grad_scaled
            - normed_two * jnp.mean(grad_scaled * normed_two, axis=-1, keepdims=True)
        )
        s["grad_branch"] = s["grad_after"].astype(BF16)
        s["gains_two"] = jnp.sum(grad_two * normed_two, axis=0)
        grad_mixed_near = nn(s["grad_branch"], out_near).astype(BF16)
        grad_mixed_far = nn(s["grad_branch"], out_far).astype(BF16)
        grad_mixed = jnp.concatenate(
            [
                jnp.where(low_first, grad_mixed_near, grad_mixed_far),
                jnp.where(low_first, grad_mixed_far, grad_mixed_near),
            ],
            axis=1,
        )
        s["grad_mixed"] = jnp.swapaxes(
            grad_mixed.reshape(span_rows, span_count, block_rows), 0, 1
        )
        return lax.all_to_all(s["grad_mixed"], ("rep", "seq"), 0, 0, tiled=True).reshape(
            total, block_rows
        )

    def heads_back(s, m, grad_heads):
        s["grad_projected"], gate_sums = attend_back(
            s["length"],
            gate_here,
            s["projected"],
            s["memory"],
            s["norm"],
            s["dot_read"],
            s["lse"],
            grad_heads,
        )
        s["gate"] = jnp.sum(gate_sums, axis=(1, 2))
        part_far, gains_far = project_back(
            1 - core, s["grad_projected"], head_weight, all_rows[m]
        )
        part_near, gains_near = project_back(
            core, s["grad_projected"], head_weight, all_rows[m], swap(part_far)
        )
        s["gains_one"] = (gains_far + gains_near)[0]
        return part_near

    def tokens_back(s, m, grad_one):
        rows_float = own_rows[m].astype(F32)
        scale_one = lax.rsqrt(jnp.mean(rows_float * rows_float, axis=-1, keepdims=True) + EPSILON)
        normed_one = rows_float * scale_one
        grad_scaled = grad_one * gain_one
        return (
            s["grad_after"]
            + scale_one
            * (
                grad_scaled
                - normed_one * jnp.mean(grad_scaled * normed_one, axis=-1, keepdims=True)
            )
        ).astype(BF16)

    heads_grads = [rows_back(saved[0])]
    last = gate_sum
    for m, s in enumerate(saved[1:]):
        last = rows_out(s, last, down_mine)
        heads_grads.append(rows_back(s))

    def spread_out(s, *earlier):
        return lax.psum_scatter(
            after(s["mlp_part"], *earlier), "dp", scatter_dimension=0, tiled=True
        )

    mlp_outs, sums = [spread_out(saved[0], saved[-1]["grad_branch"])], []
    earlier = (saved[-1]["grad_mixed"], gate_mine)
    for m, s in enumerate(saved):
        sums.append(heads_back(s, m, after(heads_grads[m], *earlier)))
        if m == 0:
            up_sum = half_grads(
                "grad_ups", "rows", 0, swap(up_far_sum), s["grad_projected"], heads_grads[-1]
            )
            up_mine = spread(up_sum)
            earlier = (up_sum, mlp_outs[0])
        else:
            mlp_outs.append(spread_out(s, up_sum))
    out_far_sum = weight_pass([(s["grad_branch"], s["mixed_far"]) for s in saved])
    out_sum = weight_pass(
        [(s["grad_branch"], s["mixed_near"]) for s in saved], swap(out_far_sum)
    )
    qkv_low = weight_pass([(s["grad_projected"], s["hidden_one"]) for s in saved]).reshape(
        3, block_rows, width
    )

    grad_ones, qkv_done, out_done = spread_sums(
        [after(p, up_mine, mlp_outs[0]).reshape(seq_count, span_rows, width) for p in sums],
        qkv_low,
        out_sum.reshape(dp_count, seq_count, shard_out, half_width),
        (dp_count, seq_count, unit, per_shard, per_block, per_column),
    )
    grad_tokens = [tokens_back(s, m, grad_ones[m]) for m, s in enumerate(saved)]
    grad_qkv = qkv_done.astype(F32)
    grad_out = jnp.swapaxes(out_done, 0, 1).reshape(shard_out, width).astype(F32)
    for s, mlp_out in zip(saved, mlp_outs):
        mlp_out = after(mlp_out, grad_ones)
        outputs.append((s["after_attn"] + mlp_out.astype(F32)).astype(BF16))

    def joined(name):
        return functools.reduce(jnp.add, [s[name] for s in saved])

    def both_cores(mine, axis):
        other = swap(mine)
        size = mine.shape[axis]
        shape = list(mine.shape)
        shape[axis] = 2 * size
        whole = jnp.zeros(shape, F32)
        whole = lax.dynamic_update_slice_in_dim(whole, mine.astype(F32), core * size, axis)
        return lax.dynamic_update_slice_in_dim(
            whole, other.astype(F32), (1 - core) * size, axis
        )

    grad_down = both_cores(down_mine, 0)
    grad_inner = both_cores(jnp.concatenate([gate_mine, up_mine], axis=1), 0)

    gate_terms = joined("gate") * gate_here * (1.0 - gate_here)
    gate_row = lax.dynamic_update_slice_in_dim(
        jnp.zeros((head_count,), F32), gate_terms, span * heads_here, 0
    )
    small = jnp.concatenate([joined("gains_one"), joined("gains_two"), gate_row])
    small = jnp.pad(small, (0, 8 * width - small.shape[0])).reshape(8, width)
    small = lax.all_gather(after(small, up_mine), ALL, axis=0, tiled=True)
    small = jnp.sum(small.reshape(devices, 8 * width)[:, : 3 * width], axis=0)
    gain_at = (column * seq_count + place) * shard_gain
    grad_gains = lax.dynamic_slice_in_dim(
        small[: 2 * width].reshape(2, width), gain_at, shard_gain, 1
    )
    grad_gate = small[2 * width : 2 * width + head_count]
    return (
        jnp.stack(outputs)[:, None],
        jnp.stack(new_memories)[:, None],
        jnp.stack(new_norms)[:, None],
        jnp.stack(grad_tokens)[:, None],
        grad_qkv,
        grad_out,
        grad_gains,
        grad_gate,
        grad_inner,
        grad_down,
    )


def solution(mesh):
    placed = (
        P(None, "dp", ("rep", "seq"), None),
        P(None, "dp"),
        P(None, "dp", None, None, None),
        P(None, "dp", None, None),
        P(("dp", "seq"), None),
        P(("dp", "seq"), None),
        P(None, ("dp", "seq")),
        P(),
        P(("dp", "seq"), None),
        P(("dp", "seq"), None),
        P(None, "dp", ("rep", "seq"), None),
    )
    return jax.shard_map(
        shards,
        mesh=mesh,
        in_specs=placed,
        out_specs=(
            P(None, "dp", ("rep", "seq"), None),
            P(None, "dp", ("rep", "seq"), None, None),
            P(None, "dp", ("rep", "seq"), None),
            P(None, "dp", ("rep", "seq"), None),
            P(("dp", "seq"), None),
            P(("dp", "seq"), None),
            P(None, ("dp", "seq")),
            P(),
            P(("dp", "seq"), None),
            P(("dp", "seq"), None),
        ),
        check_vma=False,
    )
```

```python
import functools
import math

import jax
import jax.numpy as jnp
from jax import lax
from jax.experimental import pallas as pl
from jax.experimental.pallas import tpu as pltpu
from jax.sharding import PartitionSpec as P

EPSILON = 1e-05
LOG2E = 1.4426950408889634
NEG = -1e30
F32 = jnp.float32
BF16 = jnp.bfloat16
ALL = ("rep", "dp", "seq")


def nt(left_side, right_side):
    return lax.dot_general(
        left_side, right_side, (((1,), (1,)), ((), ())), preferred_element_type=F32
    )


def nn(left_side, right_side):
    return lax.dot_general(
        left_side, right_side, (((1,), (0,)), ((), ())), preferred_element_type=F32
    )


def tn(left_side, right_side):
    return lax.dot_general(
        left_side, right_side, (((0,), (0,)), ((), ())), preferred_element_type=F32
    )


def elu_one(values):
    return jnp.where(values > 0.0, values + 1.0, jnp.exp(jnp.minimum(values, 0.0)))


def project_kernel(rows_ref, gain_ref, weight_ref, hidden_ref, projected_ref):
    rows = rows_ref[...].astype(F32)
    scale = lax.rsqrt(jnp.mean(rows * rows, axis=-1, keepdims=True) + EPSILON)
    hidden = (rows * scale * gain_ref[...]).astype(BF16)
    hidden_ref[...] = hidden
    projected_ref[...] = nt(hidden, weight_ref[...]).astype(BF16)


def project(rows, gain, weight):
    count, width = rows.shape
    outs = weight.shape[0]
    block = min(256, count)
    return pl.pallas_call(
        project_kernel,
        grid=(count // block,),
        in_specs=[
            pl.BlockSpec((block, width), lambda i: (i, 0)),
            pl.BlockSpec((1, width), lambda i: (0, 0)),
            pl.BlockSpec((outs, width), lambda i: (0, 0)),
        ],
        out_specs=[
            pl.BlockSpec((block, width), lambda i: (i, 0)),
            pl.BlockSpec((block, outs), lambda i: (i, 0)),
        ],
        out_shape=[
            jax.ShapeDtypeStruct((count, width), BF16),
            jax.ShapeDtypeStruct((count, outs), BF16),
        ],
        compiler_params=pltpu.CompilerParams(vmem_limit_bytes=32 << 20),
        cost_estimate=pl.CostEstimate(
            flops=2 * count * width * outs,
            bytes_accessed=4 * count * width + 2 * outs * (width + count),
            transcendentals=count,
        ),
        name="project",
    )(rows, gain, weight)


def attend_kernel(
    block,
    length_ref,
    gate_ref,
    q_ref,
    k_ref,
    v_ref,
    mem_ref,
    norm_ref,
    mixed_ref,
    dot_ref,
    lse_ref,
    new_mem_ref,
    new_norm_ref,
    v_turned,
):
    head, step = pl.program_id(0), pl.program_id(1)
    length = length_ref[0]
    total, width = k_ref.shape
    memory = mem_ref[0]
    norm_row = norm_ref[0]
    memory_low = memory.astype(BF16)

    @pl.when(step == 0)
    def _():
        v_turned[...] = v_ref[...].T
        key_sig = elu_one(k_ref[...].astype(F32))
        below = jnp.sum(key_sig * norm_row, axis=-1, keepdims=True)
        recalled = nn(key_sig.astype(BF16), memory_low) / below
        change = v_ref[...].astype(F32) - recalled
        live = lax.broadcasted_iota(jnp.int32, (total, width), 0) < length
        kept = jnp.where(live, key_sig, 0.0)
        new_mem_ref[0] = memory + tn(kept.astype(BF16), change.astype(BF16))
        new_norm_ref[0] = norm_row + jnp.sum(kept, axis=0, keepdims=True)

    queries = q_ref[...]
    factor = LOG2E * width ** (-0.5)

    def visit(at, carry, masked):
        high, mass, acc = carry
        start = pl.multiple_of(at * block, block)
        scores = nt(k_ref[pl.ds(start, block), :], queries) * factor
        if masked:
            key_at = start + lax.broadcasted_iota(jnp.int32, (block, block), 0)
            query_at = step * block + lax.broadcasted_iota(jnp.int32, (block, block), 1)
            scores = jnp.where((key_at <= query_at) & (key_at < length), scores, NEG)
        higher = jnp.maximum(high, jnp.max(scores, axis=0, keepdims=True))
        weights = jnp.exp2(scores - higher)
        shrink = jnp.exp2(high - higher)
        mass = mass * shrink + jnp.sum(weights, axis=0, keepdims=True)
        acc = acc * shrink + nn(v_turned[:, pl.ds(start, block)], weights.astype(BF16))
        return higher, mass, acc

    full = jnp.minimum(step, length // block)
    end = jnp.minimum(step + 1, (length + block - 1) // block)
    carry = (
        jnp.full((1, block), NEG, F32),
        jnp.zeros((1, block), F32),
        jnp.zeros((width, block), F32),
    )
    carry = lax.fori_loop(0, full, functools.partial(visit, masked=False), carry)
    high, mass, acc = lax.fori_loop(full, end, functools.partial(visit, masked=True), carry)
    dot_read = (acc / mass).T
    query_sig = elu_one(queries.astype(F32))
    below = jnp.sum(query_sig * norm_row, axis=-1, keepdims=True)
    mem_read = nn(query_sig.astype(BF16), memory_low) / below
    gate = gate_ref[head]
    mixed_ref[...] = (gate * mem_read + (1.0 - gate) * dot_read).astype(BF16)
    dot_ref[...] = dot_read
    lse_ref[0] = high + jnp.log2(mass)


def attend(length, gate, projected, memory, normalizer):
    total = projected.shape[0]
    heads, width = normalizer.shape[0], normalizer.shape[2]
    block = min(512, total)
    smem = pl.BlockSpec(memory_space=pltpu.SMEM)
    return pl.pallas_call(
        functools.partial(attend_kernel, block),
        grid=(heads, total // block),
        in_specs=[
            smem,
            smem,
            pl.BlockSpec((block, width), lambda h, i: (i, h)),
            pl.BlockSpec((total, width), lambda h, i: (0, heads + h)),
            pl.BlockSpec((total, width), lambda h, i: (0, 2 * heads + h)),
            pl.BlockSpec((1, width, width), lambda h, i: (h, 0, 0)),
            pl.BlockSpec((1, 1, width), lambda h, i: (h, 0, 0)),
        ],
        out_specs=[
            pl.BlockSpec((block, width), lambda h, i: (i, h)),
            pl.BlockSpec((block, width), lambda h, i: (i, h)),
            pl.BlockSpec((1, 1, block), lambda h, i: (h, 0, i)),
            pl.BlockSpec((1, width, width), lambda h, i: (h, 0, 0)),
            pl.BlockSpec((1, 1, width), lambda h, i: (h, 0, 0)),
        ],
        out_shape=[
            jax.ShapeDtypeStruct((total, heads * width), BF16),
            jax.ShapeDtypeStruct((total, heads * width), F32),
            jax.ShapeDtypeStruct((heads, 1, total), F32),
            jax.ShapeDtypeStruct((heads, width, width), F32),
            jax.ShapeDtypeStruct((heads, 1, width), F32),
        ],
        scratch_shapes=[pltpu.VMEM((width, total), BF16)],
        compiler_params=pltpu.CompilerParams(vmem_limit_bytes=40 << 20),
        cost_estimate=pl.CostEstimate(
            flops=4 * heads * total * total * width,
            bytes_accessed=heads * total * width * 12,
            transcendentals=heads * total * total,
        ),
        name="attend",
    )(length, gate, projected, projected, projected, memory, normalizer)


def attend_back_kernel(
    block,
    length_ref,
    gate_ref,
    q_ref,
    k_ref,
    v_ref,
    mem_ref,
    norm_ref,
    dot_ref,
    lse_ref,
    grad_ref,
    out_ref,
    gate_sum_ref,
    k_turned,
    k_sum,
    v_sum,
):
    head, step = pl.program_id(0), pl.program_id(1)
    heads, steps = pl.num_programs(0), pl.num_programs(1)
    length = length_ref[0]
    total, width = k_ref.shape
    gate = gate_ref[head]

    @pl.when(step == 0)
    def _():
        k_turned[...] = k_ref[...].T
        k_sum[...] = jnp.zeros_like(k_sum)
        v_sum[...] = jnp.zeros_like(v_sum)
        gate_sum_ref[...] = jnp.zeros_like(gate_sum_ref)

    queries = q_ref[...]
    query_float = queries.astype(F32)
    grad_mixed = grad_ref[...].astype(F32)
    grad_dot = ((1.0 - gate) * grad_mixed).astype(BF16)
    dot_read = dot_ref[...]
    offset = jnp.sum((grad_dot.astype(F32) * dot_read).T, axis=0, keepdims=True)
    lse = lse_ref[0]
    scale = width ** (-0.5)
    factor = LOG2E * scale

    def visit(at, acc, masked):
        start = pl.multiple_of(at * block, block)
        here = pl.ds(start, block)
        scores = nt(k_ref[here, :], queries) * factor
        weights = jnp.exp2(scores - lse)
        if masked:
            key_at = start + lax.broadcasted_iota(jnp.int32, (block, block), 0)
            query_at = step * block + lax.broadcasted_iota(jnp.int32, (block, block), 1)
            weights = jnp.where((key_at <= query_at) & (key_at < length), weights, 0.0)
        grad_probs = nt(v_ref[here, :], grad_dot)
        grad_scores = (weights * (grad_probs - offset) * scale).astype(BF16)
        v_sum[here, :] += nn(weights.astype(BF16), grad_dot)
        k_sum[here, :] += nn(grad_scores, queries)
        return acc + nn(k_turned[:, here], grad_scores)

    full = jnp.minimum(step, length // block)
    end = jnp.minimum(step + 1, (length + block - 1) // block)
    acc = jnp.zeros((width, block), F32)
    acc = lax.fori_loop(0, full, functools.partial(visit, masked=False), acc)
    acc = lax.fori_loop(full, end, functools.partial(visit, masked=True), acc)

    memory_low = mem_ref[0].astype(BF16)
    norm_row = norm_ref[0]
    query_sig = elu_one(query_float)
    below = jnp.sum(query_sig * norm_row, axis=-1, keepdims=True)
    numerator = nn(query_sig.astype(BF16), memory_low)
    inverse = 1.0 / below
    grad_read = gate * grad_mixed
    grad_below = -jnp.sum(grad_read * numerator, axis=-1, keepdims=True) * inverse * inverse
    grad_sig = nt((grad_read * inverse).astype(BF16), memory_low) + grad_below * norm_row
    slope = jnp.where(query_float > 0.0, 1.0, jnp.exp(jnp.minimum(query_float, 0.0)))
    rows = pl.ds(pl.multiple_of(step * block, block), block)
    out_ref[rows, pl.ds(pl.multiple_of(head * width, width), width)] = (
        acc.T + grad_sig * slope
    ).astype(BF16)
    gate_sum_ref[0] += jnp.sum(
        grad_mixed * (numerator * inverse - dot_read), axis=0, keepdims=True
    )

    @pl.when(step == steps - 1)
    def _():
        k_at = pl.multiple_of((heads + head) * width, width)
        v_at = pl.multiple_of((2 * heads + head) * width, width)
        out_ref[:, pl.ds(k_at, width)] = k_sum[...].astype(BF16)
        out_ref[:, pl.ds(v_at, width)] = v_sum[...].astype(BF16)


def attend_back(length, gate, projected, memory, normalizer, dot_read, lse, grad_mixed):
    total = projected.shape[0]
    heads, width = normalizer.shape[0], normalizer.shape[2]
    block = min(512, total)
    smem = pl.BlockSpec(memory_space=pltpu.SMEM)
    return pl.pallas_call(
        functools.partial(attend_back_kernel, block),
        grid=(heads, total // block),
        in_specs=[
            smem,
            smem,
            pl.BlockSpec((block, width), lambda h, i: (i, h)),
            pl.BlockSpec((total, width), lambda h, i: (0, heads + h)),
            pl.BlockSpec((total, width), lambda h, i: (0, 2 * heads + h)),
            pl.BlockSpec((1, width, width), lambda h, i: (h, 0, 0)),
            pl.BlockSpec((1, 1, width), lambda h, i: (h, 0, 0)),
            pl.BlockSpec((block, width), lambda h, i: (i, h)),
            pl.BlockSpec((1, 1, block), lambda h, i: (h, 0, i)),
            pl.BlockSpec((block, width), lambda h, i: (i, h)),
        ],
        out_specs=[
            pl.BlockSpec((total, 3 * heads * width), lambda h, i: (0, 0)),
            pl.BlockSpec((1, 1, width), lambda h, i: (h, 0, 0)),
        ],
        out_shape=[
            jax.ShapeDtypeStruct((total, 3 * heads * width), BF16),
            jax.ShapeDtypeStruct((heads, 1, width), F32),
        ],
        scratch_shapes=[
            pltpu.VMEM((width, total), BF16),
            pltpu.VMEM((total, width), F32),
            pltpu.VMEM((total, width), F32),
        ],
        compiler_params=pltpu.CompilerParams(vmem_limit_bytes=40 << 20),
        cost_estimate=pl.CostEstimate(
            flops=10 * heads * total * total * width,
            bytes_accessed=heads * total * width * 20,
            transcendentals=heads * total * total,
        ),
        name="attend_back",
    )(length, gate, projected, projected, projected, memory, normalizer, dot_read, lse, grad_mixed)


def unit_kernel(
    rows_ref, grad_ref, inner_ref, down_ref, hidden_ref, grad_gate_ref, grad_up_ref
):
    width = rows_ref.shape[1]
    rows = rows_ref[...]
    gates = nt(rows, inner_ref[:, :width])
    ups = nt(rows, inner_ref[:, width:])
    grad_hidden = nt(grad_ref[...], down_ref[...])
    sigmoid = 1.0 / (1.0 + jnp.exp(-gates))
    silu = gates * sigmoid
    hidden_ref[...] = (silu * ups).astype(BF16)
    grad_gate_ref[...] = (
        grad_hidden * ups * (sigmoid * (1.0 + gates * (1.0 - sigmoid)))
    ).astype(BF16)
    grad_up_ref[...] = (grad_hidden * silu).astype(BF16)


def unit_pass(rows, grads, inner, down):
    count, width = rows.shape
    units = inner.shape[0]
    tile = min(256, units)
    resident = pl.BlockSpec((count, width), lambda t: (0, 0), pipeline_mode=pl.Buffered(1))
    column = pl.BlockSpec((count, tile), lambda t: (0, t))
    unit_shape = jax.ShapeDtypeStruct((count, units), BF16)
    return pl.pallas_call(
        unit_kernel,
        grid=(units // tile,),
        in_specs=[
            resident,
            resident,
            pl.BlockSpec((tile, 2 * width), lambda t: (t, 0)),
            pl.BlockSpec((tile, width), lambda t: (t, 0)),
        ],
        out_specs=[column] * 3,
        out_shape=[unit_shape] * 3,
        compiler_params=pltpu.CompilerParams(vmem_limit_bytes=56 << 20),
        cost_estimate=pl.CostEstimate(
            flops=2 * 3 * count * width * units,
            bytes_accessed=units * (6 * width + 6 * count) + 4 * count * width,
            transcendentals=count * units,
        ),
        name="unit_pass",
    )(rows, grads, inner, down)


def weight_kernel(pairs, *refs):
    out_ref = refs[-1]
    total = tn(refs[0][...], refs[1][...])
    for at in range(1, pairs):
        total += tn(refs[2 * at][...], refs[2 * at + 1][...])
    if len(refs) > 2 * pairs + 1:
        total += refs[2 * pairs][...].astype(F32)
    out_ref[...] = total.astype(BF16)


def weight_pass(pairs, extra=None):
    size, width = pairs[0][0].shape[1], pairs[0][1].shape[1]
    tile = min(256, size)
    in_specs, operands, flops, moved = [], [], 0, 2 * size * width
    for left, right in pairs:
        count = left.shape[0]
        in_specs.append(pl.BlockSpec((count, tile), lambda t: (0, t)))
        in_specs.append(
            pl.BlockSpec((count, width), lambda t: (0, 0), pipeline_mode=pl.Buffered(1))
        )
        operands += [left, right]
        flops += 2 * count * size * width
        moved += 2 * count * (size + width)
    if extra is not None:
        in_specs.append(pl.BlockSpec((tile, width), lambda t: (t, 0)))
        operands.append(extra)
        moved += 2 * size * width
    return pl.pallas_call(
        functools.partial(weight_kernel, len(pairs)),
        grid=(size // tile,),
        in_specs=in_specs,
        out_specs=pl.BlockSpec((tile, width), lambda t: (t, 0)),
        out_shape=jax.ShapeDtypeStruct((size, width), BF16),
        compiler_params=pltpu.CompilerParams(vmem_limit_bytes=56 << 20),
        cost_estimate=pl.CostEstimate(flops=flops, bytes_accessed=moved, transcendentals=0),
        name="weight_pass",
    )(*operands)


def back_kernel(half_ref, grad_ref, weight_ref, rows_ref, *refs):
    out_ref, gain_ref = refs[-2:]

    @pl.when(pl.program_id(0) == 0)
    def _():
        gain_ref[...] = jnp.zeros_like(gain_ref)

    part = nn(grad_ref[...], weight_ref[...])
    total = part + refs[0][...].astype(F32) if len(refs) > 2 else part
    out_ref[...] = total.astype(BF16)
    rows = rows_ref[...].astype(F32)
    scale = lax.rsqrt(jnp.mean(rows * rows, axis=-1, keepdims=True) + EPSILON)
    gain_ref[...] += jnp.sum(part * (rows * scale), axis=0, keepdims=True)


def project_back(half, grads, weight, rows, extra=None):
    count, outs = grads.shape[0] // 2, grads.shape[1]
    width = weight.shape[1]
    block = min(256, count)
    steps = count // block
    return pl.pallas_call(
        back_kernel,
        grid_spec=pltpu.PrefetchScalarGridSpec(
            num_scalar_prefetch=1,
            grid=(steps,),
            in_specs=[
                pl.BlockSpec((block, outs), lambda i, at: (at[0] * steps + i, 0)),
                pl.BlockSpec((outs, width), lambda i, at: (0, 0)),
                pl.BlockSpec((block, width), lambda i, at: (at[0] * steps + i, 0)),
            ]
            + [pl.BlockSpec((block, width), lambda i, at: (i, 0))] * (extra is not None),
            out_specs=[
                pl.BlockSpec((block, width), lambda i, at: (i, 0)),
                pl.BlockSpec((1, width), lambda i, at: (0, 0)),
            ],
        ),
        out_shape=[
            jax.ShapeDtypeStruct((count, width), BF16),
            jax.ShapeDtypeStruct((1, width), F32),
        ],
        compiler_params=pltpu.CompilerParams(vmem_limit_bytes=40 << 20),
        cost_estimate=pl.CostEstimate(
            flops=2 * count * width * outs,
            bytes_accessed=4 * count * width + 2 * outs * (width + count),
            transcendentals=count,
        ),
        name="project_back",
    )(
        jnp.reshape(half, (1,)).astype(jnp.int32),
        grads,
        weight,
        rows,
        *([] if extra is None else [extra]),
    )


def swap(values):
    return lax.ppermute(values, "rep", [(0, 1), (1, 0)])


def after(values, *earlier):
    earlier = [e for e in earlier if e is not None]
    return lax.optimization_barrier((values, *earlier))[0] if earlier else values


def add_low(left_side, right_side):
    return (left_side.astype(F32) + right_side.astype(F32)).astype(BF16)


def line_gather(values, axis):
    count = lax.axis_size(axis)
    here = lax.axis_index(axis)
    rows = values.shape[0]
    table = jnp.zeros(((3 * count - 2) * rows,) + values.shape[1:], values.dtype)

    def put(table, piece, origin):
        return lax.dynamic_update_slice_in_dim(table, piece, (origin + count - 1) * rows, 0)

    table = put(table, values, here)
    rising = falling = values
    for hop in range(1, count):
        rising = lax.ppermute(
            rising, axis, [(a, a + 1) for a in range(count - 1) if a >= hop - 1]
        )
        falling = lax.ppermute(
            falling, axis, [(a, a - 1) for a in range(1, count) if a + hop - 1 < count]
        )
        table = put(table, rising, here - hop)
        table = put(table, falling, here + hop)
    return table[(count - 1) * rows : (2 * count - 1) * rows]


def line_scatter(values, axis, pins=()):
    count = lax.axis_size(axis)
    here = lax.axis_index(axis)
    rows = values.shape[0] // count

    def block(owner):
        start = jnp.clip(owner, 0, count - 1) * rows
        return lax.dynamic_slice_in_dim(values, start, rows, 0).astype(F32)

    rising = falling = None
    for hop in range(1, count):
        reach = count - hop
        up, down = block(here + reach), block(here - reach)
        if rising is not None:
            up, down = up + rising.astype(F32), down + falling.astype(F32)
        rising = lax.ppermute(
            up.astype(BF16), axis, [(a, a + 1) for a in range(count) if a + reach < count]
        )
        falling = lax.ppermute(
            down.astype(BF16), axis, [(a, a - 1) for a in range(count) if a - reach >= 0]
        )
        if hop <= len(pins):
            rising, falling = after(rising, pins[hop - 1]), after(falling, pins[hop - 1])
    return block(here) + rising.astype(F32) + falling.astype(F32)


def cube_bits(count):
    bits = [1 << b for b in range(count.bit_length() - 1)]
    return bits, bits[::-1]


def cube_order(bits):
    order = [0]
    for bit in reversed(bits):
        order = order + [k | bit for k in order]
    return order


def cube_gather(values, axis):
    count = lax.axis_size(axis)
    half = values.shape[0] // 2
    parts = []
    for bits, start in zip(cube_bits(count), (0, half)):
        held = {0: values[start : start + half]}
        for bit in bits:
            pairs = [(a, a ^ bit) for a in range(count)]
            held.update({k ^ bit: lax.ppermute(v, axis, pairs) for k, v in list(held.items())})
        parts += [held[k] for k in cube_order(bits)]
    return jnp.concatenate(parts, axis=0)


def cube_scatter(values, axis, pins=()):
    count = lax.axis_size(axis)
    half = values.shape[0] // 2
    parts = []
    for bits, start in zip(cube_bits(count), (0, half)):
        held = values[start : start + half]
        for at, bit in enumerate(bits):
            pairs = [(a, a ^ bit) for a in range(count)]
            keep = held.shape[0] // 2
            got = lax.ppermute(held[keep:].astype(BF16), axis, pairs)
            if at < len(pins):
                got = after(got, pins[at])
            held = held[:keep].astype(F32) + got.astype(F32)
        parts.append(held)
    return jnp.concatenate(parts, axis=0)


def remote(source, target, sent, landed, device):
    return pltpu.make_async_remote_copy(
        src_ref=source,
        dst_ref=target,
        send_sem=sent,
        recv_sem=landed,
        device_id=device,
        device_id_type=pl.DeviceIdType.MESH,
    )


def greet(devices):
    barrier = pltpu.get_barrier_semaphore()
    for device in devices:
        pl.semaphore_signal(barrier, inc=1, device_id=device, device_id_type=pl.DeviceIdType.MESH)
    pl.semaphore_wait(barrier, len(devices))


def heads_kernel(
    sizes,
    qkv_ref,
    gain_ref,
    head_ref,
    gains_ref,
    landed,
    unit_sent,
    unit_here,
    block_sent,
    block_here,
    line_sent,
    line_here,
    cube_sent,
    cube_here,
    local,
):
    dp_count, seq_count, unit, per_shard, per_block, per_column = sizes
    span_count = 2 * seq_count
    block_rows = unit * per_block
    core, column, place = lax.axis_index("rep"), lax.axis_index("dp"), lax.axis_index("seq")
    span, shard = core * seq_count + place, column * seq_count + place
    line = [(core, column, (place + k) % seq_count) for k in range(1, seq_count)]
    cube = [(core, (column + k) % dp_count, place) for k in range(1, dp_count)]
    greet(line + cube)

    gains = []
    for k, device in enumerate(line):
        gains.append(
            remote(gain_ref, gains_ref.at[shard], line_sent.at[k], line_here.at[k], device)
        )
    for copy in gains:
        copy.start()
    own_gain = pltpu.make_async_copy(gain_ref, gains_ref.at[shard], local.at[0])
    own_gain.start()

    def rows(ref, at, size):
        return ref.at[pl.ds(pl.multiple_of(at * size, size), size)]

    def unit_copy(i):
        number = shard * per_shard + i
        owner = (number // per_block) % span_count
        source, target = rows(qkv_ref, i, unit), rows(landed, number % per_block, unit)
        far = remote(
            source,
            target,
            unit_sent.at[i],
            unit_here.at[number % per_block],
            (core, column, owner % seq_count),
        )
        near = pltpu.make_async_copy(source, target, local.at[1 + i])
        mine = owner // seq_count == core
        stays = owner % seq_count == place
        return far, near, mine & jnp.logical_not(stays), mine & stays

    for i in range(per_shard):
        far, near, leaves, stays = unit_copy(i)
        pl.when(leaves)(far.start)
        pl.when(stays)(near.start)
    for i in range(per_shard):
        _, near, _, stays = unit_copy(i)
        pl.when(stays)(near.wait)

    def block_copies(part):
        target = rows(head_ref, part, block_rows)
        far = [
            remote(landed, target, block_sent.at[k], block_here.at[part], device)
            for k, device in enumerate(cube)
        ]
        return far, pltpu.make_async_copy(landed, target, local.at[0])

    own_gain.wait()
    for part in range(3):
        number = part * span_count + span

        @pl.when(number // per_column == column)
        def _():
            for j in range(per_block):
                source = ((number * per_block + j) // per_shard) % seq_count

                @pl.when(source != place)
                def _():
                    here = rows(landed, j, unit)
                    remote(here, here, unit_sent.at[0], unit_here.at[j], line[0]).wait_recv()

            far, near = block_copies(part)
            for copy in far:
                copy.start()
            near.start()

    for copy in gains:
        copy.wait()
    mine = gains_ref.at[pl.ds(column * seq_count, seq_count)]
    gains = [
        remote(mine, mine, cube_sent.at[k], cube_here.at[k], device)
        for k, device in enumerate(cube)
    ]
    for copy in gains:
        copy.start()
    for part in range(3):
        number = part * span_count + span
        far, near = block_copies(part)

        @pl.when(number // per_column == column)
        def _():
            near.wait()
            for copy in far:
                copy.wait_send()

        @pl.when(number // per_column != column)
        def _():
            far[0].wait_recv()

    for k, copy in enumerate(gains):
        copy.wait_send()
        origin = (column + dp_count - k - 1) % dp_count
        theirs = gains_ref.at[pl.ds(origin * seq_count, seq_count)]
        remote(theirs, theirs, cube_sent.at[k], cube_here.at[k], cube[k]).wait_recv()
    for i in range(per_shard):
        far, _, leaves, _ = unit_copy(i)
        pl.when(leaves)(far.wait_send)


def gather_heads(qkv_weight, gains, sizes):
    dp_count, seq_count, unit, per_shard, per_block, _ = sizes
    width = qkv_weight.shape[1]
    block_rows = unit * per_block
    anywhere = pl.BlockSpec(memory_space=pl.ANY)
    dma = pltpu.SemaphoreType.DMA
    return pl.pallas_call(
        functools.partial(heads_kernel, sizes),
        in_specs=[anywhere, anywhere],
        out_specs=[anywhere, anywhere],
        out_shape=[
            jax.ShapeDtypeStruct((3 * block_rows, width), BF16),
            jax.ShapeDtypeStruct((dp_count * seq_count, *gains.shape), F32),
        ],
        scratch_shapes=[
            pltpu.VMEM((block_rows, width), BF16),
            dma((per_shard,)),
            dma((per_block,)),
            dma((dp_count - 1,)),
            dma((3,)),
            dma((seq_count - 1,)),
            dma((seq_count - 1,)),
            dma((dp_count - 1,)),
            dma((dp_count - 1,)),
            dma((1 + per_shard,)),
        ],
        compiler_params=pltpu.CompilerParams(
            collective_id=0, has_side_effects=True, vmem_limit_bytes=16 << 20
        ),
        cost_estimate=pl.CostEstimate(
            flops=0, bytes_accessed=64 * block_rows * width, transcendentals=0
        ),
        name="gather_heads",
    )(qkv_weight, gains)


def flipped(value, bits):
    bit = 1
    while bit <= bits:
        if bits & bit:
            value = value + bit - 2 * bit * ((value // bit) % 2)
        bit *= 2
    return value


def cot_copies(cot_ref, cot_all, cube, sent, here, local, first):
    count = len(cube) + 1
    half = cot_ref.shape[0] // 2
    stays, leaves = [], []
    for side, bits in enumerate(cube_bits(count)):
        order = cube_order(bits)
        source = cot_ref.at[pl.ds(side * half, half)]
        for k in range(count):
            target = cot_all.at[pl.ds((side * count + order.index(k)) * half, half)]
            if k == 0:
                stays.append(pltpu.make_async_copy(source, target, local.at[first + side]))
            else:
                at = side * (count - 1) + k - 1
                leaves.append(remote(source, target, sent.at[at], here.at[at], cube[k - 1]))
    return stays, leaves


def cot_kernel(count, cot_ref, cot_all, sent, here, local):
    core, column, place = lax.axis_index("rep"), lax.axis_index("dp"), lax.axis_index("seq")
    cube = [(core, flipped(column, k), place) for k in range(1, count)]
    greet(cube)
    stays, leaves = cot_copies(cot_ref, cot_all, cube, sent, here, local, 0)
    for copy in stays + leaves:
        copy.start()
    for copy in stays + leaves:
        copy.wait()


def gather_cot(cot, count):
    rows, width = cot.shape
    anywhere = pl.BlockSpec(memory_space=pl.ANY)
    dma = pltpu.SemaphoreType.DMA
    return pl.pallas_call(
        functools.partial(cot_kernel, count),
        in_specs=[anywhere],
        out_specs=anywhere,
        out_shape=jax.ShapeDtypeStruct((count * rows, width), BF16),
        scratch_shapes=[dma((2 * (count - 1),)), dma((2 * (count - 1),)), dma((2,))],
        compiler_params=pltpu.CompilerParams(collective_id=3, has_side_effects=True),
        cost_estimate=pl.CostEstimate(
            flops=0, bytes_accessed=8 * rows * width, transcendentals=0
        ),
        name="gather_cot",
    )(cot)


def rest_kernel(sizes, *refs):
    dp_count, seq_count = sizes
    out_ref, cot_ref, out_all, cot_all = refs[:4]
    line_sent, line_here, cube_sent, cube_here, cot_sent, cot_here, local = refs[4:]
    core, column, place = lax.axis_index("rep"), lax.axis_index("dp"), lax.axis_index("seq")
    line = [(core, column, (place + k) % seq_count) for k in range(1, seq_count)]
    cube = [(core, flipped(column, k), place) for k in range(1, dp_count)]
    greet(line + cube)
    shard_rows = out_ref.shape[0]
    column_rows = seq_count * shard_rows
    def out_rows(start, size):
        return out_all.at[pl.ds(pl.multiple_of(start, shard_rows), size)]

    mine = out_rows((column * seq_count + place) * shard_rows, shard_rows)
    lines = [
        remote(out_ref, mine, line_sent.at[k], line_here.at[k], device)
        for k, device in enumerate(line)
    ]
    own_out = pltpu.make_async_copy(out_ref, mine, local.at[0])

    own_cots, cots = cot_copies(cot_ref, cot_all, cube, cot_sent, cot_here, local, 1)
    for copy in lines + [own_out] + own_cots + cots:
        copy.start()
    own_out.wait()
    for copy in lines:
        copy.wait()
    mine = out_rows(column * column_rows, column_rows)
    cubes = [
        remote(mine, mine, cube_sent.at[k], cube_here.at[k], device)
        for k, device in enumerate(cube)
    ]
    for copy in cubes:
        copy.start()
    for copy in own_cots + cots:
        copy.wait()
    for k, copy in enumerate(cubes):
        copy.wait_send()
        theirs = out_rows(cube[k][1] * column_rows, column_rows)
        remote(theirs, theirs, cube_sent.at[k], cube_here.at[k], cube[k]).wait_recv()


def gather_rest(out_half, cot, sizes):
    dp_count, seq_count = sizes
    rows, width = cot.shape
    anywhere = pl.BlockSpec(memory_space=pl.ANY)
    dma = pltpu.SemaphoreType.DMA
    return pl.pallas_call(
        functools.partial(rest_kernel, sizes),
        in_specs=[anywhere] * 2,
        out_specs=[anywhere] * 2,
        out_shape=[
            jax.ShapeDtypeStruct(
                (dp_count * seq_count * out_half.shape[0], out_half.shape[1]), BF16
            ),
            jax.ShapeDtypeStruct((dp_count * rows, width), BF16),
        ],
        scratch_shapes=[
            dma((seq_count - 1,)),
            dma((seq_count - 1,)),
            dma((dp_count - 1,)),
            dma((dp_count - 1,)),
            dma((2 * (dp_count - 1),)),
            dma((2 * (dp_count - 1),)),
            dma((3,)),
        ],
        compiler_params=pltpu.CompilerParams(collective_id=2, has_side_effects=True),
        cost_estimate=pl.CostEstimate(
            flops=0, bytes_accessed=8 * rows * width, transcendentals=0
        ),
        name="gather_rest",
    )(out_half, cot)


def row_kernel(count, *refs):
    hidden, gates, ups, gate_w, up_w, down_w = (refs[2 * i : 2 * i + 2] for i in range(6))
    out_ref, grad_ref, parts, sent, here = refs[12:17]
    landed = refs[17:]
    stages = len(landed)
    step, steps = pl.program_id(0), pl.num_programs(0)
    core, column, place = lax.axis_index("rep"), lax.axis_index("dp"), lax.axis_index("seq")
    width = parts.shape[2]
    size = out_ref.shape[0] // (2 * count)

    @pl.when(step == 0)
    def _():
        greet([(core, flipped(column, bit), place) for bit in cube_bits(count)[0]])

    def copy(t, stage, side):
        keep = (count >> (stage + 1)) * size
        flat = (t * stages + stage) * 2 + side
        return remote(
            parts.at[t, pl.ds(side * count * size + keep, keep)],
            landed[stage].at[t, side],
            sent.at[flat],
            here.at[flat],
            (core, flipped(column, cube_bits(count)[side][stage]), place),
        )

    def send(t, stage):
        for side in range(2):
            copy(t, stage, side).start()

    def take(t, stage):
        keep = (count >> (stage + 1)) * size
        for side in range(2):
            copy(t, stage, side).wait()
            rows = pl.ds(side * count * size, keep)
            total = parts[t, rows, :].astype(F32) + landed[stage][t, side].astype(F32)
            if stage + 1 < stages:
                parts[t, rows, :] = total.astype(BF16)
            else:
                columns = pl.ds(pl.multiple_of(t * width, width), width)
                grad_ref[side * size : (side + 1) * size, columns] = total
        if stage + 1 < stages:
            send(t, stage + 1)

    @pl.when(step >= 1)
    def _():
        send(step - 1, 0)

    parts[step] = (
        nn(gates[0][...], gate_w[0][...])
        + nn(gates[1][...], gate_w[1][...])
        + nn(ups[0][...], up_w[0][...])
        + nn(ups[1][...], up_w[1][...])
    ).astype(BF16)
    out = (
        nn(hidden[0][...], down_w[0][...]) + nn(hidden[1][...], down_w[1][...])
    ).astype(BF16)
    for side, bits in enumerate(cube_bits(count)):
        for at, k in enumerate(cube_order(bits)):
            owner = flipped(column, k) if k else column
            start = pl.multiple_of((2 * owner + side) * size, size)
            out_ref[pl.ds(start, size), :] = out[(side * count + at) * size :][:size]

    for stage in reversed(range(stages)):

        @pl.when(step >= 2 * (stage + 1))
        def _():
            take(step - 2 * (stage + 1), stage)

    @pl.when(step == steps - 1)
    def _():
        send(step, 0)
        for stage in range(stages):
            for back in reversed(range(2 * (stage + 1))):
                take(steps - 1 - back, stage)


def row_pass(hidden, grad_gates, grad_ups, inner, down, dp_count):
    count, units = hidden[0].shape
    width = down[0].shape[1]
    tile = min(256, width)
    tiles = width // tile
    size = count // (2 * dp_count)
    stages = dp_count.bit_length() - 1
    resident = pl.BlockSpec((count, units), lambda t: (0, 0), pipeline_mode=pl.Buffered(1))
    low = pl.BlockSpec((units, tile), lambda t: (0, t))
    high = pl.BlockSpec((units, tile), lambda t: (0, tiles + t))
    dma = pltpu.SemaphoreType.DMA
    return pl.pallas_call(
        functools.partial(row_kernel, dp_count),
        grid=(tiles,),
        in_specs=[resident] * 6 + [low, low, high, high, low, low],
        out_specs=[
            pl.BlockSpec((count, tile), lambda t: (0, t)),
            pl.BlockSpec((2 * size, width), lambda t: (0, 0)),
        ],
        out_shape=[
            jax.ShapeDtypeStruct((count, width), BF16),
            jax.ShapeDtypeStruct((2 * size, width), F32),
        ],
        scratch_shapes=[
            pltpu.VMEM((tiles, count, tile), BF16),
            dma((tiles * stages * 2,)),
            dma((tiles * stages * 2,)),
        ]
        + [
            pltpu.VMEM((tiles, 2, (dp_count >> (j + 1)) * size, tile), BF16)
            for j in range(stages)
        ],
        compiler_params=pltpu.CompilerParams(
            collective_id=4, has_side_effects=True, vmem_limit_bytes=56 << 20
        ),
        cost_estimate=pl.CostEstimate(
            flops=2 * 3 * count * width * 2 * units,
            bytes_accessed=12 * units * (width + count) + 4 * count * width,
            transcendentals=0,
        ),
        name="row_pass",
    )(*hidden, *grad_gates, *grad_ups, *inner, *inner, *down)


def add_rows(out_ref, refs, size):
    def some(i, _):
        rows = pl.ds(pl.multiple_of(i * size, size), size)
        total = refs[0][rows, :].astype(F32)
        for ref in refs[1:]:
            total += ref[rows, :].astype(F32)
        out_ref[rows, :] = total.astype(out_ref.dtype)
        return 0

    lax.fori_loop(0, out_ref.shape[0] // size, some, 0)


def spread_kernel(
    sizes,
    micros,
    *refs,
):
    spread_body(sizes, refs[:micros], *refs[micros:])


def spread_body(
    sizes,
    line_refs,
    qkv_ref,
    out_ref,
    grad_ref,
    qkv_done,
    out_done,
    rising,
    falling,
    qkv_in,
    qkv_sum,
    out_in,
    out_part,
    out_line,
    rise_sent,
    rise_here,
    fall_sent,
    fall_here,
    qkv_sent,
    qkv_here,
    out_sent,
    out_here,
    unit_sent,
    unit_here,
    line_sent,
    line_here,
    swap_sent,
    swap_here,
    local,
):
    dp_count, seq_count, unit, per_shard, per_block, per_column = sizes
    span_count = 2 * seq_count
    micros = len(line_refs)
    core, column, place = lax.axis_index("rep"), lax.axis_index("dp"), lax.axis_index("seq")
    span = core * seq_count + place
    cube = [(core, (column + k) % dp_count, place) for k in range(1, dp_count)]
    line = [(core, column, (place + k) % seq_count) for k in range(1, seq_count)]
    across = [(1 - core, column, (place + k) % seq_count) for k in range(seq_count)]
    greet(cube + line + across)

    def part_at(part, col):
        return (part * span_count + span) // per_column == col

    def out_copy(k):
        target = cube[k]
        return remote(
            out_ref.at[target[1]], out_in.at[k], out_sent.at[k], out_here.at[k], target
        )

    def qkv_copy(k, part):
        return remote(
            qkv_ref.at[part], qkv_in.at[k], qkv_sent.at[k], qkv_here.at[k], cube[k]
        )

    def hop(number, m, up):
        reach = seq_count - number
        buffer, sent, here = (
            (rising, rise_sent, rise_here) if up else (falling, fall_sent, fall_here)
        )
        behind = place if up else seq_count - 1 - place
        owner = place + reach if up else place - reach
        owner = jnp.clip(owner, 0, seq_count - 1)
        next_place = jnp.clip(place + 1 if up else place - 1, 0, seq_count - 1)
        device = (core, column, next_place)
        at = (number - 1) * micros + m
        target = buffer.at[at]

        def send(source):
            remote(source, target, sent.at[at], here.at[at], device).start()

        own = line_refs[m].at[owner]
        if number == 1:
            pl.when(behind == 0)(lambda: send(own))
            return

        @pl.when(behind == 0)
        def _():
            send(own)

        @pl.when((behind >= 1) & (behind <= number - 1))
        def _():
            before = buffer.at[at - micros]
            remote(before, before, sent.at[0], here.at[at - micros], across[0]).wait_recv()
            add_rows(before, [before, own], 64)
            send(before)

    def hop_sent(number, m, up):
        sent = rise_sent if up else fall_sent
        buffer = rising if up else falling
        behind = place if up else seq_count - 1 - place
        at = (number - 1) * micros + m
        piece = buffer.at[at]

        @pl.when(behind <= number - 1)
        def _():
            remote(piece, piece, sent.at[at], sent.at[at], across[0]).wait_send()

    def hops(number):
        for m in range(micros):
            hop(number, m, True)
            hop(number, m, False)

    hops(1)
    for k in range(dp_count - 1):
        out_copy(k).start()
        for part in range(3):

            @pl.when(part_at(part, cube[k][1]))
            def _():
                qkv_copy(k, part).start()

    hops(2)

    for k in range(dp_count - 1):
        out_copy(k).wait_recv()
    for s in range(seq_count):
        add_rows(
            out_part.at[s],
            [out_ref.at[column, s]] + [out_in.at[k, s] for k in range(dp_count - 1)],
            32,
        )

    def line_copy(k):
        return remote(
            out_part.at[line[k][2]], out_line.at[k], line_sent.at[k], line_here.at[k], line[k]
        )

    for k in range(seq_count - 1):
        line_copy(k).start()

    def unit_copies(part, j):
        number = (part * span_count + span) * per_block + j
        owner = (number // per_shard) % seq_count
        source = qkv_sum.at[pl.ds(j * unit, unit)]
        target = qkv_done.at[pl.ds(pl.multiple_of((number % per_shard) * unit, unit), unit)]
        here = unit_here.at[number % per_shard]
        other = remote(
            source, target, unit_sent.at[2 * j], here, (1 - core, column, owner)
        )
        same = remote(source, target, unit_sent.at[2 * j + 1], here, (core, column, owner))
        stays = pltpu.make_async_copy(source, target, local.at[j])
        return owner, other, same, stays

    for part in range(3):

        @pl.when(part_at(part, column))
        def _():
            for k in range(dp_count - 1):
                qkv_copy(k, part).wait_recv()
            add_rows(
                qkv_sum, [qkv_ref.at[part]] + [qkv_in.at[k] for k in range(dp_count - 1)], 32
            )
            for j in range(per_block):
                owner, other, same, stays = unit_copies(part, j)
                other.start()
                pl.when(owner != place)(same.start)
                pl.when(owner == place)(stays.start)

    for number in range(3, seq_count):
        hops(number)

    for k in range(seq_count - 1):
        line_copy(k).wait_recv()
    add_rows(
        out_done.at[core],
        [out_part.at[place]] + [out_line.at[k] for k in range(seq_count - 1)],
        32,
    )
    mine = out_done.at[core]
    swapped = remote(mine, mine, swap_sent, swap_here, across[0])
    swapped.start()

    last = (seq_count - 2) * micros
    for m in range(micros):
        own = line_refs[m].at[place]
        up, down = rising.at[last + m], falling.at[last + m]

        @pl.when(place > 0)
        def _():
            remote(up, up, rise_sent.at[0], rise_here.at[last + m], across[0]).wait_recv()

        @pl.when(place < seq_count - 1)
        def _():
            remote(down, down, fall_sent.at[0], fall_here.at[last + m], across[0]).wait_recv()

        @pl.when(place == 0)
        def _():
            add_rows(grad_ref.at[m], [own, down], 64)

        @pl.when(place == seq_count - 1)
        def _():
            add_rows(grad_ref.at[m], [own, up], 64)

        @pl.when((place > 0) & (place < seq_count - 1))
        def _():
            add_rows(grad_ref.at[m], [own, up, down], 64)

    for number in range(1, seq_count):
        for m in range(micros):
            hop_sent(number, m, True)
            hop_sent(number, m, False)
    for k in range(dp_count - 1):
        out_copy(k).wait_send()
        for part in range(3):

            @pl.when(part_at(part, cube[k][1]))
            def _():
                qkv_copy(k, part).wait_send()

    for k in range(seq_count - 1):
        line_copy(k).wait_send()
    for part in range(3):

        @pl.when(part_at(part, column))
        def _():
            for j in range(per_block):
                owner, other, same, stays = unit_copies(part, j)
                other.wait_send()
                pl.when(owner != place)(same.wait_send)
                pl.when(owner == place)(stays.wait)

    for i in range(per_shard):
        number = (column * seq_count + place) * per_shard + i
        piece = qkv_done.at[pl.ds(i * unit, unit)]

        @pl.when((number // per_block) % span_count != span)
        def _():
            remote(piece, piece, unit_sent.at[0], unit_here.at[i], across[0]).wait_recv()

    swapped.wait_send()
    theirs = out_done.at[1 - core]
    remote(theirs, theirs, swap_sent, swap_here, across[0]).wait_recv()


def spread_sums(lines, qkv, out, sizes):
    dp_count, seq_count, unit, per_shard, per_block, _ = sizes
    micros = len(lines)
    _, rows, width = lines[0].shape
    shard_out, half_width = out.shape[2:]
    block_rows = unit * per_block
    hops = (seq_count - 1) * micros
    vmem = pl.BlockSpec(memory_space=pltpu.VMEM)
    dma = pltpu.SemaphoreType.DMA
    return pl.pallas_call(
        functools.partial(spread_kernel, sizes, micros),
        in_specs=[vmem] * (micros + 2),
        out_specs=[vmem] * 3,
        out_shape=[
            jax.ShapeDtypeStruct((micros, rows, width), F32),
            jax.ShapeDtypeStruct((per_shard * unit, width), BF16),
            jax.ShapeDtypeStruct((2, shard_out, half_width), BF16),
        ],
        scratch_shapes=[
            pltpu.VMEM((hops, rows, width), BF16),
            pltpu.VMEM((hops, rows, width), BF16),
            pltpu.VMEM((dp_count - 1, block_rows, width), BF16),
            pltpu.VMEM((block_rows, width), BF16),
            pltpu.VMEM((dp_count - 1, seq_count, shard_out, half_width), BF16),
            pltpu.VMEM((seq_count, shard_out, half_width), BF16),
            pltpu.VMEM((seq_count - 1, shard_out, half_width), BF16),
            dma((hops,)),
            dma((hops,)),
            dma((hops,)),
            dma((hops,)),
            dma((dp_count - 1,)),
            dma((dp_count - 1,)),
            dma((dp_count - 1,)),
            dma((dp_count - 1,)),
            dma((2 * per_block,)),
            dma((per_shard,)),
            dma((seq_count - 1,)),
            dma((seq_count - 1,)),
            dma,
            dma,
            dma((per_block,)),
        ],
        compiler_params=pltpu.CompilerParams(
            collective_id=1, has_side_effects=True, vmem_limit_bytes=56 << 20
        ),
        cost_estimate=pl.CostEstimate(
            flops=0, bytes_accessed=256 * rows * width, transcendentals=0
        ),
        name="spread_sums",
    )(*lines, qkv, out)


def pick(table, number):
    return jnp.asarray(table, jnp.int32)[number]


def shards(
    tokens,
    lengths,
    memory,
    normalizer,
    qkv_weight,
    out_weight,
    norm_gains,
    gate_logit,
    inner_weight,
    down_weight,
    cotangent,
):
    micros, _, span_rows, width = tokens.shape
    head_count = gate_logit.shape[0]
    head_dim = width // head_count
    dp_count, seq_count = lax.axis_size("dp"), lax.axis_size("seq")
    span_count = 2 * seq_count
    total = span_rows * span_count
    heads_here = head_count // span_count
    block_rows = heads_here * head_dim
    core, column, place = lax.axis_index("rep"), lax.axis_index("dp"), lax.axis_index("seq")
    span = core * seq_count + place
    inner_half = inner_weight.shape[0] // 2

    own_rows = [tokens[m, 0] for m in range(micros)]

    def gather_rows(rows):
        return lax.all_gather(rows, ("rep", "seq"), axis=0, tiled=True)

    all_rows = [gather_rows(own_rows[0])]

    unit = math.gcd(qkv_weight.shape[0], block_rows)
    per_shard, per_block = qkv_weight.shape[0] // unit, block_rows // unit
    per_column = 3 * span_count // dp_count
    devices = 2 * dp_count * seq_count
    shard_out, shard_gain = out_weight.shape[0], norm_gains.shape[1]
    lanes = -(-shard_gain // 128) * 128
    gain_tile = jnp.zeros((8, lanes), F32)
    gain_tile = lax.dynamic_update_slice(gain_tile, norm_gains.astype(F32), (0, 0))
    head_weight, gains_all = gather_heads(
        qkv_weight, gain_tile, (dp_count, seq_count, unit, per_shard, per_block, per_column)
    )
    gains_all = jnp.swapaxes(gains_all[:, :2, :shard_gain], 0, 1).reshape(2, width)
    gain_one, gain_two = gains_all[0:1], gains_all[1:2]
    half_width = width // 2
    positions = span * span_rows + jnp.arange(span_rows)
    lives = []
    for m in range(micros):
        live_rows = (positions < lengths[m, 0]).astype(F32)
        lives.append(cotangent[m, 0].astype(F32) * live_rows[:, None])
    for rows in own_rows[1:]:
        all_rows.append(gather_rows(after(rows, all_rows[-1], head_weight)))
    out_half = lax.dynamic_slice_in_dim(out_weight, core * half_width, half_width, 1)
    cots = [live.astype(BF16) for live in lives]
    out_near, cot_all = gather_rest(
        after(out_half, head_weight, all_rows[0]), cots[0], (dp_count, seq_count)
    )
    grads_all = [cot_all]
    for cot in cots[1:]:
        grads_all.append(gather_cot(after(cot, grads_all[-1], all_rows[-1]), dp_count))
    out_far = swap(out_near)

    gate_share = jax.nn.sigmoid(gate_logit)
    gate_here = lax.dynamic_slice_in_dim(gate_share, span * heads_here, heads_here, 0)
    near_at, far_at = core * half_width, (1 - core) * half_width
    low_first = core == 0

    saved = []
    outputs, new_memories, new_norms = [], [], []
    for m in range(micros):
        hidden_one, projected = project(
            after(all_rows[m], all_rows[-1], grads_all[-1]),
            gain_one,
            head_weight,
        )
        if m == 0:
            near_units, near_downs = (
                lax.dynamic_slice_in_dim(w, core * inner_half, inner_half, 0)
                for w in (inner_weight, down_weight)
            )
        memory_here = lax.dynamic_slice_in_dim(memory[m, 0], span * heads_here, heads_here, 0)
        norm_here = lax.dynamic_slice_in_dim(
            normalizer[m, 0], span * heads_here, heads_here, 0
        ).reshape(heads_here, 1, head_dim)
        length = lengths[m]
        mixed_heads, dot_read, lse, new_memory, new_norm = attend(
            length, gate_here, projected, memory_here, norm_here
        )
        if m == 0:
            inner_near = lax.all_gather(
                after(near_units, all_rows[-1], out_near),
                "seq",
                axis=0,
                tiled=True,
            )
        new_memories.append(new_memory)
        new_norms.append(new_norm.reshape(heads_here, head_dim))
        mixed = lax.all_to_all(
            mixed_heads.reshape(span_count, span_rows, block_rows),
            ("rep", "seq"),
            0,
            0,
            tiled=True,
        )
        mixed = jnp.swapaxes(mixed, 0, 1).reshape(span_rows, width)
        mixed_near = lax.dynamic_slice_in_dim(mixed, near_at, half_width, 1)
        mixed_far = lax.dynamic_slice_in_dim(mixed, far_at, half_width, 1)
        after_attn = (
            own_rows[m].astype(F32)
            + nt(mixed_near, out_near)
            + nt(mixed_far, out_far)
        )
        scale_two = lax.rsqrt(jnp.mean(after_attn * after_attn, axis=-1, keepdims=True) + EPSILON)
        normed_two = after_attn * scale_two
        hidden_two = (normed_two * gain_two).astype(BF16)
        if m + 1 == micros:
            hidden_two = after(hidden_two, inner_near)
        rows_all = cube_gather(hidden_two, "dp")
        saved.append(
            dict(
                hidden_one=hidden_one,
                projected=projected,
                live=lives[m],
                grads=grads_all[m],
                memory=memory_here,
                norm=norm_here,
                length=length,
                dot_read=dot_read,
                lse=lse,
                mixed_heads=mixed_heads,
                mixed_near=mixed_near,
                mixed_far=mixed_far,
                after_attn=after_attn,
                scale_two=scale_two,
                normed_two=normed_two,
                rows=rows_all,
            )
        )

    down_near = after(
        lax.all_gather(near_downs, "seq", axis=0, tiled=True), *[s["rows"] for s in saved]
    )
    inner_far, down_far = swap(inner_near), swap(down_near)

    inner, down = (inner_near, inner_far), (down_near, down_far)
    last = None
    for s in saved:
        halves = []
        for half in range(2):
            halves.append(unit_pass(after(s["rows"], last), s["grads"], inner[half], down[half]))
            last = halves[-1][0]
        s["hidden"], s["grad_gates"], s["grad_ups"] = zip(*halves)

    def half_grads(left, right, half, extra, *earlier):
        pairs = [(s[left][half], s[right]) for s in saved]
        pairs[0] = (after(pairs[0][0], *earlier), pairs[0][1])
        return weight_pass(pairs, extra)

    def spread(values):
        return lax.psum_scatter(values, "seq", scatter_dimension=0, tiled=True)

    def rows_out(s, *earlier):
        gates = (after(s["grad_gates"][0], *earlier), s["grad_gates"][1])
        s["mlp_part"], s["grad_two"] = row_pass(
            s["hidden"], gates, s["grad_ups"], inner, down, dp_count
        )
        return s["grad_two"]

    down_far_sum = half_grads("hidden", "grads", 1, None, last)
    gate_far_sum = half_grads("grad_gates", "rows", 1, None, down_far_sum)
    down_sum = half_grads("hidden", "grads", 0, swap(down_far_sum), gate_far_sum)
    down_mine = spread(down_sum)
    last = rows_out(saved[0], down_sum)
    up_far_sum = half_grads("grad_ups", "rows", 1, None, last)
    gate_sum = half_grads("grad_gates", "rows", 0, swap(gate_far_sum), up_far_sum)
    gate_mine = spread(gate_sum)
    def rows_back(s):
        grad_two = s["grad_two"]
        grad_scaled = grad_two * gain_two
        normed_two = s["normed_two"]
        s["grad_after"] = s["live"] + s["scale_two"] * (
            grad_scaled
            - normed_two * jnp.mean(grad_scaled * normed_two, axis=-1, keepdims=True)
        )
        s["grad_branch"] = s["grad_after"].astype(BF16)
        s["gains_two"] = jnp.sum(grad_two * normed_two, axis=0)
        grad_mixed_near = nn(s["grad_branch"], out_near).astype(BF16)
        grad_mixed_far = nn(s["grad_branch"], out_far).astype(BF16)
        grad_mixed = jnp.concatenate(
            [
                jnp.where(low_first, grad_mixed_near, grad_mixed_far),
                jnp.where(low_first, grad_mixed_far, grad_mixed_near),
            ],
            axis=1,
        )
        s["grad_mixed"] = jnp.swapaxes(
            grad_mixed.reshape(span_rows, span_count, block_rows), 0, 1
        )
        return lax.all_to_all(s["grad_mixed"], ("rep", "seq"), 0, 0, tiled=True).reshape(
            total, block_rows
        )

    def heads_back(s, m, grad_heads):
        s["grad_projected"], gate_sums = attend_back(
            s["length"],
            gate_here,
            s["projected"],
            s["memory"],
            s["norm"],
            s["dot_read"],
            s["lse"],
            grad_heads,
        )
        s["gate"] = jnp.sum(gate_sums, axis=(1, 2))
        part_far, gains_far = project_back(
            1 - core, s["grad_projected"], head_weight, all_rows[m]
        )
        part_near, gains_near = project_back(
            core, s["grad_projected"], head_weight, all_rows[m], swap(part_far)
        )
        s["gains_one"] = (gains_far + gains_near)[0]
        return part_near

    def tokens_back(s, m, grad_one):
        rows_float = own_rows[m].astype(F32)
        scale_one = lax.rsqrt(jnp.mean(rows_float * rows_float, axis=-1, keepdims=True) + EPSILON)
        normed_one = rows_float * scale_one
        grad_scaled = grad_one * gain_one
        return (
            s["grad_after"]
            + scale_one
            * (
                grad_scaled
                - normed_one * jnp.mean(grad_scaled * normed_one, axis=-1, keepdims=True)
            )
        ).astype(BF16)

    heads_grads = [rows_back(saved[0])]
    last = gate_sum
    for m, s in enumerate(saved[1:]):
        last = rows_out(s, last, down_mine)
        heads_grads.append(rows_back(s))

    def spread_out(s, *earlier):
        return lax.psum_scatter(
            after(s["mlp_part"], *earlier), "dp", scatter_dimension=0, tiled=True
        )

    mlp_outs, sums = [spread_out(saved[0], saved[-1]["grad_branch"])], []
    earlier = (saved[-1]["grad_mixed"], gate_mine)
    for m, s in enumerate(saved):
        sums.append(heads_back(s, m, after(heads_grads[m], *earlier)))
        if m == 0:
            up_sum = half_grads(
                "grad_ups", "rows", 0, swap(up_far_sum), s["grad_projected"], heads_grads[-1]
            )
            up_mine = spread(up_sum)
            earlier = (up_sum, mlp_outs[0])
        else:
            mlp_outs.append(spread_out(s, up_sum))
    out_far_sum = weight_pass([(s["grad_branch"], s["mixed_far"]) for s in saved])
    out_sum = weight_pass(
        [(s["grad_branch"], s["mixed_near"]) for s in saved], swap(out_far_sum)
    )
    qkv_low = weight_pass([(s["grad_projected"], s["hidden_one"]) for s in saved]).reshape(
        3, block_rows, width
    )

    grad_ones, qkv_done, out_done = spread_sums(
        [after(p, up_mine, mlp_outs[0]).reshape(seq_count, span_rows, width) for p in sums],
        qkv_low,
        out_sum.reshape(dp_count, seq_count, shard_out, half_width),
        (dp_count, seq_count, unit, per_shard, per_block, per_column),
    )
    grad_tokens = [tokens_back(s, m, grad_ones[m]) for m, s in enumerate(saved)]
    grad_qkv = qkv_done.astype(F32)
    grad_out = jnp.swapaxes(out_done, 0, 1).reshape(shard_out, width).astype(F32)
    for s, mlp_out in zip(saved, mlp_outs):
        mlp_out = after(mlp_out, grad_ones)
        outputs.append((s["after_attn"] + mlp_out.astype(F32)).astype(BF16))

    def joined(name):
        return functools.reduce(jnp.add, [s[name] for s in saved])

    def both_cores(mine, axis):
        other = swap(mine)
        size = mine.shape[axis]
        shape = list(mine.shape)
        shape[axis] = 2 * size
        whole = jnp.zeros(shape, F32)
        whole = lax.dynamic_update_slice_in_dim(whole, mine.astype(F32), core * size, axis)
        return lax.dynamic_update_slice_in_dim(
            whole, other.astype(F32), (1 - core) * size, axis
        )

    grad_down = both_cores(down_mine, 0)
    grad_inner = both_cores(jnp.concatenate([gate_mine, up_mine], axis=1), 0)

    gate_terms = joined("gate") * gate_here * (1.0 - gate_here)
    gate_row = lax.dynamic_update_slice_in_dim(
        jnp.zeros((head_count,), F32), gate_terms, span * heads_here, 0
    )
    small = jnp.concatenate([joined("gains_one"), joined("gains_two"), gate_row])
    small = jnp.pad(small, (0, 8 * width - small.shape[0])).reshape(8, width)
    small = lax.all_gather(after(small, up_mine), ALL, axis=0, tiled=True)
    small = jnp.sum(small.reshape(devices, 8 * width)[:, : 3 * width], axis=0)
    gain_at = (column * seq_count + place) * shard_gain
    grad_gains = lax.dynamic_slice_in_dim(
        small[: 2 * width].reshape(2, width), gain_at, shard_gain, 1
    )
    grad_gate = small[2 * width : 2 * width + head_count]
    return (
        jnp.stack(outputs)[:, None],
        jnp.stack(new_memories)[:, None],
        jnp.stack(new_norms)[:, None],
        jnp.stack(grad_tokens)[:, None],
        grad_qkv,
        grad_out,
        grad_gains,
        grad_gate,
        grad_inner,
        grad_down,
    )


def solution(mesh):
    placed = (
        P(None, "dp", ("rep", "seq"), None),
        P(None, "dp"),
        P(None, "dp", None, None, None),
        P(None, "dp", None, None),
        P(("dp", "seq"), None),
        P(("dp", "seq"), None),
        P(None, ("dp", "seq")),
        P(),
        P(("dp", "seq"), None),
        P(("dp", "seq"), None),
        P(None, "dp", ("rep", "seq"), None),
    )
    return jax.shard_map(
        shards,
        mesh=mesh,
        in_specs=placed,
        out_specs=(
            P(None, "dp", ("rep", "seq"), None),
            P(None, "dp", ("rep", "seq"), None, None),
            P(None, "dp", ("rep", "seq"), None),
            P(None, "dp", ("rep", "seq"), None),
            P(("dp", "seq"), None),
            P(("dp", "seq"), None),
            P(None, ("dp", "seq")),
            P(),
            P(("dp", "seq"), None),
            P(("dp", "seq"), None),
        ),
        check_vma=False,
    )
```
